32 devices in a mesh: field: 4 (over y, x), gz: 8 (over z, core).
Axes of the slice: x: 2, y: 2, z: 4, core: 2. Of those that a mesh axis runs over, the one named last changes fastest.
Arguments:
- fields: bfloat16 [2048, 2, 8, 16, 256], P('gz', None, 'field'), may hold values from -8 to 8
- shells: int32 [2048, 16, 256], P('gz'), may hold values from 0 to 255
- mubins: int32 [2048, 16, 256], P('gz'), may hold values from 0 to 7, as said below
Outputs:
- power: float32 [3, 8, 256], replicated
The draws below stay inside these ranges and needn't reach their ends.
Inputs may be any that keep to these rules, and one draw needn't show every extreme that they name: `mubins`: A cell's mu-bin index is never above its k-shell index.
All inputs are finite; a program needn't handle non-finite values.
Results may differ from the reference program's by a relative error of at most 0.00052.
Values may be sent and summed in bfloat16 or wider, within the bound.
A program may use at most 192 MiB of HBM per device.

```python
import math
import jax
import jax.numpy as jnp
import numpy as np
from jax import lax

NZ = 2048
FIELDS = 8
SHELLS = 256
MUBINS = 8
PLANES = 16
YROWS = 256
N_FIELD = 4


def draw_fields(key, part):
    first_key, second_key, third_key = jax.random.split(jax.random.fold_in(key, 11), 3)
    common = jax.random.normal(first_key, (NZ, 2, 1, PLANES, YROWS), jnp.float32)
    mixing = jax.random.uniform(second_key, (FIELDS,), jnp.float32, 0.5, 1.0).at[0].set(1.0)
    noise = jax.random.normal(third_key, (NZ, 2, FIELDS, PLANES, YROWS), jnp.float32)
    values = mixing[None, None, :, None, None] * common + 0.7 * noise
    return jnp.clip(values, -8.0, 8.0).astype(jnp.bfloat16)


def shell_and_mu(key):
    shell_key, mu_key = jax.random.split(jax.random.fold_in(key, 23))
    shell_ids = jax.random.randint(shell_key, (NZ, PLANES, YROWS), 0, SHELLS, jnp.int32)
    upper = jnp.minimum(shell_ids + 1, MUBINS)
    mu_ids = jax.random.randint(mu_key, (NZ, PLANES, YROWS), 0, upper, jnp.int32)
    return (shell_ids, mu_ids)


def draw_shells(key, part):
    return shell_and_mu(key)[0]


def draw_mubins(key, part):
    return shell_and_mu(key)[1]


def setup_inputs(seed: int = 0) -> dict:
    seeds = jax.random.split(jax.random.key(seed), 4)
    return {
        "fields": draw_fields(jax.random.fold_in(seeds[3], 71), 0),
        "shells": draw_shells(jax.random.fold_in(seeds[3], 71), 0),
        "mubins": draw_mubins(jax.random.fold_in(seeds[3], 71), 0),
    }


def make_coef():
    table = np.zeros((3, 8, 7), np.float32)
    table[0, 0, 0] = 1.0
    table[1, 1, 0] = 1.0
    table[2, 1, 0] = -0.5
    table[2, 2, 1] = 1.5
    table[2, 3, 2] = 1.5
    table[2, 4, 3] = 1.5
    table[2, 5, 4] = 3.0
    table[2, 6, 5] = 3.0
    table[2, 7, 6] = 3.0
    return table

def dft_tables(length):
    index = jnp.arange(length, dtype=jnp.int32)
    product = index[:, None] * index[None, :] % length
    angle = product.astype(jnp.float32) * (2.0 * math.pi / length)
    factor = 1.0 / math.sqrt(length)
    return ((jnp.cos(angle) * factor).astype(jnp.bfloat16), (jnp.sin(angle) * factor).astype(jnp.bfloat16))

def monomials(wave_x, wave_y, wave_z):
    square = wave_x * wave_x + wave_y * wave_y + wave_z * wave_z
    ones = jnp.ones_like(square)
    return jnp.stack([ones, wave_x * wave_x / square, wave_y * wave_y / square, wave_z * wave_z / square, wave_x * wave_y / square, wave_x * wave_z / square, wave_y * wave_z / square])

def bin_cells(values, shell_ids, mu_ids):
    cells = values.shape[1]
    block = math.gcd(cells, 32768)
    blocks = cells // block
    value_blocks = values.reshape(3, blocks, block).transpose(1, 0, 2)
    shell_blocks = shell_ids.reshape(blocks, block)
    mu_blocks = mu_ids.reshape(blocks, block)

    def step(total, pieces):
        value_piece, shell_piece, mu_piece = pieces
        mu_hot = (mu_piece[None, :] == jnp.arange(MUBINS, dtype=jnp.int32)[:, None]).astype(jnp.float32)
        rows = (value_piece[:, None, :] * mu_hot[None]).reshape(3 * MUBINS, block)
        rows = jnp.concatenate([rows, mu_hot], axis=0)
        shell_hot = (shell_piece[None, :] == jnp.arange(SHELLS, dtype=jnp.int32)[:, None]).astype(jnp.float32)
        return (total + lax.dot_general(rows, shell_hot, (((1,), (1,)), ((), ())), precision=lax.Precision.HIGHEST), None)
    start = jnp.zeros((4 * MUBINS, SHELLS), jnp.float32)
    total, _ = lax.scan(step, start, (value_blocks, shell_blocks, mu_blocks))
    return total

def reference(fields, shells, mubins):
    group = FIELDS // N_FIELD
    cos_table, sin_table = dft_tables(NZ)
    cos_wide = cos_table.astype(jnp.float32)
    sin_wide = sin_table.astype(jnp.float32)
    coef = jnp.asarray(make_coef())
    depth = jnp.arange(NZ, dtype=jnp.int32)
    wave_z = jnp.where(depth >= NZ // 2, depth - NZ, depth).astype(jnp.float32)
    wave_y = (NZ // 8 + jnp.arange(YROWS, dtype=jnp.int32)).astype(jnp.float32)

    def plane(total, plane_index):
        data = lax.dynamic_index_in_dim(fields, plane_index, 3, keepdims=False)
        flat = data.astype(jnp.float32).reshape(NZ, 2 * FIELDS * YROWS)
        first = jnp.dot(cos_wide, flat, precision=lax.Precision.HIGHEST).reshape(NZ, 2, FIELDS, YROWS)
        second = jnp.dot(sin_wide, flat, precision=lax.Precision.HIGHEST).reshape(NZ, 2, FIELDS, YROWS)
        real_part = first[:, 0] + second[:, 1]
        imag_part = first[:, 1] - second[:, 0]
        cross = real_part[:, :1] * real_part + imag_part[:, :1] * imag_part
        wave_x = (NZ // 4 + plane_index).astype(jnp.float32)
        terms = monomials(wave_x + jnp.zeros((NZ, YROWS), jnp.float32), wave_y[None, :], wave_z[:, None])
        weights = jnp.einsum('maj,jzy->mazy', coef, terms, precision=lax.Precision.HIGHEST)
        contrib = weights * jnp.transpose(cross, (1, 0, 2))[None]
        per_group = contrib.reshape(3, N_FIELD, group, NZ, YROWS).sum(axis=2)
        rounded = lax.optimization_barrier(per_group.astype(jnp.bfloat16)).astype(jnp.float32)
        cell_values = rounded.sum(axis=1).reshape(3, NZ * YROWS)
        shell_ids = lax.dynamic_index_in_dim(shells, plane_index, 1, keepdims=False).reshape(NZ * YROWS)
        mu_ids = lax.dynamic_index_in_dim(mubins, plane_index, 1, keepdims=False).reshape(NZ * YROWS)
        return (total + bin_cells(cell_values, shell_ids, mu_ids), None)
    start = jnp.zeros((4 * MUBINS, SHELLS), jnp.float32)
    total, _ = lax.scan(plane, start, jnp.arange(PLANES, dtype=jnp.int32))
    sums = total[:3 * MUBINS].reshape(3, MUBINS, SHELLS)
    counts = total[3 * MUBINS:]
    return sums / jnp.maximum(counts, 1.0)[None]
```

```python
import functools
import math

import jax
import jax.numpy as jnp
import numpy as np
from jax import lax
from jax.experimental import pallas as pl
from jax.experimental.pallas import tpu as pltpu
from jax.sharding import PartitionSpec as P

SHELLS = 256
MUBINS = 8
LANES = 128
LOW = 16
ROWS = 5
PAIRS = 8


def quarter_tables(length, zero):
    quarter, half = length // 4, length // 2
    unit = 2.0 * math.pi / length
    factor = 1.0 / math.sqrt(length)

    def pair(rows, stride):
        shape = (2, rows, half)
        parity = lax.broadcasted_iota(jnp.int32, shape, 0)
        row = lax.broadcasted_iota(jnp.int32, shape, 1) * stride + zero
        depth = 2 * lax.broadcasted_iota(jnp.int32, shape, 2) + parity
        angle = (row * depth % length).astype(jnp.float32) * unit
        return jnp.cos(angle), jnp.sin(angle)

    fine = 16
    ca, sa, cb, sb = lax.optimization_barrier(pair(quarter // fine, fine) + pair(fine, 1))
    ca, sa, cb, sb = ca[:, :, None], sa[:, :, None], cb[:, None], sb[:, None]
    cos_part = ((ca * cb - sa * sb) * factor).reshape(2, quarter, half)
    sin_part = ((sa * cb + ca * sb) * factor).reshape(2, quarter, half)
    row = lax.broadcasted_iota(jnp.int32, sin_part.shape, 1)
    column = lax.broadcasted_iota(jnp.int32, sin_part.shape, 2)
    alternate = (1 - 2 * (column % 2)).astype(jnp.float32) * factor
    sin_part = jnp.where(row == 0, alternate, sin_part)
    return jnp.concatenate(
        [cos_part.astype(jnp.bfloat16), sin_part.astype(jnp.bfloat16)], axis=1
    )


def round16(value):
    return value.astype(jnp.bfloat16).astype(jnp.float32)


def unpack(index_ref, keys):
    depth = index_ref.shape[1]

    def block(g, carry):
        word = index_ref[g]
        mu = word // 65536
        key = (word - mu * 65536) * MUBINS + mu
        upper = key // LOW
        rows = pl.ds(pl.multiple_of(g * depth, depth), depth)
        keys[0, rows, :] = (key - upper * LOW).astype(jnp.float32)
        keys[1, rows, :] = upper.astype(jnp.float32)
        return carry

    lax.fori_loop(0, index_ref.shape[0], block, 0)


def products(table_ref, lines_ref, prod, parity):
    half = table_ref.shape[1]

    def group(f, carry):
        right = lines_ref[f, :, parity].reshape(half, lines_ref.shape[-1])

        def rows_of(i, inner):
            rows = pl.ds(pl.multiple_of(i * 256, 256), 256)
            prod[f, parity, rows, :] = jnp.dot(
                table_ref[parity, rows, :], right, preferred_element_type=jnp.float32
            )
            return inner

        return lax.fori_loop(0, half // 256, rows_of, carry)

    lax.fori_loop(0, prod.shape[0], group, 0)


def local_kernel(length, table_ref, lines_ref, index_ref, wave_ref, out_ref, prod, vals, keys):
    unpack(index_ref, keys)
    products(table_ref, lines_ref, prod, 0)
    products(table_ref, lines_ref, prod, 1)
    bins(length, wave_ref, out_ref, prod, vals, keys)


def exchange_kernel(
    length, field_count, gz_count, table_ref, lines_ref, index_ref, wave_ref, out_ref,
    prod, vals, keys, lines, index, send, recv, own, index_send, index_recv, index_own,
):
    devices = field_count * gz_count
    me_field, me_gz = lax.axis_index("field"), lax.axis_index("gz")
    far = gz_count // 2
    mine = (gz_count - far) * field_count

    def peer(step):
        f = lax.rem(me_field + lax.rem(step, field_count), field_count)
        g = lax.rem(me_gz + step // field_count + far, gz_count)
        return f, g

    def others(run):
        def loop(step, carry):
            run(step)
            return carry

        lax.fori_loop(0, mine, loop, 0)
        lax.fori_loop(mine + 1, devices, loop, 0)

    def along(run):
        def loop(step, carry):
            run(step)
            return carry

        lax.fori_loop(1, gz_count, loop, 0)

    barrier = pltpu.get_barrier_semaphore()
    others(
        lambda step: pl.semaphore_signal(
            barrier, inc=1, device_id=peer(step), device_id_type=pl.DeviceIdType.MESH
        )
    )
    pl.semaphore_wait(barrier, devices - 1)

    def index_copy(step):
        g = lax.rem(me_gz + step, gz_count)
        return pltpu.make_async_remote_copy(
            src_ref=index_ref.at[g],
            dst_ref=index.at[me_gz],
            send_sem=index_send.at[step],
            recv_sem=index_recv.at[step],
            device_id=(me_field, g),
            device_id_type=pl.DeviceIdType.MESH,
        )

    def lines_copy(parity):
        def copy(step):
            f, g = peer(step)
            return pltpu.make_async_remote_copy(
                src_ref=lines_ref.at[f * gz_count + g, parity],
                dst_ref=lines.at[me_field, me_gz, parity],
                send_sem=send.at[parity, step],
                recv_sem=recv.at[parity, step],
                device_id=(f, g),
                device_id_type=pl.DeviceIdType.MESH,
            )

        return copy

    along(lambda step: index_copy(step).start())
    for parity in range(2):
        others(lambda step: lines_copy(parity)(step).start())
    me = me_field * gz_count + me_gz
    kept = [
        pltpu.make_async_copy(
            lines_ref.at[me, parity], lines.at[me_field, me_gz, parity], own.at[parity]
        )
        for parity in range(2)
    ]
    kept_index = pltpu.make_async_copy(index_ref.at[me_gz], index.at[me_gz], index_own)
    for copy in kept + [kept_index]:
        copy.start()

    kept_index.wait()
    along(lambda step: index_copy(step).wait_recv())
    unpack(index, keys)
    for parity in range(2):
        kept[parity].wait()
        others(lambda step: lines_copy(parity)(step).wait_recv())
        products(table_ref, lines, prod, parity)
    bins(length, wave_ref, out_ref, prod, vals, keys)
    along(lambda step: index_copy(step).wait_send())
    for parity in range(2):
        others(lambda step: lines_copy(parity)(step).wait_send())


def bins(length, wave_ref, out_ref, prod, vals, keys):
    quarter, half = length // 4, length // 2
    groups, local = prod.shape[0], prod.shape[3] // (2 * LANES)
    fields = groups * local
    out_ref[...] = jnp.zeros_like(out_ref)
    wave_x = wave_ref[0:1, :]
    wave_y = wave_ref[1:2, :]
    low_iota = lax.broadcasted_iota(jnp.int32, (16, LANES), 0).astype(jnp.float32)
    iotas = [(low_iota + 16.0 * j).astype(jnp.bfloat16) for j in range(LANES // 16)]
    one = jnp.ones((16, LANES), jnp.bfloat16)
    none = jnp.zeros((16, LANES), jnp.bfloat16)

    def cell_row(j, k):
        start = 1 - (k + quarter - 1) // quarter
        return (
            k,
            half - k,
            half + k - quarter * start,
            length - k - quarter * start,
        )[j]

    def tile(t, carry):
        first = pl.multiple_of(t * 8, 8)
        row = lax.broadcasted_iota(jnp.int32, (8, LANES), 0) + first
        special = row == 0

        def load(a, c, parity, sine):
            g, i = a // local, a % local
            at = (c * local + i) * LANES
            return prod[g, parity, pl.ds(sine * quarter + first, 8), at : at + LANES]

        def spectra(a):
            parts = []
            for c in range(2):
                ec, oc = load(a, c, 0, 0), load(a, c, 1, 0)
                es, os = load(a, c, 0, 1), load(a, c, 1, 1)
                p, q, m, n = ec + oc, es + os, ec - oc, os - es
                parts.append(
                    (
                        (p, jnp.where(special, 0.0, q)),
                        (m, jnp.where(special, 0.0, n)),
                        (jnp.where(special, es, m), jnp.where(special, os, -n)),
                        (jnp.where(special, es, p), jnp.where(special, -os, -q)),
                    )
                )
            u, v = parts
            return [(u[j][0] + v[j][1], v[j][0] - u[j][1]) for j in range(4)]

        k = row.astype(jnp.float32)
        zero_wave = (0.0, -half, quarter, -quarter)
        waves = (k, half - k, k - half, -k)
        base = spectra(0)
        second = None
        totals = [None] * 4
        saved = [None] * 4
        pending = [None] * 4
        for a in range(fields):
            spec = base if a == 0 else spectra(a)
            for j in range(4):
                cross = base[j][0] * spec[j][0] + base[j][1] * spec[j][1]
                if a == 0:
                    wz = jnp.where(special, float(zero_wave[j]), waves[j])
                    square = wave_x * wave_x + wave_y * wave_y + wz * wz
                    saved[j] = (wz, 1.0 / square)
                    vals[0, j * 8 : j * 8 + 8] = round16(cross)
                    continue
                wz, inverse = saved[j]
                if a == 1:
                    vals[1, j * 8 : j * 8 + 8] = round16(cross)
                    term = -0.5 * cross
                else:
                    weight = (
                        1.5 * wave_x * wave_x,
                        1.5 * wave_y * wave_y,
                        1.5 * wz * wz,
                        3.0 * wave_x * wave_y,
                        3.0 * wave_x * wz,
                        3.0 * wave_y * wz,
                    )[a - 2]
                    term = weight * inverse * cross
                pending[j] = term if pending[j] is None else pending[j] + term
                if a % local == local - 1:
                    rounded = round16(pending[j])
                    totals[j] = rounded if totals[j] is None else totals[j] + rounded
                    pending[j] = None
        for j in range(4):
            high = round16(totals[j])
            vals[2, j * 8 : j * 8 + 8] = high
            vals[3, j * 8 : j * 8 + 8] = totals[j] - high
        total = out_ref[...]
        for start in range(0, 32, PAIRS):
            left, hot = [], []
            for r in range(start, start + PAIRS):
                cell = cell_row(r // 8, first + r % 8)
                spread = [
                    jnp.broadcast_to(part, (16, LANES)).astype(jnp.bfloat16)
                    for part in [vals[i, r : r + 1] for i in range(4)]
                    + [keys[i, pl.ds(cell, 1), :] for i in range(2)]
                ]
                match = spread[4] == iotas[0]
                left.append(
                    jnp.concatenate(
                        [jnp.where(match, spread[i], none) for i in range(4)]
                        + [jnp.where(match, one, none)],
                        axis=0,
                    )
                )
                hot.append(
                    jnp.concatenate(
                        [jnp.where(spread[5] == it, one, none) for it in iotas], axis=0
                    )
                )
            total = total + lax.dot_general(
                jnp.concatenate(left, axis=1),
                jnp.concatenate(hot, axis=1),
                (((1,), (1,)), ((), ())),
                preferred_element_type=jnp.float32,
            )
        out_ref[...] = total
        return carry

    lax.fori_loop(0, quarter // 8, tile, 0)


def relayout_kernel(fields_ref, out_ref):
    for c in range(2):
        for i in range(fields_ref.shape[2]):
            at = (c * fields_ref.shape[2] + i) * LANES
            for h in range(out_ref.shape[1]):
                block = fields_ref[:, c, i, :, h * LANES : (h + 1) * LANES]
                block = block.reshape(16, 2, block.shape[1], LANES)
                for parity in range(2):
                    out_ref[:, h, parity, :, at : at + LANES] = jnp.swapaxes(
                        block[:, parity], 0, 1
                    )


def relayout(fields):
    depth, _, local, planes, yrows = fields.shape
    parts = yrows // LANES
    out = pl.pallas_call(
        relayout_kernel,
        grid=(depth // 32,),
        out_shape=jax.ShapeDtypeStruct(
            (planes, parts, 2, depth // 2, 2 * local * LANES), fields.dtype
        ),
        in_specs=[pl.BlockSpec((32, 2, local, planes, yrows), lambda i: (i, 0, 0, 0, 0))],
        out_specs=pl.BlockSpec(
            (planes, parts, 2, 16, 2 * local * LANES), lambda i: (0, 0, 0, i, 0)
        ),
    )(fields)
    return out.reshape(planes * parts, 2, depth // 2, 2 * local * LANES)


def reduce_kernel(field_count, gz_count, mine_ref, out_ref, parts, answer, send, recv, send2, recv2):
    devices = field_count * gz_count
    me_field, me_gz = lax.axis_index("field"), lax.axis_index("gz")
    me = me_field * gz_count + me_gz

    def peer(step):
        other = lax.rem(me + step, devices)
        return other, (other // gz_count, lax.rem(other, gz_count))

    barrier = pltpu.get_barrier_semaphore()

    def greet(step, carry):
        _, place = peer(step)
        pl.semaphore_signal(
            barrier, inc=1, device_id=place, device_id_type=pl.DeviceIdType.MESH
        )
        return carry

    lax.fori_loop(1, devices, greet, 0)
    pl.semaphore_wait(barrier, devices - 1)

    def scatter(step):
        other, place = peer(step)
        return pltpu.make_async_remote_copy(
            src_ref=mine_ref.at[other],
            dst_ref=parts.at[step],
            send_sem=send.at[step],
            recv_sem=recv.at[step],
            device_id=place,
            device_id_type=pl.DeviceIdType.MESH,
        )

    def gather(step):
        _, place = peer(step)
        return pltpu.make_async_remote_copy(
            src_ref=answer,
            dst_ref=out_ref.at[me],
            send_sem=send2.at[step],
            recv_sem=recv2.at[step],
            device_id=place,
            device_id_type=pl.DeviceIdType.MESH,
        )

    def start(copy):
        def run(step, carry):
            copy(step).start()
            return carry

        lax.fori_loop(1, devices, run, 0)

    start(scatter)

    def collect(step, total):
        scatter(step).wait_recv()
        return total + parts[step]

    answer[...] = lax.fori_loop(1, devices, collect, mine_ref[me])
    start(gather)
    out_ref[me] = answer[...]

    def finish(step, carry):
        scatter(step).wait_send()
        gather(step).wait()
        return carry

    lax.fori_loop(1, devices, finish, 0)


def all_reduce(total, field_count, gz_count):
    devices = field_count * gz_count
    rows = max(1, total.shape[0] // devices)
    total = jnp.pad(total, ((0, devices * rows - total.shape[0]), (0, 0)))
    total = total.reshape(devices, rows, LANES)
    return pl.pallas_call(
        functools.partial(reduce_kernel, field_count, gz_count),
        out_shape=jax.ShapeDtypeStruct(total.shape, jnp.float32),
        in_specs=[pl.BlockSpec(memory_space=pltpu.VMEM)],
        out_specs=pl.BlockSpec(memory_space=pltpu.VMEM),
        scratch_shapes=[
            pltpu.VMEM(total.shape, jnp.float32),
            pltpu.VMEM(total.shape[1:], jnp.float32),
            pltpu.SemaphoreType.DMA((devices,)),
            pltpu.SemaphoreType.DMA((devices,)),
            pltpu.SemaphoreType.DMA((devices,)),
            pltpu.SemaphoreType.DMA((devices,)),
        ],
        compiler_params=pltpu.CompilerParams(collective_id=0, has_side_effects=True),
    )(total).reshape(devices * rows, LANES)


SLOTS = 6
KEPT = 5


def wave_tables(length):
    quarter, half = length // 4, length // 2
    unit = 2.0 * math.pi / length

    def pair(rows, stride):
        row = np.arange(rows)[None, :, None] * stride
        depth = 2 * np.arange(half)[None, None, :] + np.arange(2)[:, None, None]
        angle = (row * depth % length).astype(np.float32) * np.float32(unit)
        return np.cos(angle), np.sin(angle)

    ca, sa = pair(quarter // 16, 16)
    cb, sb = pair(16, 1)
    return np.stack([ca, sa]), np.stack([cb, sb])


def build_table(length, coarse_ref, fine_ref, table):
    quarter, half = length // 4, length // 2
    factor = 1.0 / math.sqrt(length)
    parts = table.shape[0]
    wide = half // parts

    def rows_of(a, carry):
        rows = pl.ds(pl.multiple_of(a * 16, 16), 16)
        under = pl.ds(pl.multiple_of(quarter + a * 16, 16), 16)
        for parity in range(2):
            for q in range(parts):
                at = slice(q * wide, (q + 1) * wide)
                ca, sa = (coarse_ref[i, parity, pl.ds(a, 1), at] for i in range(2))
                cb, sb = (fine_ref[i, parity, :, at] for i in range(2))
                cos_part = (ca * cb - sa * sb) * factor
                sin_part = (sa * cb + ca * sb) * factor
                row = lax.broadcasted_iota(jnp.int32, sin_part.shape, 0) + a
                column = lax.broadcasted_iota(jnp.int32, sin_part.shape, 1)
                alternate = (1 - 2 * (column % 2)).astype(jnp.float32) * factor
                sin_part = jnp.where(row == 0, alternate, sin_part)
                table[q, parity, rows, :] = cos_part.astype(jnp.bfloat16)
                table[q, parity, under, :] = sin_part.astype(jnp.bfloat16)
        return carry

    lax.fori_loop(0, quarter // 16, rows_of, 0)


def split_keys(index, keys):
    depth = index.shape[1]

    def block(g, carry):
        word = index[g]
        mu = lax.shift_right_logical(word, 16)
        shell = word & 65535
        rows = pl.ds(pl.multiple_of(g * depth, depth), depth)
        keys[0, rows, :] = (mu + MUBINS * lax.shift_right_logical(shell, 7)).astype(jnp.float32)
        keys[1, rows, :] = (shell & (LANES - 1)).astype(jnp.float32)
        return carry

    lax.fori_loop(0, index.shape[0], block, 0)


def arrange(length, me_field, stage, spread, chunk):
    planes = stage.shape[3]
    rows = pl.ds(pl.multiple_of(chunk * 16, 16), 16)

    def put(block, h, i, c):
        block = block.reshape(16, 2, planes, LANES)
        for parity in range(2):
            spread[:, h, i, parity, rows, c * LANES : (c + 1) * LANES] = jnp.swapaxes(
                block[:, parity], 0, 1
            )

    def take(c, i, h):
        return stage[:, c, i, :, h * LANES : (h + 1) * LANES]

    @pl.when(me_field % 2 == 0)
    def _():
        for c in range(2):
            for i in range(2):
                for h in range(2):
                    put(take(c, i, h), h, i, c)

    @pl.when(me_field % 2 == 1)
    def _():
        wave_x = lax.broadcasted_iota(jnp.int32, (planes, LANES), 0).astype(jnp.float32)
        wave_x = wave_x + float(length // 4)
        squared = me_field == 1
        for h in range(2):
            wave_y = lax.broadcasted_iota(jnp.int32, (planes, LANES), 1).astype(jnp.float32)
            wave_y = wave_y + float(length // 8 + h * LANES)
            first = jnp.where(squared, 1.5 * wave_x * wave_x, wave_x)[None]
            other = jnp.where(squared, 1.5 * wave_y * wave_y, wave_y)[None]
            for c in range(2):
                value = first * take(c, 0, h).astype(jnp.float32)
                value = value + other * take(c, 1, h).astype(jnp.float32)
                put(value.astype(jnp.bfloat16), h, 0, c)


def accumulate(table, land, prod, plane, fresh):
    half = prod.shape[2]

    def group(n, carry):
        a, parity = n // 2, n % 2
        right = land[plane, a, parity].reshape(-1, land.shape[-1])

        def rows_of(r, inner):
            rows = pl.ds(pl.multiple_of(r * 256, 256), 256)
            part = jnp.dot(
                table[plane, parity, rows, :], right, preferred_element_type=jnp.float32
            )
            prod[a, parity, rows, :] = part if fresh else prod[a, parity, rows, :] + part
            return inner

        return lax.fori_loop(0, half // 256, rows_of, carry)

    lax.fori_loop(0, 2 * KEPT, group, 0)


def histogram(length, plane, prod, vals, keys, acc):
    quarter, half = length // 4, length // 2
    acc[...] = jnp.zeros_like(acc)
    lane = lax.broadcasted_iota(jnp.int32, (8, LANES), 1).astype(jnp.float32)
    wave_x = (length // 4 + plane // 2).astype(jnp.float32)
    wave_y = (length // 8 + (plane % 2) * LANES).astype(jnp.float32) + lane
    flat = wave_x * wave_x + wave_y * wave_y
    low_iota = lax.broadcasted_iota(jnp.int32, (16, LANES), 0).astype(jnp.float32)
    iotas = [(low_iota + 16.0 * j).astype(jnp.bfloat16) for j in range(LANES // 16)]
    one = jnp.ones((16, LANES), jnp.bfloat16)
    none = jnp.zeros((16, LANES), jnp.bfloat16)

    def cell_row(j, k):
        start = 1 - (k + quarter - 1) // quarter
        return (
            k,
            half - k,
            half + k - quarter * start,
            length - k - quarter * start,
        )[j]

    def tile(t, edge):
        first = t * 8 if edge else pl.multiple_of(t * 8, 8)
        row = lax.broadcasted_iota(jnp.int32, (8, LANES), 0) + first
        special = row == 0

        def load(a, c, parity, sine):
            at = pl.ds(sine * quarter + first, 8)
            return prod[a, parity, at, c * LANES : (c + 1) * LANES]

        def spectra(a):
            parts = []
            for c in range(2):
                ec, oc = load(a, c, 0, 0), load(a, c, 1, 0)
                es, os = load(a, c, 0, 1), load(a, c, 1, 1)
                p, q, m, n = ec + oc, es + os, ec - oc, os - es
                if edge:
                    parts.append(
                        (
                            (p, jnp.where(special, 0.0, q)),
                            (m, jnp.where(special, 0.0, n)),
                            (jnp.where(special, es, m), jnp.where(special, os, -n)),
                            (jnp.where(special, es, p), jnp.where(special, -os, -q)),
                        )
                    )
                else:
                    parts.append(((p, q), (m, n), (m, n), (p, q)))
            u, v = parts
            result = []
            for j in range(4):
                if edge or j < 2:
                    result.append((u[j][0] + v[j][1], v[j][0] - u[j][1]))
                else:
                    result.append((u[j][0] - v[j][1], v[j][0] + u[j][1]))
            return result

        k = row.astype(jnp.float32)
        zero_wave = (0.0, -half, quarter, -quarter)
        waves = [k, half - k, k - half, -k]
        if edge:
            waves = [jnp.where(special, float(z), w) for z, w in zip(zero_wave, waves)]
            inverse = [1.0 / (flat + w * w) for w in waves]
        else:
            inverse = [1.0 / (flat + w * w) for w in waves[:2]]
            inverse = [inverse[0], inverse[1], inverse[1], inverse[0]]
        cross_b, base, first_cross, cubic, mixed = (spectra(a) for a in range(KEPT))
        for j in range(4):
            re, im = base[j]
            auto = re * re + im * im
            pair = re * first_cross[j][0] + im * first_cross[j][1]
            w = waves[j]
            three, half_more = 3.0 * w, 1.5 * (w * w)
            qre = mixed[j][0] + three * cross_b[j][0] + half_more * cubic[j][0]
            qim = mixed[j][1] + three * cross_b[j][1] + half_more * cubic[j][1]
            quad = inverse[j] * (re * qre + im * qim) - 0.5 * pair
            vals[0, j * 8 : j * 8 + 8] = auto
            vals[1, j * 8 : j * 8 + 8] = pair
            vals[2, j * 8 : j * 8 + 8] = quad
        total = acc[...]
        for start in range(0, 32, PAIRS):
            left, hot = [], []
            for r in range(start, start + PAIRS):
                cell = cell_row(r // 8, first + r % 8)
                spread = [
                    jnp.broadcast_to(part, (16, LANES)).astype(jnp.bfloat16)
                    for part in [vals[i, r : r + 1] for i in range(3)]
                    + [keys[i, pl.ds(cell, 1), :] for i in range(2)]
                ]
                match = spread[3] == iotas[0]
                left.append(
                    jnp.concatenate(
                        [jnp.where(match, spread[i], none) for i in range(3)]
                        + [jnp.where(match, one, none)],
                        axis=0,
                    )
                )
                hot.append(
                    jnp.concatenate(
                        [jnp.where(spread[4] == it, one, none) for it in iotas], axis=0
                    )
                )
            total = total + lax.dot_general(
                jnp.concatenate(left, axis=1),
                jnp.concatenate(hot, axis=1),
                (((1,), (1,)), ((), ())),
                preferred_element_type=jnp.float32,
            )
        acc[...] = total

    tile(0, True)

    def step(t, carry):
        tile(t, False)
        return carry

    lax.fori_loop(1, quarter // 8, step, 0)


def whole_kernel(
    length, coarse_ref, fine_ref, fields_ref, shells_ref, mubins_ref, out_ref,
    stage, spread, mix, joined, land, prod, table, raw, index_out, index, keys, vals, acc,
    parts, answer,
    stage_sem, raw_sem, index_sent, index_come, mix_sent, mix_come, land_sent, land_come,
    part_sent, part_come, answer_sent, answer_come,
):
    fields, cores = 4, 2
    planes_z = land.shape[0]
    gz_count = planes_z * cores
    devices = fields * gz_count
    me_field, me_gz = lax.axis_index("field"), lax.axis_index("gz")
    me = me_field * gz_count + me_gz
    me_plane, me_core = me_gz // cores, me_gz % cores
    chunks = fields_ref.shape[0] // 32
    MESH = pl.DeviceIdType.MESH

    def loop(low, high, run):
        def step(i, carry):
            run(i)
            return carry

        lax.fori_loop(low, high, step, 0)

    barrier = pltpu.get_barrier_semaphore()

    def greet(step):
        other = lax.rem(me + step, devices)
        pl.semaphore_signal(
            barrier, inc=1, device_id=(other // gz_count, lax.rem(other, gz_count)),
            device_id_type=MESH,
        )

    loop(1, devices, greet)

    def raw_copy(n):
        b = n % gz_count
        lanes = pl.ds(pl.multiple_of((b % 2) * LANES, LANES), LANES)
        at = (slice(None), me_field * (gz_count // 2) + b // 2, lanes)
        return [
            pltpu.make_async_copy(ref.at[at], raw.at[i, b], raw_sem.at[i])
            for i, ref in enumerate((shells_ref, mubins_ref))
        ]

    def fetch(n):
        return pltpu.make_async_copy(
            fields_ref.at[pl.ds(n * 32, 32)], stage.at[n % 2], stage_sem.at[n % 2]
        )

    loop(0, gz_count, lambda n: [copy.start() for copy in raw_copy(n)])
    for n in range(2):
        fetch(n).start()

    def target(i):
        plane = lax.rem(me_plane + 2 + i // 2, planes_z)
        return plane * cores + lax.rem(me_core + i, cores)

    for i in range(2):
        pltpu.make_async_copy(raw.at[i], raw.at[i], raw_sem.at[i]).wait()

    def join(n):
        index_out[n] = raw[0, n] + raw[1, n] * 65536

    loop(0, gz_count, join)
    pl.semaphore_wait(barrier, devices - 1)

    def index_send(i):
        g = target(i)

        @pl.when(g != me_gz)
        def _():
            pltpu.make_async_remote_copy(
                src_ref=index_out.at[g], dst_ref=index.at[me_gz],
                send_sem=index_sent, recv_sem=index_come,
                device_id=(me_field, g), device_id_type=MESH,
            ).start()

        @pl.when(g == me_gz)
        def _():
            pltpu.make_async_copy(index_out.at[g], index.at[g], index_come).start()

    loop(0, gz_count, index_send)

    def place(n):
        fetch(n).wait()
        arrange(length, me_field, stage.at[n % 2], spread, n)

        @pl.when(n + 2 < chunks)
        def _():
            fetch(n + 2).start()

    loop(0, chunks, place)

    even = 1 - me_field % 2
    slot = even * (me_field + 1) + (1 - even) * ((15 - 5 * me_field) // 2)

    def mix_send(i):
        g = target(i)

        def piece(f, s):
            return spread.at[f * (gz_count // 2) + g // 2, g % 2, s]

        def send(f, s):
            pltpu.make_async_remote_copy(
                src_ref=piece(f, s), dst_ref=mix.at[g, slot + s],
                send_sem=mix_sent, recv_sem=mix_come.at[g],
                device_id=(f, me_gz), device_id_type=MESH,
            ).start()

        def keep(s):
            pltpu.make_async_copy(
                piece(me_field, s), mix.at[g, slot + s], mix_come.at[g]
            ).start()

        others = [lax.rem(me_field + 2, 4), me_field + 1 - 2 * (me_field % 2), 3 - me_field]
        for f in others:
            send(f, 0)
        keep(0)

        @pl.when(even == 1)
        def _():
            for f in others:
                send(f, 1)
            keep(1)

    loop(0, gz_count, mix_send)
    build_table(length, coarse_ref, fine_ref, table)

    def join_send(i):
        g = target(i)
        pltpu.make_async_copy(mix.at[g], mix.at[g], mix_come.at[g]).wait()
        wave_x = (length // 4 + me_field * (gz_count // 2) + g // 2).astype(jnp.float32)
        lane = lax.broadcasted_iota(jnp.int32, (1, 2 * LANES), 1) % LANES
        wave_y = (length // 8 + (g % 2) * LANES + lane).astype(jnp.float32)
        weight = 3.0 * wave_x * wave_y
        for parity in range(2):
            value = mix[g, 5, parity].astype(jnp.float32)
            value = value + weight * mix[g, 4, parity].astype(jnp.float32)
            joined[g, parity] = value.astype(jnp.bfloat16)
        pairs = (
            (mix.at[g, pl.ds(0, 4)], land.at[me_plane, pl.ds(0, 4), :, me_core]),
            (joined.at[g], land.at[me_plane, 4, :, me_core]),
        )

        @pl.when(g != me_gz)
        def _():
            for source, goal in pairs:
                pltpu.make_async_remote_copy(
                    src_ref=source, dst_ref=goal,
                    send_sem=land_sent, recv_sem=land_come.at[me_gz],
                    device_id=(me_field, g), device_id_type=MESH,
                ).start()

        @pl.when(g == me_gz)
        def _():
            for source, goal in pairs:
                pltpu.make_async_copy(source, goal, land_come.at[me_gz]).start()

    loop(0, gz_count // 2, join_send)
    pltpu.make_async_copy(index, index, index_come).wait()
    split_keys(index, keys)
    loop(gz_count // 2, gz_count, join_send)

    for j in range(planes_z):
        plane = lax.rem(me_plane + planes_z + 2 - j, planes_z)
        for core in range(cores):
            block = land.at[plane, :, :, core]
            pltpu.make_async_copy(block, block, land_come.at[plane * cores + core]).wait()
        accumulate(table, land, prod, plane, j == 0)

    histogram(length, me_field * gz_count + me_gz, prod, vals, keys, acc)

    ranks = acc.shape[0] // 8
    root = lax.rem(me_gz, fields) == me_field

    def part_copy(r):
        return pltpu.make_async_remote_copy(
            src_ref=acc.at[pl.ds(pl.multiple_of(r * 8, 8), 8)], dst_ref=parts.at[me],
            send_sem=part_sent, recv_sem=part_come,
            device_id=(lax.rem(r, fields), r), device_id_type=MESH,
        )

    def part_send(n):
        r = lax.rem(me_gz + n, ranks)

        @pl.when((r != me_gz) | jnp.logical_not(root))
        def _():
            part_copy(r).start()

    loop(0, ranks, part_send)

    def answer_copy(step):
        other = lax.rem(me + step, devices)
        return pltpu.make_async_remote_copy(
            src_ref=answer.at[me_gz], dst_ref=answer.at[me_gz],
            send_sem=answer_sent, recv_sem=answer_come,
            device_id=(other // gz_count, lax.rem(other, gz_count)), device_id_type=MESH,
        )

    @pl.when(root)
    def _():
        parts[me] = acc[pl.ds(pl.multiple_of(me_gz * 8, 8), 8), :]
        rest = parts.at[pl.ds(0, devices - 1)]
        pltpu.make_async_copy(rest, rest, part_come).wait()
        answer[me_gz] = lax.fori_loop(
            1, devices, lambda d, total: total + parts[d], parts[0]
        )
        loop(1, devices, lambda step: answer_copy(step).start())
        got = answer.at[pl.ds(0, ranks - 1)]
        pltpu.make_async_copy(got, got, answer_come).wait()
        pltpu.make_async_copy(rest, rest, answer_sent).wait()
        pltpu.make_async_copy(got, got, part_sent).wait()

    @pl.when(jnp.logical_not(root))
    def _():
        pltpu.make_async_copy(answer, answer, answer_come).wait()
        pltpu.make_async_copy(answer, answer, part_sent).wait()

    for hi in range(2):
        scale = 1.0 / jnp.maximum(answer[6 + hi], 1.0)
        for m in range(3):
            out_ref[m, :, hi * LANES : (hi + 1) * LANES] = answer[2 * m + hi] * scale

    sent = index_out.at[pl.ds(0, gz_count - 1)]
    pltpu.make_async_copy(sent, sent, index_sent).wait()
    sent = mix.at[pl.ds(0, gz_count - 1), pl.ds(0, KEPT)]
    pltpu.make_async_copy(sent, sent, land_sent).wait()

    @pl.when(even == 1)
    def _():
        sent = spread.at[pl.ds(0, 12)]
        pltpu.make_async_copy(sent, sent, mix_sent).wait()

    @pl.when(even == 0)
    def _():
        sent = spread.at[pl.ds(0, 12), :, 0]
        pltpu.make_async_copy(sent, sent, mix_sent).wait()


def whole(fields, shells, mubins, gz_count):
    depth, _, local, planes, yrows = fields.shape
    length = depth * gz_count
    half = length // 2
    coarse, fine = wave_tables(length)
    vmem, anywhere = pl.BlockSpec(memory_space=pltpu.VMEM), pl.BlockSpec(memory_space=pl.ANY)
    wide = 2 * LANES
    dma = pltpu.SemaphoreType.DMA
    low = jnp.bfloat16
    return pl.pallas_call(
        functools.partial(whole_kernel, length),
        out_shape=jax.ShapeDtypeStruct((3, MUBINS, SHELLS), jnp.float32),
        in_specs=[vmem, vmem, anywhere, anywhere, anywhere],
        out_specs=vmem,
        scratch_shapes=[
            pltpu.VMEM((2, 32) + fields.shape[1:], low),
            pltpu.VMEM((planes, 2, local, 2, depth // 2, wide), low),
            pltpu.VMEM((gz_count, SLOTS, 2, depth // 2, wide), low),
            pltpu.VMEM((gz_count, 2, depth // 2, wide), low),
            pltpu.VMEM((gz_count // 2, KEPT, 2, 2, depth // 2, wide), low),
            pltpu.VMEM((KEPT, 2, half, wide), jnp.float32),
            pltpu.VMEM((gz_count // 2, 2, half, depth), low),
            pltpu.VMEM((2, gz_count, depth, LANES), jnp.int32),
            pltpu.VMEM((gz_count, depth, LANES), jnp.int32),
            pltpu.VMEM((gz_count, depth, LANES), jnp.int32),
            pltpu.VMEM((2, length, LANES), jnp.float32),
            pltpu.VMEM((3, 32, LANES), jnp.float32),
            pltpu.VMEM((4 * LOW, LANES), jnp.float32),
            pltpu.VMEM((4 * gz_count, 8, LANES), jnp.float32),
            pltpu.VMEM((8, 8, LANES), jnp.float32),
            dma((2,)), dma((2,)), dma, dma, dma, dma((gz_count,)), dma, dma((gz_count,)),
            dma, dma, dma, dma,
        ],
        compiler_params=pltpu.CompilerParams(
            vmem_limit_bytes=60 * 1024 * 1024, collective_id=2, has_side_effects=True
        ),
    )(jnp.asarray(coarse), jnp.asarray(fine), fields, shells, mubins)


def body(fields, shells, mubins):
    depth_local, _, local_fields, planes, yrows = fields.shape
    gz_count, field_count = lax.axis_size("gz"), lax.axis_size("field")
    devices = gz_count * field_count
    length = depth_local * gz_count
    half = length // 2
    plane_rows = planes * yrows
    width = plane_rows // devices
    me_gz, me_field = lax.axis_index("gz"), lax.axis_index("field")

    if (field_count, gz_count, local_fields, planes, yrows) == (4, 8, 2, 16, 256):
        if depth_local == 256 and (SHELLS, MUBINS) == (256, 8):
            return whole(fields, shells, mubins, gz_count)

    exchange = width == LANES and depth_local % 32 == 0
    if exchange:
        lines = relayout(fields)
    else:
        lines = fields.reshape(depth_local // 2, 2, 2, local_fields, devices, width)
        lines = lines.transpose(4, 1, 0, 2, 3, 5).reshape(
            devices, 2, depth_local // 2, 2 * local_fields * width
        )

    share = planes // field_count
    shells, mubins = (
        lax.dynamic_slice_in_dim(ids, me_field * share, share, 1) for ids in (shells, mubins)
    )
    index = (shells + mubins * 65536).reshape(depth_local, gz_count, width).transpose(1, 0, 2)

    span = 2 * local_fields * LANES
    table = quarter_tables(length, jnp.minimum(me_gz, 0))
    column = (me_field * gz_count + me_gz) * width + jnp.arange(LANES, dtype=jnp.int32)
    waves = jnp.stack([length // 4 + column // yrows, length // 8 + column % yrows])
    waves = jnp.pad(waves.astype(jnp.float32), ((0, 6), (0, 0)))
    landed = (field_count, gz_count, 2, depth_local // 2, span)
    scratch = [
        pltpu.VMEM((field_count, 2, half, span), jnp.float32),
        pltpu.VMEM((4, 32, LANES), jnp.float32),
        pltpu.VMEM((2, length, LANES), jnp.float32),
    ]
    vmem, anywhere = pl.BlockSpec(memory_space=pltpu.VMEM), pl.BlockSpec(memory_space=pl.ANY)
    if exchange:
        run, places, wide = (
            functools.partial(exchange_kernel, length, field_count, gz_count),
            anywhere,
            dict(collective_id=1, has_side_effects=True),
        )
        scratch += [
            pltpu.VMEM(landed, jnp.bfloat16),
            pltpu.VMEM((gz_count, depth_local, LANES), jnp.int32),
            pltpu.SemaphoreType.DMA((2, devices)),
            pltpu.SemaphoreType.DMA((2, devices)),
            pltpu.SemaphoreType.DMA((2,)),
            pltpu.SemaphoreType.DMA((gz_count,)),
            pltpu.SemaphoreType.DMA((gz_count,)),
            pltpu.SemaphoreType.DMA,
        ]
    else:
        run, places, wide = functools.partial(local_kernel, length), vmem, {}
        lines = lax.all_to_all(lines, ("field", "gz"), split_axis=0, concat_axis=0, tiled=True)
        lines = lines.reshape(landed[:-1] + (2 * local_fields, width))
        lines = jnp.pad(lines, ((0, 0),) * 5 + ((0, LANES - width),)).reshape(landed)
        index = lax.all_to_all(index, "gz", split_axis=0, concat_axis=0, tiled=True)
        index = jnp.pad(index, ((0, 0), (0, 0), (0, LANES - width)), constant_values=SHELLS)

    total = pl.pallas_call(
        run,
        out_shape=jax.ShapeDtypeStruct((ROWS * LOW, LANES), jnp.float32),
        in_specs=[vmem, places, places, vmem],
        out_specs=vmem,
        scratch_shapes=scratch,
        compiler_params=pltpu.CompilerParams(vmem_limit_bytes=56 * 1024 * 1024, **wide),
    )(table, lines, index, waves)

    total = total.reshape(ROWS, LOW, LANES)
    total = jnp.concatenate([total[:2], total[2:3] + total[3:4], total[4:]])
    total = all_reduce(total.reshape(-1, LANES), field_count, gz_count)[: 4 * LOW]
    total = total.reshape(4, 2, MUBINS, LANES).transpose(0, 2, 3, 1)
    total = total.reshape(4, MUBINS, SHELLS)
    return total[:3] / jnp.maximum(total[3], 1.0)[None]


def solution(mesh):
    in_specs = (P("gz", None, "field", None, None), P("gz", None, None), P("gz", None, None))
    return jax.shard_map(body, mesh=mesh, in_specs=in_specs, out_specs=P(), check_vma=False)
```

```python
import functools
import math

import jax
import jax.numpy as jnp
import numpy as np
from jax import lax
from jax.experimental import pallas as pl
from jax.experimental.pallas import tpu as pltpu
from jax.sharding import PartitionSpec as P

SHELLS = 256
MUBINS = 8
LANES = 128
LOW = 16
ROWS = 5
PAIRS = 8


def quarter_tables(length, zero):
    quarter, half = length // 4, length // 2
    unit = 2.0 * math.pi / length
    factor = 1.0 / math.sqrt(length)

    def pair(rows, stride):
        shape = (2, rows, half)
        parity = lax.broadcasted_iota(jnp.int32, shape, 0)
        row = lax.broadcasted_iota(jnp.int32, shape, 1) * stride + zero
        depth = 2 * lax.broadcasted_iota(jnp.int32, shape, 2) + parity
        angle = (row * depth % length).astype(jnp.float32) * unit
        return jnp.cos(angle), jnp.sin(angle)

    fine = 16
    ca, sa, cb, sb = lax.optimization_barrier(pair(quarter // fine, fine) + pair(fine, 1))
    ca, sa, cb, sb = ca[:, :, None], sa[:, :, None], cb[:, None], sb[:, None]
    cos_part = ((ca * cb - sa * sb) * factor).reshape(2, quarter, half)
    sin_part = ((sa * cb + ca * sb) * factor).reshape(2, quarter, half)
    row = lax.broadcasted_iota(jnp.int32, sin_part.shape, 1)
    column = lax.broadcasted_iota(jnp.int32, sin_part.shape, 2)
    alternate = (1 - 2 * (column % 2)).astype(jnp.float32) * factor
    sin_part = jnp.where(row == 0, alternate, sin_part)
    return jnp.concatenate(
        [cos_part.astype(jnp.bfloat16), sin_part.astype(jnp.bfloat16)], axis=1
    )


def round16(value):
    return value.astype(jnp.bfloat16).astype(jnp.float32)


def unpack(index_ref, keys):
    depth = index_ref.shape[1]

    def block(g, carry):
        word = index_ref[g]
        mu = word // 65536
        key = (word - mu * 65536) * MUBINS + mu
        upper = key // LOW
        rows = pl.ds(pl.multiple_of(g * depth, depth), depth)
        keys[0, rows, :] = (key - upper * LOW).astype(jnp.float32)
        keys[1, rows, :] = upper.astype(jnp.float32)
        return carry

    lax.fori_loop(0, index_ref.shape[0], block, 0)


def products(table_ref, lines_ref, prod, parity):
    half = table_ref.shape[1]

    def group(f, carry):
        right = lines_ref[f, :, parity].reshape(half, lines_ref.shape[-1])

        def rows_of(i, inner):
            rows = pl.ds(pl.multiple_of(i * 256, 256), 256)
            prod[f, parity, rows, :] = jnp.dot(
                table_ref[parity, rows, :], right, preferred_element_type=jnp.float32
            )
            return inner

        return lax.fori_loop(0, half // 256, rows_of, carry)

    lax.fori_loop(0, prod.shape[0], group, 0)


def local_kernel(length, table_ref, lines_ref, index_ref, wave_ref, out_ref, prod, vals, keys):
    unpack(index_ref, keys)
    products(table_ref, lines_ref, prod, 0)
    products(table_ref, lines_ref, prod, 1)
    bins(length, wave_ref, out_ref, prod, vals, keys)


def exchange_kernel(
    length, field_count, gz_count, table_ref, lines_ref, index_ref, wave_ref, out_ref,
    prod, vals, keys, lines, index, send, recv, own, index_send, index_recv, index_own,
):
    devices = field_count * gz_count
    me_field, me_gz = lax.axis_index("field"), lax.axis_index("gz")
    far = gz_count // 2
    mine = (gz_count - far) * field_count

    def peer(step):
        f = lax.rem(me_field + lax.rem(step, field_count), field_count)
        g = lax.rem(me_gz + step // field_count + far, gz_count)
        return f, g

    def others(run):
        def loop(step, carry):
            run(step)
            return carry

        lax.fori_loop(0, mine, loop, 0)
        lax.fori_loop(mine + 1, devices, loop, 0)

    def along(run):
        def loop(step, carry):
            run(step)
            return carry

        lax.fori_loop(1, gz_count, loop, 0)

    barrier = pltpu.get_barrier_semaphore()
    others(
        lambda step: pl.semaphore_signal(
            barrier, inc=1, device_id=peer(step), device_id_type=pl.DeviceIdType.MESH
        )
    )
    pl.semaphore_wait(barrier, devices - 1)

    def index_copy(step):
        g = lax.rem(me_gz + step, gz_count)
        return pltpu.make_async_remote_copy(
            src_ref=index_ref.at[g],
            dst_ref=index.at[me_gz],
            send_sem=index_send.at[step],
            recv_sem=index_recv.at[step],
            device_id=(me_field, g),
            device_id_type=pl.DeviceIdType.MESH,
        )

    def lines_copy(parity):
        def copy(step):
            f, g = peer(step)
            return pltpu.make_async_remote_copy(
                src_ref=lines_ref.at[f * gz_count + g, parity],
                dst_ref=lines.at[me_field, me_gz, parity],
                send_sem=send.at[parity, step],
                recv_sem=recv.at[parity, step],
                device_id=(f, g),
                device_id_type=pl.DeviceIdType.MESH,
            )

        return copy

    along(lambda step: index_copy(step).start())
    for parity in range(2):
        others(lambda step: lines_copy(parity)(step).start())
    me = me_field * gz_count + me_gz
    kept = [
        pltpu.make_async_copy(
            lines_ref.at[me, parity], lines.at[me_field, me_gz, parity], own.at[parity]
        )
        for parity in range(2)
    ]
    kept_index = pltpu.make_async_copy(index_ref.at[me_gz], index.at[me_gz], index_own)
    for copy in kept + [kept_index]:
        copy.start()

    kept_index.wait()
    along(lambda step: index_copy(step).wait_recv())
    unpack(index, keys)
    for parity in range(2):
        kept[parity].wait()
        others(lambda step: lines_copy(parity)(step).wait_recv())
        products(table_ref, lines, prod, parity)
    bins(length, wave_ref, out_ref, prod, vals, keys)
    along(lambda step: index_copy(step).wait_send())
    for parity in range(2):
        others(lambda step: lines_copy(parity)(step).wait_send())


def bins(length, wave_ref, out_ref, prod, vals, keys):
    quarter, half = length // 4, length // 2
    groups, local = prod.shape[0], prod.shape[3] // (2 * LANES)
    fields = groups * local
    out_ref[...] = jnp.zeros_like(out_ref)
    wave_x = wave_ref[0:1, :]
    wave_y = wave_ref[1:2, :]
    low_iota = lax.broadcasted_iota(jnp.int32, (16, LANES), 0).astype(jnp.float32)
    iotas = [(low_iota + 16.0 * j).astype(jnp.bfloat16) for j in range(LANES // 16)]
    one = jnp.ones((16, LANES), jnp.bfloat16)
    none = jnp.zeros((16, LANES), jnp.bfloat16)

    def cell_row(j, k):
        start = 1 - (k + quarter - 1) // quarter
        return (
            k,
            half - k,
            half + k - quarter * start,
            length - k - quarter * start,
        )[j]

    def tile(t, carry):
        first = pl.multiple_of(t * 8, 8)
        row = lax.broadcasted_iota(jnp.int32, (8, LANES), 0) + first
        special = row == 0

        def load(a, c, parity, sine):
            g, i = a // local, a % local
            at = (c * local + i) * LANES
            return prod[g, parity, pl.ds(sine * quarter + first, 8), at : at + LANES]

        def spectra(a):
            parts = []
            for c in range(2):
                ec, oc = load(a, c, 0, 0), load(a, c, 1, 0)
                es, os = load(a, c, 0, 1), load(a, c, 1, 1)
                p, q, m, n = ec + oc, es + os, ec - oc, os - es
                parts.append(
                    (
                        (p, jnp.where(special, 0.0, q)),
                        (m, jnp.where(special, 0.0, n)),
                        (jnp.where(special, es, m), jnp.where(special, os, -n)),
                        (jnp.where(special, es, p), jnp.where(special, -os, -q)),
                    )
                )
            u, v = parts
            return [(u[j][0] + v[j][1], v[j][0] - u[j][1]) for j in range(4)]

        k = row.astype(jnp.float32)
        zero_wave = (0.0, -half, quarter, -quarter)
        waves = (k, half - k, k - half, -k)
        base = spectra(0)
        second = None
        totals = [None] * 4
        saved = [None] * 4
        pending = [None] * 4
        for a in range(fields):
            spec = base if a == 0 else spectra(a)
            for j in range(4):
                cross = base[j][0] * spec[j][0] + base[j][1] * spec[j][1]
                if a == 0:
                    wz = jnp.where(special, float(zero_wave[j]), waves[j])
                    square = wave_x * wave_x + wave_y * wave_y + wz * wz
                    saved[j] = (wz, 1.0 / square)
                    vals[0, j * 8 : j * 8 + 8] = round16(cross)
                    continue
                wz, inverse = saved[j]
                if a == 1:
                    vals[1, j * 8 : j * 8 + 8] = round16(cross)
                    term = -0.5 * cross
                else:
                    weight = (
                        1.5 * wave_x * wave_x,
                        1.5 * wave_y * wave_y,
                        1.5 * wz * wz,
                        3.0 * wave_x * wave_y,
                        3.0 * wave_x * wz,
                        3.0 * wave_y * wz,
                    )[a - 2]
                    term = weight * inverse * cross
                pending[j] = term if pending[j] is None else pending[j] + term
                if a % local == local - 1:
                    rounded = round16(pending[j])
                    totals[j] = rounded if totals[j] is None else totals[j] + rounded
                    pending[j] = None
        for j in range(4):
            high = round16(totals[j])
            vals[2, j * 8 : j * 8 + 8] = high
            vals[3, j * 8 : j * 8 + 8] = totals[j] - high
        total = out_ref[...]
        for start in range(0, 32, PAIRS):
            left, hot = [], []
            for r in range(start, start + PAIRS):
                cell = cell_row(r // 8, first + r % 8)
                spread = [
                    jnp.broadcast_to(part, (16, LANES)).astype(jnp.bfloat16)
                    for part in [vals[i, r : r + 1] for i in range(4)]
                    + [keys[i, pl.ds(cell, 1), :] for i in range(2)]
                ]
                match = spread[4] == iotas[0]
                left.append(
                    jnp.concatenate(
                        [jnp.where(match, spread[i], none) for i in range(4)]
                        + [jnp.where(match, one, none)],
                        axis=0,
                    )
                )
                hot.append(
                    jnp.concatenate(
                        [jnp.where(spread[5] == it, one, none) for it in iotas], axis=0
                    )
                )
            total = total + lax.dot_general(
                jnp.concatenate(left, axis=1),
                jnp.concatenate(hot, axis=1),
                (((1,), (1,)), ((), ())),
                preferred_element_type=jnp.float32,
            )
        out_ref[...] = total
        return carry

    lax.fori_loop(0, quarter // 8, tile, 0)


def relayout_kernel(fields_ref, out_ref):
    for c in range(2):
        for i in range(fields_ref.shape[2]):
            at = (c * fields_ref.shape[2] + i) * LANES
            for h in range(out_ref.shape[1]):
                block = fields_ref[:, c, i, :, h * LANES : (h + 1) * LANES]
                block = block.reshape(16, 2, block.shape[1], LANES)
                for parity in range(2):
                    out_ref[:, h, parity, :, at : at + LANES] = jnp.swapaxes(
                        block[:, parity], 0, 1
                    )


def relayout(fields):
    depth, _, local, planes, yrows = fields.shape
    parts = yrows // LANES
    out = pl.pallas_call(
        relayout_kernel,
        grid=(depth // 32,),
        out_shape=jax.ShapeDtypeStruct(
            (planes, parts, 2, depth // 2, 2 * local * LANES), fields.dtype
        ),
        in_specs=[pl.BlockSpec((32, 2, local, planes, yrows), lambda i: (i, 0, 0, 0, 0))],
        out_specs=pl.BlockSpec(
            (planes, parts, 2, 16, 2 * local * LANES), lambda i: (0, 0, 0, i, 0)
        ),
    )(fields)
    return out.reshape(planes * parts, 2, depth // 2, 2 * local * LANES)


def reduce_kernel(field_count, gz_count, mine_ref, out_ref, parts, answer, send, recv, send2, recv2):
    devices = field_count * gz_count
    me_field, me_gz = lax.axis_index("field"), lax.axis_index("gz")
    me = me_field * gz_count + me_gz

    def peer(step):
        other = lax.rem(me + step, devices)
        return other, (other // gz_count, lax.rem(other, gz_count))

    barrier = pltpu.get_barrier_semaphore()

    def greet(step, carry):
        _, place = peer(step)
        pl.semaphore_signal(
            barrier, inc=1, device_id=place, device_id_type=pl.DeviceIdType.MESH
        )
        return carry

    lax.fori_loop(1, devices, greet, 0)
    pl.semaphore_wait(barrier, devices - 1)

    def scatter(step):
        other, place = peer(step)
        return pltpu.make_async_remote_copy(
            src_ref=mine_ref.at[other],
            dst_ref=parts.at[step],
            send_sem=send.at[step],
            recv_sem=recv.at[step],
            device_id=place,
            device_id_type=pl.DeviceIdType.MESH,
        )

    def gather(step):
        _, place = peer(step)
        return pltpu.make_async_remote_copy(
            src_ref=answer,
            dst_ref=out_ref.at[me],
            send_sem=send2.at[step],
            recv_sem=recv2.at[step],
            device_id=place,
            device_id_type=pl.DeviceIdType.MESH,
        )

    def start(copy):
        def run(step, carry):
            copy(step).start()
            return carry

        lax.fori_loop(1, devices, run, 0)

    start(scatter)

    def collect(step, total):
        scatter(step).wait_recv()
        return total + parts[step]

    answer[...] = lax.fori_loop(1, devices, collect, mine_ref[me])
    start(gather)
    out_ref[me] = answer[...]

    def finish(step, carry):
        scatter(step).wait_send()
        gather(step).wait()
        return carry

    lax.fori_loop(1, devices, finish, 0)


def all_reduce(total, field_count, gz_count):
    devices = field_count * gz_count
    rows = max(1, total.shape[0] // devices)
    total = jnp.pad(total, ((0, devices * rows - total.shape[0]), (0, 0)))
    total = total.reshape(devices, rows, LANES)
    return pl.pallas_call(
        functools.partial(reduce_kernel, field_count, gz_count),
        out_shape=jax.ShapeDtypeStruct(total.shape, jnp.float32),
        in_specs=[pl.BlockSpec(memory_space=pltpu.VMEM)],
        out_specs=pl.BlockSpec(memory_space=pltpu.VMEM),
        scratch_shapes=[
            pltpu.VMEM(total.shape, jnp.float32),
            pltpu.VMEM(total.shape[1:], jnp.float32),
            pltpu.SemaphoreType.DMA((devices,)),
            pltpu.SemaphoreType.DMA((devices,)),
            pltpu.SemaphoreType.DMA((devices,)),
            pltpu.SemaphoreType.DMA((devices,)),
        ],
        compiler_params=pltpu.CompilerParams(collective_id=0, has_side_effects=True),
    )(total).reshape(devices * rows, LANES)


SLOTS = 6
KEPT = 5


def wave_tables(length):
    quarter, half = length // 4, length // 2
    unit = 2.0 * math.pi / length

    def pair(rows, stride):
        row = np.arange(rows)[None, :, None] * stride
        depth = 2 * np.arange(half)[None, None, :] + np.arange(2)[:, None, None]
        angle = (row * depth % length).astype(np.float32) * np.float32(unit)
        return np.cos(angle), np.sin(angle)

    ca, sa = pair(quarter // 16, 16)
    cb, sb = pair(16, 1)
    return np.stack([ca, sa]), np.stack([cb, sb])


def build_table(length, coarse_ref, fine_ref, table):
    quarter, half = length // 4, length // 2
    factor = 1.0 / math.sqrt(length)
    parts = table.shape[0]
    wide = half // parts

    def rows_of(a, carry):
        rows = pl.ds(pl.multiple_of(a * 16, 16), 16)
        under = pl.ds(pl.multiple_of(quarter + a * 16, 16), 16)
        for parity in range(2):
            for q in range(parts):
                at = slice(q * wide, (q + 1) * wide)
                ca, sa = (coarse_ref[i, parity, pl.ds(a, 1), at] for i in range(2))
                cb, sb = (fine_ref[i, parity, :, at] for i in range(2))
                cos_part = (ca * cb - sa * sb) * factor
                sin_part = (sa * cb + ca * sb) * factor
                row = lax.broadcasted_iota(jnp.int32, sin_part.shape, 0) + a
                column = lax.broadcasted_iota(jnp.int32, sin_part.shape, 1)
                alternate = (1 - 2 * (column % 2)).astype(jnp.float32) * factor
                sin_part = jnp.where(row == 0, alternate, sin_part)
                table[q, parity, rows, :] = cos_part.astype(jnp.bfloat16)
                table[q, parity, under, :] = sin_part.astype(jnp.bfloat16)
        return carry

    lax.fori_loop(0, quarter // 16, rows_of, 0)


def split_keys(index, keys):
    depth = index.shape[1]

    def block(g, carry):
        word = index[g]
        mu = lax.shift_right_logical(word, 16)
        shell = word & 65535
        rows = pl.ds(pl.multiple_of(g * depth, depth), depth)
        keys[0, rows, :] = (mu + MUBINS * lax.shift_right_logical(shell, 7)).astype(jnp.float32)
        keys[1, rows, :] = (shell & (LANES - 1)).astype(jnp.float32)
        return carry

    lax.fori_loop(0, index.shape[0], block, 0)


def arrange(length, me_field, stage, spread, chunk):
    planes = stage.shape[3]
    rows = pl.ds(pl.multiple_of(chunk * 16, 16), 16)

    def put(block, h, i, c):
        block = block.reshape(16, 2, planes, LANES)
        for parity in range(2):
            spread[:, h, i, parity, rows, c * LANES : (c + 1) * LANES] = jnp.swapaxes(
                block[:, parity], 0, 1
            )

    def take(c, i, h):
        return stage[:, c, i, :, h * LANES : (h + 1) * LANES]

    @pl.when(me_field % 2 == 0)
    def _():
        for c in range(2):
            for i in range(2):
                for h in range(2):
                    put(take(c, i, h), h, i, c)

    @pl.when(me_field % 2 == 1)
    def _():
        wave_x = lax.broadcasted_iota(jnp.int32, (planes, LANES), 0).astype(jnp.float32)
        wave_x = wave_x + float(length // 4)
        squared = me_field == 1
        for h in range(2):
            wave_y = lax.broadcasted_iota(jnp.int32, (planes, LANES), 1).astype(jnp.float32)
            wave_y = wave_y + float(length // 8 + h * LANES)
            first = jnp.where(squared, 1.5 * wave_x * wave_x, wave_x)[None]
            other = jnp.where(squared, 1.5 * wave_y * wave_y, wave_y)[None]
            for c in range(2):
                value = first * take(c, 0, h).astype(jnp.float32)
                value = value + other * take(c, 1, h).astype(jnp.float32)
                put(value.astype(jnp.bfloat16), h, 0, c)


def accumulate(table, land, prod, plane, fresh):
    def group(n, carry):
        a, parity = n // 2, n % 2
        right = land[plane, a, parity].reshape(-1, land.shape[-1])

        part = jnp.dot(table[plane, parity], right, preferred_element_type=jnp.float32)
        prod[a, parity] = part if fresh else prod[a, parity] + part
        return carry

    lax.fori_loop(0, 2 * KEPT, group, 0)


def histogram(length, plane, prod, vals, keys, acc):
    quarter, half = length // 4, length // 2
    acc[...] = jnp.zeros_like(acc)
    lane = lax.broadcasted_iota(jnp.int32, (8, LANES), 1).astype(jnp.float32)
    wave_x = (length // 4 + plane // 2).astype(jnp.float32)
    wave_y = (length // 8 + (plane % 2) * LANES).astype(jnp.float32) + lane
    flat = wave_x * wave_x + wave_y * wave_y
    low_iota = lax.broadcasted_iota(jnp.int32, (16, LANES), 0).astype(jnp.float32)
    iotas = [(low_iota + 16.0 * j).astype(jnp.bfloat16) for j in range(LANES // 16)]
    one = jnp.ones((16, LANES), jnp.bfloat16)
    none = jnp.zeros((16, LANES), jnp.bfloat16)

    def cell_row(j, k):
        start = 1 - (k + quarter - 1) // quarter
        return (
            k,
            half - k,
            half + k - quarter * start,
            length - k - quarter * start,
        )[j]

    def tile(t, edge):
        first = t * 8 if edge else pl.multiple_of(t * 8, 8)
        row = lax.broadcasted_iota(jnp.int32, (8, LANES), 0) + first
        special = row == 0

        def load(a, c, parity, sine):
            at = pl.ds(sine * quarter + first, 8)
            return prod[a, parity, at, c * LANES : (c + 1) * LANES]

        def spectra(a):
            parts = []
            for c in range(2):
                ec, oc = load(a, c, 0, 0), load(a, c, 1, 0)
                es, os = load(a, c, 0, 1), load(a, c, 1, 1)
                p, q, m, n = ec + oc, es + os, ec - oc, os - es
                if edge:
                    parts.append(
                        (
                            (p, jnp.where(special, 0.0, q)),
                            (m, jnp.where(special, 0.0, n)),
                            (jnp.where(special, es, m), jnp.where(special, os, -n)),
                            (jnp.where(special, es, p), jnp.where(special, -os, -q)),
                        )
                    )
                else:
                    parts.append(((p, q), (m, n), (m, n), (p, q)))
            u, v = parts
            result = []
            for j in range(4):
                if edge or j < 2:
                    result.append((u[j][0] + v[j][1], v[j][0] - u[j][1]))
                else:
                    result.append((u[j][0] - v[j][1], v[j][0] + u[j][1]))
            return result

        k = row.astype(jnp.float32)
        zero_wave = (0.0, -half, quarter, -quarter)
        waves = [k, half - k, k - half, -k]
        if edge:
            waves = [jnp.where(special, float(z), w) for z, w in zip(zero_wave, waves)]
            inverse = [1.0 / (flat + w * w) for w in waves]
        else:
            inverse = [1.0 / (flat + w * w) for w in waves[:2]]
            inverse = [inverse[0], inverse[1], inverse[1], inverse[0]]
        cross_b, base, first_cross, cubic, mixed = (spectra(a) for a in range(KEPT))
        for j in range(4):
            re, im = base[j]
            auto = re * re + im * im
            pair = re * first_cross[j][0] + im * first_cross[j][1]
            w = waves[j]
            three, half_more = 3.0 * w, 1.5 * (w * w)
            qre = mixed[j][0] + three * cross_b[j][0] + half_more * cubic[j][0]
            qim = mixed[j][1] + three * cross_b[j][1] + half_more * cubic[j][1]
            quad = inverse[j] * (re * qre + im * qim) - 0.5 * pair
            vals[0, j * 8 : j * 8 + 8] = auto
            vals[1, j * 8 : j * 8 + 8] = pair
            vals[2, j * 8 : j * 8 + 8] = quad
        total = acc[...]
        for start in range(0, 32, PAIRS):
            left, hot = [], []
            for r in range(start, start + PAIRS):
                cell = cell_row(r // 8, first + r % 8)
                spread = [
                    jnp.broadcast_to(part, (16, LANES)).astype(jnp.bfloat16)
                    for part in [vals[i, r : r + 1] for i in range(3)]
                    + [keys[i, pl.ds(cell, 1), :] for i in range(2)]
                ]
                match = spread[3] == iotas[0]
                left.append(
                    jnp.concatenate(
                        [jnp.where(match, spread[i], none) for i in range(3)]
                        + [jnp.where(match, one, none)],
                        axis=0,
                    )
                )
                hot.append(
                    jnp.concatenate(
                        [jnp.where(spread[4] == it, one, none) for it in iotas], axis=0
                    )
                )
            total = total + lax.dot_general(
                jnp.concatenate(left, axis=1),
                jnp.concatenate(hot, axis=1),
                (((1,), (1,)), ((), ())),
                preferred_element_type=jnp.float32,
            )
        acc[...] = total

    tile(0, True)

    def step(t, carry):
        tile(t, False)
        return carry

    lax.fori_loop(1, quarter // 8, step, 0)


def whole_kernel(
    length, coarse_ref, fine_ref, fields_ref, shells_ref, mubins_ref, out_ref,
    stage, spread, mix, joined, land, prod, table, raw, index_out, index, keys, vals, acc,
    parts, answer,
    stage_sem, raw_sem, index_sent, index_come, mix_sent, mix_come, land_sent, land_come,
    part_sent, part_come, answer_sent, answer_come,
):
    fields, cores = 4, 2
    planes_z = land.shape[0]
    gz_count = planes_z * cores
    devices = fields * gz_count
    me_field, me_gz = lax.axis_index("field"), lax.axis_index("gz")
    me = me_field * gz_count + me_gz
    me_plane, me_core = me_gz // cores, me_gz % cores
    chunks = fields_ref.shape[0] // 32
    MESH = pl.DeviceIdType.MESH

    def loop(low, high, run):
        def step(i, carry):
            run(i)
            return carry

        lax.fori_loop(low, high, step, 0)

    barrier = pltpu.get_barrier_semaphore()

    def greet(step):
        other = lax.rem(me + step, devices)
        pl.semaphore_signal(
            barrier, inc=1, device_id=(other // gz_count, lax.rem(other, gz_count)),
            device_id_type=MESH,
        )

    loop(1, devices, greet)

    def raw_copy(n):
        b = n % gz_count
        lanes = pl.ds(pl.multiple_of((b % 2) * LANES, LANES), LANES)
        at = (slice(None), me_field * (gz_count // 2) + b // 2, lanes)
        return [
            pltpu.make_async_copy(ref.at[at], raw.at[i, b], raw_sem.at[i])
            for i, ref in enumerate((shells_ref, mubins_ref))
        ]

    def fetch(n):
        return pltpu.make_async_copy(
            fields_ref.at[pl.ds(n * 32, 32)], stage.at[n % 2], stage_sem.at[n % 2]
        )

    loop(0, gz_count, lambda n: [copy.start() for copy in raw_copy(n)])
    for n in range(2):
        fetch(n).start()

    side = 1 + 2 * (me_plane // 2)

    def target(i):
        turn = i // 2
        steps = (2 + 11 * turn * (turn - 1) // 2 - turn) * side
        plane = lax.rem(me_plane + steps, planes_z)
        return plane * cores + lax.rem(me_core + i, cores)

    for i in range(2):
        pltpu.make_async_copy(raw.at[i], raw.at[i], raw_sem.at[i]).wait()

    def join(n):
        index_out[n] = raw[0, n] + raw[1, n] * 65536

    loop(0, gz_count, join)
    pl.semaphore_wait(barrier, devices - 1)

    def index_send(i):
        g = target(i)

        @pl.when(g != me_gz)
        def _():
            pltpu.make_async_remote_copy(
                src_ref=index_out.at[g], dst_ref=index.at[me_gz],
                send_sem=index_sent, recv_sem=index_come,
                device_id=(me_field, g), device_id_type=MESH,
            ).start()

        @pl.when(g == me_gz)
        def _():
            pltpu.make_async_copy(index_out.at[g], index.at[g], index_come).start()

    loop(0, gz_count, index_send)

    def place(n):
        fetch(n).wait()
        arrange(length, me_field, stage.at[n % 2], spread, n)

        @pl.when(n + 2 < chunks)
        def _():
            fetch(n + 2).start()

    loop(0, chunks, place)

    even = 1 - me_field % 2
    slot = even * (me_field + 1) + (1 - even) * ((15 - 5 * me_field) // 2)

    def mix_send(i):
        g = target(i)

        def piece(f, s):
            return spread.at[f * (gz_count // 2) + g // 2, g % 2, s]

        def send(f, s):
            pltpu.make_async_remote_copy(
                src_ref=piece(f, s), dst_ref=mix.at[g, slot + s],
                send_sem=mix_sent, recv_sem=mix_come.at[g],
                device_id=(f, me_gz), device_id_type=MESH,
            ).start()

        def keep(s):
            pltpu.make_async_copy(
                piece(me_field, s), mix.at[g, slot + s], mix_come.at[g]
            ).start()

        others = [lax.rem(me_field + 2, 4), me_field + 1 - 2 * (me_field % 2), 3 - me_field]
        for f in others:
            send(f, 0)
        keep(0)

        @pl.when(even == 1)
        def _():
            for f in others:
                send(f, 1)
            keep(1)

    loop(0, gz_count, mix_send)
    build_table(length, coarse_ref, fine_ref, table)

    def join_send(i):
        g = target(i)
        pltpu.make_async_copy(mix.at[g], mix.at[g], mix_come.at[g]).wait()
        wave_x = (length // 4 + me_field * (gz_count // 2) + g // 2).astype(jnp.float32)
        lane = lax.broadcasted_iota(jnp.int32, (1, 2 * LANES), 1) % LANES
        wave_y = (length // 8 + (g % 2) * LANES + lane).astype(jnp.float32)
        weight = 3.0 * wave_x * wave_y
        for parity in range(2):
            value = mix[g, 5, parity].astype(jnp.float32)
            value = value + weight * mix[g, 4, parity].astype(jnp.float32)
            joined[g, parity] = value.astype(jnp.bfloat16)
        pairs = (
            (mix.at[g, pl.ds(0, 4)], land.at[me_plane, pl.ds(0, 4), :, me_core]),
            (joined.at[g], land.at[me_plane, 4, :, me_core]),
        )

        @pl.when(g != me_gz)
        def _():
            for source, goal in pairs:
                pltpu.make_async_remote_copy(
                    src_ref=source, dst_ref=goal,
                    send_sem=land_sent, recv_sem=land_come.at[me_gz],
                    device_id=(me_field, g), device_id_type=MESH,
                ).start()

        @pl.when(g == me_gz)
        def _():
            for source, goal in pairs:
                pltpu.make_async_copy(source, goal, land_come.at[me_gz]).start()

    loop(0, gz_count // 2, join_send)
    pltpu.make_async_copy(index, index, index_come).wait()
    split_keys(index, keys)
    loop(gz_count // 2, gz_count, join_send)

    near = 1 - 2 * (me_plane % 2)
    for j, steps in enumerate((2, near, 0, 2 + near)):
        plane = lax.rem(me_plane + steps, planes_z)
        for core in range(cores):
            block = land.at[plane, :, :, core]
            pltpu.make_async_copy(block, block, land_come.at[plane * cores + core]).wait()
        accumulate(table, land, prod, plane, j == 0)

    histogram(length, me_field * gz_count + me_gz, prod, vals, keys, acc)

    ranks = acc.shape[0] // 8
    root = lax.rem(me_gz, fields) == me_field

    def part_copy(r):
        return pltpu.make_async_remote_copy(
            src_ref=acc.at[pl.ds(pl.multiple_of(r * 8, 8), 8)], dst_ref=parts.at[me],
            send_sem=part_sent, recv_sem=part_come,
            device_id=(lax.rem(r, fields), r), device_id_type=MESH,
        )

    def part_send(n):
        r = lax.rem(me_gz + n, ranks)

        @pl.when((r != me_gz) | jnp.logical_not(root))
        def _():
            part_copy(r).start()

    loop(0, ranks, part_send)

    def answer_copy(step):
        other = lax.rem(me + step, devices)
        return pltpu.make_async_remote_copy(
            src_ref=answer.at[me_gz], dst_ref=answer.at[me_gz],
            send_sem=answer_sent, recv_sem=answer_come,
            device_id=(other // gz_count, lax.rem(other, gz_count)), device_id_type=MESH,
        )

    @pl.when(root)
    def _():
        parts[me] = acc[pl.ds(pl.multiple_of(me_gz * 8, 8), 8), :]
        rest = parts.at[pl.ds(0, devices - 1)]
        pltpu.make_async_copy(rest, rest, part_come).wait()
        answer[me_gz] = lax.fori_loop(
            1, devices, lambda d, total: total + parts[d], parts[0]
        )
        loop(1, devices, lambda step: answer_copy(step).start())
        got = answer.at[pl.ds(0, ranks - 1)]
        pltpu.make_async_copy(got, got, answer_come).wait()
        pltpu.make_async_copy(rest, rest, answer_sent).wait()
        pltpu.make_async_copy(got, got, part_sent).wait()

    @pl.when(jnp.logical_not(root))
    def _():
        pltpu.make_async_copy(answer, answer, answer_come).wait()
        pltpu.make_async_copy(answer, answer, part_sent).wait()

    for hi in range(2):
        scale = 1.0 / jnp.maximum(answer[6 + hi], 1.0)
        for m in range(3):
            out_ref[m, :, hi * LANES : (hi + 1) * LANES] = answer[2 * m + hi] * scale

    sent = index_out.at[pl.ds(0, gz_count - 1)]
    pltpu.make_async_copy(sent, sent, index_sent).wait()
    sent = mix.at[pl.ds(0, gz_count - 1), pl.ds(0, KEPT)]
    pltpu.make_async_copy(sent, sent, land_sent).wait()

    @pl.when(even == 1)
    def _():
        sent = spread.at[pl.ds(0, 12)]
        pltpu.make_async_copy(sent, sent, mix_sent).wait()

    @pl.when(even == 0)
    def _():
        sent = spread.at[pl.ds(0, 12), :, 0]
        pltpu.make_async_copy(sent, sent, mix_sent).wait()


def whole(fields, shells, mubins, gz_count):
    depth, _, local, planes, yrows = fields.shape
    length = depth * gz_count
    half = length // 2
    coarse, fine = wave_tables(length)
    vmem, anywhere = pl.BlockSpec(memory_space=pltpu.VMEM), pl.BlockSpec(memory_space=pl.ANY)
    wide = 2 * LANES
    dma = pltpu.SemaphoreType.DMA
    low = jnp.bfloat16
    return pl.pallas_call(
        functools.partial(whole_kernel, length),
        out_shape=jax.ShapeDtypeStruct((3, MUBINS, SHELLS), jnp.float32),
        in_specs=[vmem, vmem, anywhere, anywhere, anywhere],
        out_specs=vmem,
        scratch_shapes=[
            pltpu.VMEM((2, 32) + fields.shape[1:], low),
            pltpu.VMEM((planes, 2, local, 2, depth // 2, wide), low),
            pltpu.VMEM((gz_count, SLOTS, 2, depth // 2, wide), low),
            pltpu.VMEM((gz_count, 2, depth // 2, wide), low),
            pltpu.VMEM((gz_count // 2, KEPT, 2, 2, depth // 2, wide), low),
            pltpu.VMEM((KEPT, 2, half, wide), jnp.float32),
            pltpu.VMEM((gz_count // 2, 2, half, depth), low),
            pltpu.VMEM((2, gz_count, depth, LANES), jnp.int32),
            pltpu.VMEM((gz_count, depth, LANES), jnp.int32),
            pltpu.VMEM((gz_count, depth, LANES), jnp.int32),
            pltpu.VMEM((2, length, LANES), jnp.float32),
            pltpu.VMEM((3, 32, LANES), jnp.float32),
            pltpu.VMEM((4 * LOW, LANES), jnp.float32),
            pltpu.VMEM((4 * gz_count, 8, LANES), jnp.float32),
            pltpu.VMEM((8, 8, LANES), jnp.float32),
            dma((2,)), dma((2,)), dma, dma, dma, dma((gz_count,)), dma, dma((gz_count,)),
            dma, dma, dma, dma,
        ],
        compiler_params=pltpu.CompilerParams(
            vmem_limit_bytes=60 * 1024 * 1024, collective_id=2, has_side_effects=True
        ),
    )(jnp.asarray(coarse), jnp.asarray(fine), fields, shells, mubins)


def body(fields, shells, mubins):
    depth_local, _, local_fields, planes, yrows = fields.shape
    gz_count, field_count = lax.axis_size("gz"), lax.axis_size("field")
    devices = gz_count * field_count
    length = depth_local * gz_count
    half = length // 2
    plane_rows = planes * yrows
    width = plane_rows // devices
    me_gz, me_field = lax.axis_index("gz"), lax.axis_index("field")

    if (field_count, gz_count, local_fields, planes, yrows) == (4, 8, 2, 16, 256):
        if depth_local == 256 and (SHELLS, MUBINS) == (256, 8):
            return whole(fields, shells, mubins, gz_count)

    exchange = width == LANES and depth_local % 32 == 0
    if exchange:
        lines = relayout(fields)
    else:
        lines = fields.reshape(depth_local // 2, 2, 2, local_fields, devices, width)
        lines = lines.transpose(4, 1, 0, 2, 3, 5).reshape(
            devices, 2, depth_local // 2, 2 * local_fields * width
        )

    share = planes // field_count
    shells, mubins = (
        lax.dynamic_slice_in_dim(ids, me_field * share, share, 1) for ids in (shells, mubins)
    )
    index = (shells + mubins * 65536).reshape(depth_local, gz_count, width).transpose(1, 0, 2)

    span = 2 * local_fields * LANES
    table = quarter_tables(length, jnp.minimum(me_gz, 0))
    column = (me_field * gz_count + me_gz) * width + jnp.arange(LANES, dtype=jnp.int32)
    waves = jnp.stack([length // 4 + column // yrows, length // 8 + column % yrows])
    waves = jnp.pad(waves.astype(jnp.float32), ((0, 6), (0, 0)))
    landed = (field_count, gz_count, 2, depth_local // 2, span)
    scratch = [
        pltpu.VMEM((field_count, 2, half, span), jnp.float32),
        pltpu.VMEM((4, 32, LANES), jnp.float32),
        pltpu.VMEM((2, length, LANES), jnp.float32),
    ]
    vmem, anywhere = pl.BlockSpec(memory_space=pltpu.VMEM), pl.BlockSpec(memory_space=pl.ANY)
    if exchange:
        run, places, wide = (
            functools.partial(exchange_kernel, length, field_count, gz_count),
            anywhere,
            dict(collective_id=1, has_side_effects=True),
        )
        scratch += [
            pltpu.VMEM(landed, jnp.bfloat16),
            pltpu.VMEM((gz_count, depth_local, LANES), jnp.int32),
            pltpu.SemaphoreType.DMA((2, devices)),
            pltpu.SemaphoreType.DMA((2, devices)),
            pltpu.SemaphoreType.DMA((2,)),
            pltpu.SemaphoreType.DMA((gz_count,)),
            pltpu.SemaphoreType.DMA((gz_count,)),
            pltpu.SemaphoreType.DMA,
        ]
    else:
        run, places, wide = functools.partial(local_kernel, length), vmem, {}
        lines = lax.all_to_all(lines, ("field", "gz"), split_axis=0, concat_axis=0, tiled=True)
        lines = lines.reshape(landed[:-1] + (2 * local_fields, width))
        lines = jnp.pad(lines, ((0, 0),) * 5 + ((0, LANES - width),)).reshape(landed)
        index = lax.all_to_all(index, "gz", split_axis=0, concat_axis=0, tiled=True)
        index = jnp.pad(index, ((0, 0), (0, 0), (0, LANES - width)), constant_values=SHELLS)

    total = pl.pallas_call(
        run,
        out_shape=jax.ShapeDtypeStruct((ROWS * LOW, LANES), jnp.float32),
        in_specs=[vmem, places, places, vmem],
        out_specs=vmem,
        scratch_shapes=scratch,
        compiler_params=pltpu.CompilerParams(vmem_limit_bytes=56 * 1024 * 1024, **wide),
    )(table, lines, index, waves)

    total = total.reshape(ROWS, LOW, LANES)
    total = jnp.concatenate([total[:2], total[2:3] + total[3:4], total[4:]])
    total = all_reduce(total.reshape(-1, LANES), field_count, gz_count)[: 4 * LOW]
    total = total.reshape(4, 2, MUBINS, LANES).transpose(0, 2, 3, 1)
    total = total.reshape(4, MUBINS, SHELLS)
    return total[:3] / jnp.maximum(total[3], 1.0)[None]


def solution(mesh):
    in_specs = (P("gz", None, "field", None, None), P("gz", None, None), P("gz", None, None))
    return jax.shard_map(body, mesh=mesh, in_specs=in_specs, out_specs=P(), check_vma=False)
```

```python
import functools
import math

import jax
import jax.numpy as jnp
import numpy as np
from jax import lax
from jax.experimental import pallas as pl
from jax.experimental.pallas import tpu as pltpu
from jax.sharding import PartitionSpec as P

SHELLS = 256
MUBINS = 8
LANES = 128
LOW = 16
ROWS = 5
PAIRS = 8


def quarter_tables(length, zero):
    quarter, half = length // 4, length // 2
    unit = 2.0 * math.pi / length
    factor = 1.0 / math.sqrt(length)

    def pair(rows, stride):
        shape = (2, rows, half)
        parity = lax.broadcasted_iota(jnp.int32, shape, 0)
        row = lax.broadcasted_iota(jnp.int32, shape, 1) * stride + zero
        depth = 2 * lax.broadcasted_iota(jnp.int32, shape, 2) + parity
        angle = (row * depth % length).astype(jnp.float32) * unit
        return jnp.cos(angle), jnp.sin(angle)

    fine = 16
    ca, sa, cb, sb = lax.optimization_barrier(pair(quarter // fine, fine) + pair(fine, 1))
    ca, sa, cb, sb = ca[:, :, None], sa[:, :, None], cb[:, None], sb[:, None]
    cos_part = ((ca * cb - sa * sb) * factor).reshape(2, quarter, half)
    sin_part = ((sa * cb + ca * sb) * factor).reshape(2, quarter, half)
    row = lax.broadcasted_iota(jnp.int32, sin_part.shape, 1)
    column = lax.broadcasted_iota(jnp.int32, sin_part.shape, 2)
    alternate = (1 - 2 * (column % 2)).astype(jnp.float32) * factor
    sin_part = jnp.where(row == 0, alternate, sin_part)
    return jnp.concatenate(
        [cos_part.astype(jnp.bfloat16), sin_part.astype(jnp.bfloat16)], axis=1
    )


def round16(value):
    return value.astype(jnp.bfloat16).astype(jnp.float32)


def unpack(index_ref, keys):
    depth = index_ref.shape[1]

    def block(g, carry):
        word = index_ref[g]
        mu = word // 65536
        key = (word - mu * 65536) * MUBINS + mu
        upper = key // LOW
        rows = pl.ds(pl.multiple_of(g * depth, depth), depth)
        keys[0, rows, :] = (key - upper * LOW).astype(jnp.float32)
        keys[1, rows, :] = upper.astype(jnp.float32)
        return carry

    lax.fori_loop(0, index_ref.shape[0], block, 0)


def products(table_ref, lines_ref, prod, parity):
    half = table_ref.shape[1]

    def group(f, carry):
        right = lines_ref[f, :, parity].reshape(half, lines_ref.shape[-1])

        def rows_of(i, inner):
            rows = pl.ds(pl.multiple_of(i * 256, 256), 256)
            prod[f, parity, rows, :] = jnp.dot(
                table_ref[parity, rows, :], right, preferred_element_type=jnp.float32
            )
            return inner

        return lax.fori_loop(0, half // 256, rows_of, carry)

    lax.fori_loop(0, prod.shape[0], group, 0)


def local_kernel(length, table_ref, lines_ref, index_ref, wave_ref, out_ref, prod, vals, keys):
    unpack(index_ref, keys)
    products(table_ref, lines_ref, prod, 0)
    products(table_ref, lines_ref, prod, 1)
    bins(length, wave_ref, out_ref, prod, vals, keys)


def exchange_kernel(
    length, field_count, gz_count, table_ref, lines_ref, index_ref, wave_ref, out_ref,
    prod, vals, keys, lines, index, send, recv, own, index_send, index_recv, index_own,
):
    devices = field_count * gz_count
    me_field, me_gz = lax.axis_index("field"), lax.axis_index("gz")
    far = gz_count // 2
    mine = (gz_count - far) * field_count

    def peer(step):
        f = lax.rem(me_field + lax.rem(step, field_count), field_count)
        g = lax.rem(me_gz + step // field_count + far, gz_count)
        return f, g

    def others(run):
        def loop(step, carry):
            run(step)
            return carry

        lax.fori_loop(0, mine, loop, 0)
        lax.fori_loop(mine + 1, devices, loop, 0)

    def along(run):
        def loop(step, carry):
            run(step)
            return carry

        lax.fori_loop(1, gz_count, loop, 0)

    barrier = pltpu.get_barrier_semaphore()
    others(
        lambda step: pl.semaphore_signal(
            barrier, inc=1, device_id=peer(step), device_id_type=pl.DeviceIdType.MESH
        )
    )
    pl.semaphore_wait(barrier, devices - 1)

    def index_copy(step):
        g = lax.rem(me_gz + step, gz_count)
        return pltpu.make_async_remote_copy(
            src_ref=index_ref.at[g],
            dst_ref=index.at[me_gz],
            send_sem=index_send.at[step],
            recv_sem=index_recv.at[step],
            device_id=(me_field, g),
            device_id_type=pl.DeviceIdType.MESH,
        )

    def lines_copy(parity):
        def copy(step):
            f, g = peer(step)
            return pltpu.make_async_remote_copy(
                src_ref=lines_ref.at[f * gz_count + g, parity],
                dst_ref=lines.at[me_field, me_gz, parity],
                send_sem=send.at[parity, step],
                recv_sem=recv.at[parity, step],
                device_id=(f, g),
                device_id_type=pl.DeviceIdType.MESH,
            )

        return copy

    along(lambda step: index_copy(step).start())
    for parity in range(2):
        others(lambda step: lines_copy(parity)(step).start())
    me = me_field * gz_count + me_gz
    kept = [
        pltpu.make_async_copy(
            lines_ref.at[me, parity], lines.at[me_field, me_gz, parity], own.at[parity]
        )
        for parity in range(2)
    ]
    kept_index = pltpu.make_async_copy(index_ref.at[me_gz], index.at[me_gz], index_own)
    for copy in kept + [kept_index]:
        copy.start()

    kept_index.wait()
    along(lambda step: index_copy(step).wait_recv())
    unpack(index, keys)
    for parity in range(2):
        kept[parity].wait()
        others(lambda step: lines_copy(parity)(step).wait_recv())
        products(table_ref, lines, prod, parity)
    bins(length, wave_ref, out_ref, prod, vals, keys)
    along(lambda step: index_copy(step).wait_send())
    for parity in range(2):
        others(lambda step: lines_copy(parity)(step).wait_send())


def bins(length, wave_ref, out_ref, prod, vals, keys):
    quarter, half = length // 4, length // 2
    groups, local = prod.shape[0], prod.shape[3] // (2 * LANES)
    fields = groups * local
    out_ref[...] = jnp.zeros_like(out_ref)
    wave_x = wave_ref[0:1, :]
    wave_y = wave_ref[1:2, :]
    low_iota = lax.broadcasted_iota(jnp.int32, (16, LANES), 0).astype(jnp.float32)
    iotas = [(low_iota + 16.0 * j).astype(jnp.bfloat16) for j in range(LANES // 16)]
    one = jnp.ones((16, LANES), jnp.bfloat16)
    none = jnp.zeros((16, LANES), jnp.bfloat16)

    def cell_row(j, k):
        start = 1 - (k + quarter - 1) // quarter
        return (
            k,
            half - k,
            half + k - quarter * start,
            length - k - quarter * start,
        )[j]

    def tile(t, carry):
        first = pl.multiple_of(t * 8, 8)
        row = lax.broadcasted_iota(jnp.int32, (8, LANES), 0) + first
        special = row == 0

        def load(a, c, parity, sine):
            g, i = a // local, a % local
            at = (c * local + i) * LANES
            return prod[g, parity, pl.ds(sine * quarter + first, 8), at : at + LANES]

        def spectra(a):
            parts = []
            for c in range(2):
                ec, oc = load(a, c, 0, 0), load(a, c, 1, 0)
                es, os = load(a, c, 0, 1), load(a, c, 1, 1)
                p, q, m, n = ec + oc, es + os, ec - oc, os - es
                parts.append(
                    (
                        (p, jnp.where(special, 0.0, q)),
                        (m, jnp.where(special, 0.0, n)),
                        (jnp.where(special, es, m), jnp.where(special, os, -n)),
                        (jnp.where(special, es, p), jnp.where(special, -os, -q)),
                    )
                )
            u, v = parts
            return [(u[j][0] + v[j][1], v[j][0] - u[j][1]) for j in range(4)]

        k = row.astype(jnp.float32)
        zero_wave = (0.0, -half, quarter, -quarter)
        waves = (k, half - k, k - half, -k)
        base = spectra(0)
        second = None
        totals = [None] * 4
        saved = [None] * 4
        pending = [None] * 4
        for a in range(fields):
            spec = base if a == 0 else spectra(a)
            for j in range(4):
                cross = base[j][0] * spec[j][0] + base[j][1] * spec[j][1]
                if a == 0:
                    wz = jnp.where(special, float(zero_wave[j]), waves[j])
                    square = wave_x * wave_x + wave_y * wave_y + wz * wz
                    saved[j] = (wz, 1.0 / square)
                    vals[0, j * 8 : j * 8 + 8] = round16(cross)
                    continue
                wz, inverse = saved[j]
                if a == 1:
                    vals[1, j * 8 : j * 8 + 8] = round16(cross)
                    term = -0.5 * cross
                else:
                    weight = (
                        1.5 * wave_x * wave_x,
                        1.5 * wave_y * wave_y,
                        1.5 * wz * wz,
                        3.0 * wave_x * wave_y,
                        3.0 * wave_x * wz,
                        3.0 * wave_y * wz,
                    )[a - 2]
                    term = weight * inverse * cross
                pending[j] = term if pending[j] is None else pending[j] + term
                if a % local == local - 1:
                    rounded = round16(pending[j])
                    totals[j] = rounded if totals[j] is None else totals[j] + rounded
                    pending[j] = None
        for j in range(4):
            high = round16(totals[j])
            vals[2, j * 8 : j * 8 + 8] = high
            vals[3, j * 8 : j * 8 + 8] = totals[j] - high
        total = out_ref[...]
        for start in range(0, 32, PAIRS):
            left, hot = [], []
            for r in range(start, start + PAIRS):
                cell = cell_row(r // 8, first + r % 8)
                spread = [
                    jnp.broadcast_to(part, (16, LANES)).astype(jnp.bfloat16)
                    for part in [vals[i, r : r + 1] for i in range(4)]
                    + [keys[i, pl.ds(cell, 1), :] for i in range(2)]
                ]
                match = spread[4] == iotas[0]
                left.append(
                    jnp.concatenate(
                        [jnp.where(match, spread[i], none) for i in range(4)]
                        + [jnp.where(match, one, none)],
                        axis=0,
                    )
                )
                hot.append(
                    jnp.concatenate(
                        [jnp.where(spread[5] == it, one, none) for it in iotas], axis=0
                    )
                )
            total = total + lax.dot_general(
                jnp.concatenate(left, axis=1),
                jnp.concatenate(hot, axis=1),
                (((1,), (1,)), ((), ())),
                preferred_element_type=jnp.float32,
            )
        out_ref[...] = total
        return carry

    lax.fori_loop(0, quarter // 8, tile, 0)


def relayout_kernel(fields_ref, out_ref):
    for c in range(2):
        for i in range(fields_ref.shape[2]):
            at = (c * fields_ref.shape[2] + i) * LANES
            for h in range(out_ref.shape[1]):
                block = fields_ref[:, c, i, :, h * LANES : (h + 1) * LANES]
                block = block.reshape(16, 2, block.shape[1], LANES)
                for parity in range(2):
                    out_ref[:, h, parity, :, at : at + LANES] = jnp.swapaxes(
                        block[:, parity], 0, 1
                    )


def relayout(fields):
    depth, _, local, planes, yrows = fields.shape
    parts = yrows // LANES
    out = pl.pallas_call(
        relayout_kernel,
        grid=(depth // 32,),
        out_shape=jax.ShapeDtypeStruct(
            (planes, parts, 2, depth // 2, 2 * local * LANES), fields.dtype
        ),
        in_specs=[pl.BlockSpec((32, 2, local, planes, yrows), lambda i: (i, 0, 0, 0, 0))],
        out_specs=pl.BlockSpec(
            (planes, parts, 2, 16, 2 * local * LANES), lambda i: (0, 0, 0, i, 0)
        ),
    )(fields)
    return out.reshape(planes * parts, 2, depth // 2, 2 * local * LANES)


def reduce_kernel(field_count, gz_count, mine_ref, out_ref, parts, answer, send, recv, send2, recv2):
    devices = field_count * gz_count
    me_field, me_gz = lax.axis_index("field"), lax.axis_index("gz")
    me = me_field * gz_count + me_gz

    def peer(step):
        other = lax.rem(me + step, devices)
        return other, (other // gz_count, lax.rem(other, gz_count))

    barrier = pltpu.get_barrier_semaphore()

    def greet(step, carry):
        _, place = peer(step)
        pl.semaphore_signal(
            barrier, inc=1, device_id=place, device_id_type=pl.DeviceIdType.MESH
        )
        return carry

    lax.fori_loop(1, devices, greet, 0)
    pl.semaphore_wait(barrier, devices - 1)

    def scatter(step):
        other, place = peer(step)
        return pltpu.make_async_remote_copy(
            src_ref=mine_ref.at[other],
            dst_ref=parts.at[step],
            send_sem=send.at[step],
            recv_sem=recv.at[step],
            device_id=place,
            device_id_type=pl.DeviceIdType.MESH,
        )

    def gather(step):
        _, place = peer(step)
        return pltpu.make_async_remote_copy(
            src_ref=answer,
            dst_ref=out_ref.at[me],
            send_sem=send2.at[step],
            recv_sem=recv2.at[step],
            device_id=place,
            device_id_type=pl.DeviceIdType.MESH,
        )

    def start(copy):
        def run(step, carry):
            copy(step).start()
            return carry

        lax.fori_loop(1, devices, run, 0)

    start(scatter)

    def collect(step, total):
        scatter(step).wait_recv()
        return total + parts[step]

    answer[...] = lax.fori_loop(1, devices, collect, mine_ref[me])
    start(gather)
    out_ref[me] = answer[...]

    def finish(step, carry):
        scatter(step).wait_send()
        gather(step).wait()
        return carry

    lax.fori_loop(1, devices, finish, 0)


def all_reduce(total, field_count, gz_count):
    devices = field_count * gz_count
    rows = max(1, total.shape[0] // devices)
    total = jnp.pad(total, ((0, devices * rows - total.shape[0]), (0, 0)))
    total = total.reshape(devices, rows, LANES)
    return pl.pallas_call(
        functools.partial(reduce_kernel, field_count, gz_count),
        out_shape=jax.ShapeDtypeStruct(total.shape, jnp.float32),
        in_specs=[pl.BlockSpec(memory_space=pltpu.VMEM)],
        out_specs=pl.BlockSpec(memory_space=pltpu.VMEM),
        scratch_shapes=[
            pltpu.VMEM(total.shape, jnp.float32),
            pltpu.VMEM(total.shape[1:], jnp.float32),
            pltpu.SemaphoreType.DMA((devices,)),
            pltpu.SemaphoreType.DMA((devices,)),
            pltpu.SemaphoreType.DMA((devices,)),
            pltpu.SemaphoreType.DMA((devices,)),
        ],
        compiler_params=pltpu.CompilerParams(collective_id=0, has_side_effects=True),
    )(total).reshape(devices * rows, LANES)


SLOTS = 6
KEPT = 5


def wave_tables(length):
    quarter, half = length // 4, length // 2
    unit = 2.0 * math.pi / length

    def pair(rows, stride):
        row = np.arange(rows)[None, :, None] * stride
        depth = 2 * np.arange(half)[None, None, :] + np.arange(2)[:, None, None]
        angle = (row * depth % length).astype(np.float32) * np.float32(unit)
        return np.cos(angle), np.sin(angle)

    ca, sa = pair(quarter // 16, 16)
    cb, sb = pair(16, 1)
    return np.stack([ca, sa]), np.stack([cb, sb])


def build_table(length, coarse_ref, fine_ref, table):
    quarter, half = length // 4, length // 2
    factor = 1.0 / math.sqrt(length)
    parts = table.shape[0]
    wide = half // parts

    def rows_of(a, carry):
        rows = pl.ds(pl.multiple_of(a * 16, 16), 16)
        under = pl.ds(pl.multiple_of(quarter + a * 16, 16), 16)
        for parity in range(2):
            for q in range(parts):
                at = slice(q * wide, (q + 1) * wide)
                ca, sa = (coarse_ref[i, parity, pl.ds(a, 1), at] for i in range(2))
                cb, sb = (fine_ref[i, parity, :, at] for i in range(2))
                cos_part = (ca * cb - sa * sb) * factor
                sin_part = (sa * cb + ca * sb) * factor
                row = lax.broadcasted_iota(jnp.int32, sin_part.shape, 0) + a
                column = lax.broadcasted_iota(jnp.int32, sin_part.shape, 1)
                alternate = (1 - 2 * (column % 2)).astype(jnp.float32) * factor
                sin_part = jnp.where(row == 0, alternate, sin_part)
                table[q, parity, rows, :] = cos_part.astype(jnp.bfloat16)
                table[q, parity, under, :] = sin_part.astype(jnp.bfloat16)
        return carry

    lax.fori_loop(0, quarter // 16, rows_of, 0)


def split_keys(index, keys):
    depth = index.shape[1]

    def block(g, carry):
        word = index[g]
        mu = lax.shift_right_logical(word, 16)
        shell = word & 65535
        rows = pl.ds(pl.multiple_of(g * depth, depth), depth)
        keys[0, rows, :] = (mu + MUBINS * lax.shift_right_logical(shell, 7)).astype(jnp.float32)
        keys[1, rows, :] = (shell & (LANES - 1)).astype(jnp.float32)
        return carry

    lax.fori_loop(0, index.shape[0], block, 0)


def arrange(length, me_field, stage, spread, chunk):
    planes = stage.shape[3]
    rows = pl.ds(pl.multiple_of(chunk * 16, 16), 16)

    def put(block, h, i, c):
        block = block.reshape(16, 2, planes, LANES)
        for parity in range(2):
            spread[:, h, i, parity, rows, c * LANES : (c + 1) * LANES] = jnp.swapaxes(
                block[:, parity], 0, 1
            )

    def take(c, i, h):
        return stage[:, c, i, :, h * LANES : (h + 1) * LANES]

    @pl.when(me_field % 2 == 0)
    def _():
        for c in range(2):
            for i in range(2):
                for h in range(2):
                    put(take(c, i, h), h, i, c)

    @pl.when(me_field % 2 == 1)
    def _():
        wave_x = lax.broadcasted_iota(jnp.int32, (planes, LANES), 0).astype(jnp.float32)
        wave_x = wave_x + float(length // 4)
        squared = me_field == 1
        for h in range(2):
            wave_y = lax.broadcasted_iota(jnp.int32, (planes, LANES), 1).astype(jnp.float32)
            wave_y = wave_y + float(length // 8 + h * LANES)
            first = jnp.where(squared, 1.5 * wave_x * wave_x, wave_x)[None]
            other = jnp.where(squared, 1.5 * wave_y * wave_y, wave_y)[None]
            for c in range(2):
                value = first * take(c, 0, h).astype(jnp.float32)
                value = value + other * take(c, 1, h).astype(jnp.float32)
                put(value.astype(jnp.bfloat16), h, 0, c)


def accumulate(table, land, prod, plane, local, fields, start, fresh):
    def group(n, carry):
        a, parity = n // 2, n % 2
        right = land[local, a, parity].reshape(-1, land.shape[-1])
        part = jnp.dot(table[plane, parity], right, preferred_element_type=jnp.float32)
        prod[start + a, parity] = part if fresh else prod[start + a, parity] + part
        return carry

    lax.fori_loop(0, 2 * fields, group, 0)


def histogram(length, plane, prod, vals, keys, acc, low, high):
    quarter, half = length // 4, length // 2
    lane = lax.broadcasted_iota(jnp.int32, (8, LANES), 1).astype(jnp.float32)
    wave_x = (length // 4 + plane // 2).astype(jnp.float32)
    wave_y = (length // 8 + (plane % 2) * LANES).astype(jnp.float32) + lane
    flat = wave_x * wave_x + wave_y * wave_y
    low_iota = lax.broadcasted_iota(jnp.int32, (16, LANES), 0).astype(jnp.float32)
    iotas = [(low_iota + 16.0 * j).astype(jnp.bfloat16) for j in range(LANES // 16)]
    one = jnp.ones((16, LANES), jnp.bfloat16)
    none = jnp.zeros((16, LANES), jnp.bfloat16)

    def cell_row(j, k):
        start = 1 - (k + quarter - 1) // quarter
        return (
            k,
            half - k,
            half + k - quarter * start,
            length - k - quarter * start,
        )[j]

    def tile(t, edge):
        first = t * 8 if edge else pl.multiple_of(t * 8, 8)
        row = lax.broadcasted_iota(jnp.int32, (8, LANES), 0) + first
        special = row == 0

        def load(a, c, parity, sine):
            at = pl.ds(sine * quarter + first, 8)
            return prod[a, parity, at, c * LANES : (c + 1) * LANES]

        def spectra(a):
            parts = []
            for c in range(2):
                ec, oc = load(a, c, 0, 0), load(a, c, 1, 0)
                es, os = load(a, c, 0, 1), load(a, c, 1, 1)
                p, q, m, n = ec + oc, es + os, ec - oc, os - es
                if edge:
                    parts.append(
                        (
                            (p, jnp.where(special, 0.0, q)),
                            (m, jnp.where(special, 0.0, n)),
                            (jnp.where(special, es, m), jnp.where(special, os, -n)),
                            (jnp.where(special, es, p), jnp.where(special, -os, -q)),
                        )
                    )
                else:
                    parts.append(((p, q), (m, n), (m, n), (p, q)))
            u, v = parts
            result = []
            for j in range(4):
                if edge or j < 2:
                    result.append((u[j][0] + v[j][1], v[j][0] - u[j][1]))
                else:
                    result.append((u[j][0] - v[j][1], v[j][0] + u[j][1]))
            return result

        k = row.astype(jnp.float32)
        zero_wave = (0.0, -half, quarter, -quarter)
        waves = [k, half - k, k - half, -k]
        if edge:
            waves = [jnp.where(special, float(z), w) for z, w in zip(zero_wave, waves)]
            inverse = [1.0 / (flat + w * w) for w in waves]
        else:
            inverse = [1.0 / (flat + w * w) for w in waves[:2]]
            inverse = [inverse[0], inverse[1], inverse[1], inverse[0]]
        base, first_cross, cross_b, cubic, mixed = (spectra(a) for a in range(KEPT))
        for j in range(4):
            re, im = base[j]
            auto = re * re + im * im
            pair = re * first_cross[j][0] + im * first_cross[j][1]
            w = waves[j]
            three, half_more = 3.0 * w, 1.5 * (w * w)
            qre = mixed[j][0] + three * cross_b[j][0] + half_more * cubic[j][0]
            qim = mixed[j][1] + three * cross_b[j][1] + half_more * cubic[j][1]
            quad = inverse[j] * (re * qre + im * qim) - 0.5 * pair
            vals[0, j * 8 : j * 8 + 8] = auto
            vals[1, j * 8 : j * 8 + 8] = pair
            vals[2, j * 8 : j * 8 + 8] = quad
        total = acc[...]
        for start in range(0, 32, PAIRS):
            left, hot = [], []
            for r in range(start, start + PAIRS):
                cell = cell_row(r // 8, first + r % 8)
                spread = [
                    jnp.broadcast_to(part, (16, LANES)).astype(jnp.bfloat16)
                    for part in [vals[i, r : r + 1] for i in range(3)]
                    + [keys[i, pl.ds(cell, 1), :] for i in range(2)]
                ]
                match = spread[3] == iotas[0]
                left.append(
                    jnp.concatenate(
                        [jnp.where(match, spread[i], none) for i in range(3)]
                        + [jnp.where(match, one, none)],
                        axis=0,
                    )
                )
                hot.append(
                    jnp.concatenate(
                        [jnp.where(spread[4] == it, one, none) for it in iotas], axis=0
                    )
                )
            total = total + lax.dot_general(
                jnp.concatenate(left, axis=1),
                jnp.concatenate(hot, axis=1),
                (((1,), (1,)), ((), ())),
                preferred_element_type=jnp.float32,
            )
        acc[...] = total

    @pl.when(low == 0)
    def _():
        tile(0, True)

    def step(t, carry):
        tile(t, False)
        return carry

    lax.fori_loop(jnp.maximum(low, 1), high, step, 0)


def whole_kernel(
    length, coarse_ref, fine_ref, fields_ref, shells_ref, mubins_ref, out_ref,
    stage, spread, mix, joined, first, land, prod, table, raw, index_out, index, keys, vals, acc,
    parts, answer,
    stage_sem, raw_sem, index_sent, index_come, mix_sent, mix_come, land_sent, first_come,
    land_come, part_sent, part_come, answer_sent, answer_come,
):
    fields, cores, chunks = 4, 2, 2
    planes_z = table.shape[0]
    gz_count = planes_z * cores
    owners = gz_count // chunks
    devices = fields * gz_count
    me_field, me_gz = lax.axis_index("field"), lax.axis_index("gz")
    me = me_field * gz_count + me_gz
    me_plane, me_core = me_gz // cores, me_gz % cores
    me_half, me_owner = me_gz // owners, me_gz % owners
    steps = fields_ref.shape[0] // 32
    MESH = pl.DeviceIdType.MESH

    def loop(low, high, run):
        def step(i, carry):
            run(i)
            return carry

        lax.fori_loop(low, high, step, 0)

    def wait(ref, sem):
        pltpu.make_async_copy(ref, ref, sem).wait()

    barrier = pltpu.get_barrier_semaphore()

    def greet(step):
        other = lax.rem(me + step, devices)
        pl.semaphore_signal(
            barrier, inc=1, device_id=(other // gz_count, lax.rem(other, gz_count)),
            device_id_type=MESH,
        )

    loop(1, devices, greet)

    def raw_copy(b):
        lanes = pl.ds(pl.multiple_of((b % 2) * LANES, LANES), LANES)
        at = (slice(None), me_field * (gz_count // 2) + b // 2, lanes)
        return [
            pltpu.make_async_copy(ref.at[at], raw.at[i, b], raw_sem.at[i])
            for i, ref in enumerate((shells_ref, mubins_ref))
        ]

    def fetch(n):
        return pltpu.make_async_copy(
            fields_ref.at[pl.ds(n * 32, 32)], stage.at[n % 2], stage_sem.at[n % 2]
        )

    loop(0, gz_count, lambda b: [copy.start() for copy in raw_copy(b)])
    for n in range(2):
        fetch(n).start()
    for i in range(2):
        wait(raw.at[i], raw_sem.at[i])

    def join(n):
        index_out[n] = raw[0, n] + raw[1, n] * 65536

    loop(0, gz_count, join)
    pl.semaphore_wait(barrier, devices - 1)

    def owner_of(i):
        plane = lax.rem(me_plane + 1 + (i % owners) // 2, 2)
        return plane * cores + lax.rem(me_core + i, cores)

    def forward(source, goal, sent, come, g):
        pltpu.make_async_remote_copy(
            src_ref=source, dst_ref=goal, send_sem=sent, recv_sem=come,
            device_id=(me_field, g), device_id_type=MESH,
        ).start()

    def index_send(i):
        chunk, owner = i // owners, owner_of(i)
        b = chunk * owners + owner
        goal = index.at[chunk, me_gz]
        forward(
            index_out.at[b], goal, index_sent, index_come.at[chunk],
            (1 - me_half) * owners + owner,
        )

        @pl.when(owner != me_owner)
        def _():
            forward(
                index_out.at[b], goal, index_sent, index_come.at[chunk],
                me_half * owners + owner,
            )

        @pl.when(owner == me_owner)
        def _():
            pltpu.make_async_copy(index_out.at[b], goal, index_come.at[chunk]).start()

    loop(0, gz_count, index_send)

    def place(n):
        fetch(n).wait()
        arrange(length, me_field, stage.at[n % 2], spread, n)

        @pl.when(n + 2 < steps)
        def _():
            fetch(n + 2).start()

    loop(0, steps, place)

    even = 1 - me_field % 2
    slot = even * (3 * me_field // 2) + (1 - even) * ((13 - 3 * me_field) // 2)

    def mix_send(i):
        b = (i // owners) * owners + owner_of(i)

        def piece(f, s):
            return spread.at[f * (gz_count // 2) + b // 2, b % 2, s]

        def send(f, s):
            pltpu.make_async_remote_copy(
                src_ref=piece(f, s), dst_ref=mix.at[b, slot + s],
                send_sem=mix_sent, recv_sem=mix_come.at[b],
                device_id=(f, me_gz), device_id_type=MESH,
            ).start()

        def keep(s):
            pltpu.make_async_copy(
                piece(me_field, s), mix.at[b, slot + s], mix_come.at[b]
            ).start()

        others = [lax.rem(me_field + 2, 4), me_field + 1 - 2 * (me_field % 2), 3 - me_field]
        for f in others:
            send(f, 0)
        keep(0)

        @pl.when(even == 1)
        def _():
            for f in others:
                send(f, 1)
            keep(1)

    loop(0, gz_count, mix_send)
    build_table(length, coarse_ref, fine_ref, table)
    acc[...] = jnp.zeros_like(acc)

    def join_send(i):
        chunk, owner = i // owners, owner_of(i)
        b = chunk * owners + owner
        wait(mix.at[b], mix_come.at[b])
        wave_x = (length // 4 + me_field * (gz_count // 2) + b // 2).astype(jnp.float32)
        lane = lax.broadcasted_iota(jnp.int32, (1, 2 * LANES), 1) % LANES
        wave_y = (length // 8 + (b % 2) * LANES + lane).astype(jnp.float32)
        weight = 3.0 * wave_x * wave_y
        for parity in range(2):
            value = mix[b, 5, parity].astype(jnp.float32)
            value = value + weight * mix[b, 4, parity].astype(jnp.float32)
            joined[b, parity] = value.astype(jnp.bfloat16)
        base = (mix.at[b, 0], first.at[chunk, me_plane, 0, :, me_core])
        me_near = me_plane % 2
        pairs = (
            (mix.at[b, pl.ds(1, 3)], land.at[chunk, me_near, pl.ds(0, 3), :, me_core]),
            (joined.at[b], land.at[chunk, me_near, 3, :, me_core]),
        )
        forward(*base, land_sent, first_come.at[chunk, me_gz], (1 - me_half) * owners + owner)

        @pl.when(owner != me_owner)
        def _():
            g = me_half * owners + owner
            forward(*base, land_sent, first_come.at[chunk, me_gz], g)
            for source, goal in pairs:
                forward(source, goal, land_sent, land_come.at[chunk, me_owner], g)

        @pl.when(owner == me_owner)
        def _():
            pltpu.make_async_copy(*base, first_come.at[chunk, me_gz]).start()
            for source, goal in pairs:
                pltpu.make_async_copy(source, goal, land_come.at[chunk, me_owner]).start()

    def transform(chunk):
        near = 1 - 2 * (me_plane % 2)
        for n, hop in enumerate((0, near)):
            plane = me_plane + hop
            local = plane % 2
            for core in range(cores):
                wait(land.at[chunk, local, :, :, core], land_come.at[chunk, local * cores + core])
            accumulate(table, land.at[chunk], prod, plane, local, KEPT - 1, 1, n == 0)
        for n in range(planes_z):
            plane = lax.rem(me_plane + n, planes_z)
            for core in range(cores):
                block = first.at[chunk, plane, :, :, core]
                wait(block, first_come.at[chunk, plane * cores + core])
            accumulate(table, first.at[chunk], prod, plane, plane, 1, 0, n == 0)

    tiles = length // 32
    span = tiles // owners

    def bin_lines(chunk, n, count):
        b = me_field * gz_count + chunk * owners + me_owner
        histogram(
            length, b, prod, vals, keys.at[chunk], acc, n * span, (n + count) * span
        )

    loop(0, owners, join_send)
    for chunk in range(chunks):
        wait(index.at[chunk], index_come.at[chunk])
        split_keys(index.at[chunk], keys.at[chunk])
    join_send(owners)
    transform(0)

    def mixed_step(n):
        bin_lines(0, n, 1)

        @pl.when(n < owners - 1)
        def _():
            join_send(owners + 1 + n)

    loop(0, owners, mixed_step)
    transform(1)
    bin_lines(1, 0, owners)

    ranks = acc.shape[0] // 8
    root = lax.rem(me_gz, fields) == me_field

    def part_copy(r):
        return pltpu.make_async_remote_copy(
            src_ref=acc.at[pl.ds(pl.multiple_of(r * 8, 8), 8)], dst_ref=parts.at[me],
            send_sem=part_sent, recv_sem=part_come,
            device_id=(lax.rem(r, fields), r), device_id_type=MESH,
        )

    def part_send(n):
        r = lax.rem(me_gz + n, ranks)

        @pl.when((r != me_gz) | jnp.logical_not(root))
        def _():
            part_copy(r).start()

    loop(0, ranks, part_send)

    def answer_copy(step):
        other = lax.rem(me + step, devices)
        return pltpu.make_async_remote_copy(
            src_ref=answer.at[me_gz], dst_ref=answer.at[me_gz],
            send_sem=answer_sent, recv_sem=answer_come,
            device_id=(other // gz_count, lax.rem(other, gz_count)), device_id_type=MESH,
        )

    @pl.when(root)
    def _():
        parts[me] = acc[pl.ds(pl.multiple_of(me_gz * 8, 8), 8), :]
        rest = parts.at[pl.ds(0, devices - 1)]
        wait(rest, part_come)
        answer[me_gz] = lax.fori_loop(
            1, devices, lambda d, total: total + parts[d], parts[0]
        )
        loop(1, devices, lambda step: answer_copy(step).start())
        got = answer.at[pl.ds(0, ranks - 1)]
        wait(got, answer_come)
        wait(rest, answer_sent)
        wait(got, part_sent)

    @pl.when(jnp.logical_not(root))
    def _():
        wait(answer, answer_come)
        wait(answer, part_sent)

    for hi in range(2):
        scale = 1.0 / jnp.maximum(0.5 * answer[6 + hi], 1.0)
        for m in range(3):
            half_scale = 0.5 * scale if m == 0 else scale
            out_ref[m, :, hi * LANES : (hi + 1) * LANES] = answer[2 * m + hi] * half_scale

    for _ in range(2):
        sent = index_out.at[pl.ds(0, gz_count - 1)]
        wait(sent, index_sent)
    wait(mix.at[:, 0], land_sent)
    wait(mix.at[pl.ds(0, 2 * (owners - 1)), pl.ds(0, KEPT)], land_sent)

    @pl.when(even == 1)
    def _():
        wait(spread.at[pl.ds(0, 12)], mix_sent)

    @pl.when(even == 0)
    def _():
        wait(spread.at[pl.ds(0, 12), :, 0], mix_sent)


def whole(fields, shells, mubins, gz_count):
    depth, _, local, planes, yrows = fields.shape
    length = depth * gz_count
    half = length // 2
    coarse, fine = wave_tables(length)
    vmem, anywhere = pl.BlockSpec(memory_space=pltpu.VMEM), pl.BlockSpec(memory_space=pl.ANY)
    wide = 2 * LANES
    dma = pltpu.SemaphoreType.DMA
    low = jnp.bfloat16
    line_block = (2, depth // 2, wide)
    pair_block = (2, 2, depth // 2, wide)
    return pl.pallas_call(
        functools.partial(whole_kernel, length),
        out_shape=jax.ShapeDtypeStruct((3, MUBINS, SHELLS), jnp.float32),
        in_specs=[vmem, vmem, anywhere, anywhere, anywhere],
        out_specs=vmem,
        scratch_shapes=[
            pltpu.VMEM((2, 32) + fields.shape[1:], low),
            pltpu.VMEM((planes, 2, local) + line_block, low),
            pltpu.VMEM((gz_count, SLOTS) + line_block, low),
            pltpu.VMEM((gz_count,) + line_block, low),
            pltpu.VMEM((2, gz_count // 2, 1) + pair_block, low),
            pltpu.VMEM((2, gz_count // 4, KEPT - 1) + pair_block, low),
            pltpu.VMEM((KEPT, 2, half, wide), jnp.float32),
            pltpu.VMEM((gz_count // 2, 2, half, depth), low),
            pltpu.VMEM((2, gz_count, depth, LANES), jnp.int32),
            pltpu.VMEM((gz_count, depth, LANES), jnp.int32),
            pltpu.VMEM((2, gz_count, depth, LANES), jnp.int32),
            pltpu.VMEM((2, 2, length, LANES), jnp.float32),
            pltpu.VMEM((3, 32, LANES), jnp.float32),
            pltpu.VMEM((4 * LOW, LANES), jnp.float32),
            pltpu.VMEM((4 * gz_count, 8, LANES), jnp.float32),
            pltpu.VMEM((8, 8, LANES), jnp.float32),
            dma((2,)), dma((2,)), dma, dma((2,)), dma, dma((gz_count,)), dma,
            dma((2, gz_count)), dma((2, gz_count // 2)), dma, dma, dma, dma,
        ],
        compiler_params=pltpu.CompilerParams(
            vmem_limit_bytes=60 * 1024 * 1024, collective_id=2, has_side_effects=True
        ),
    )(jnp.asarray(coarse), jnp.asarray(fine), fields, shells, mubins)


def body(fields, shells, mubins):
    depth_local, _, local_fields, planes, yrows = fields.shape
    gz_count, field_count = lax.axis_size("gz"), lax.axis_size("field")
    devices = gz_count * field_count
    length = depth_local * gz_count
    half = length // 2
    plane_rows = planes * yrows
    width = plane_rows // devices
    me_gz, me_field = lax.axis_index("gz"), lax.axis_index("field")

    if (field_count, gz_count, local_fields, planes, yrows) == (4, 8, 2, 16, 256):
        if depth_local == 256 and (SHELLS, MUBINS) == (256, 8):
            return whole(fields, shells, mubins, gz_count)

    exchange = width == LANES and depth_local % 32 == 0
    if exchange:
        lines = relayout(fields)
    else:
        lines = fields.reshape(depth_local // 2, 2, 2, local_fields, devices, width)
        lines = lines.transpose(4, 1, 0, 2, 3, 5).reshape(
            devices, 2, depth_local // 2, 2 * local_fields * width
        )

    share = planes // field_count
    shells, mubins = (
        lax.dynamic_slice_in_dim(ids, me_field * share, share, 1) for ids in (shells, mubins)
    )
    index = (shells + mubins * 65536).reshape(depth_local, gz_count, width).transpose(1, 0, 2)

    span = 2 * local_fields * LANES
    table = quarter_tables(length, jnp.minimum(me_gz, 0))
    column = (me_field * gz_count + me_gz) * width + jnp.arange(LANES, dtype=jnp.int32)
    waves = jnp.stack([length // 4 + column // yrows, length // 8 + column % yrows])
    waves = jnp.pad(waves.astype(jnp.float32), ((0, 6), (0, 0)))
    landed = (field_count, gz_count, 2, depth_local // 2, span)
    scratch = [
        pltpu.VMEM((field_count, 2, half, span), jnp.float32),
        pltpu.VMEM((4, 32, LANES), jnp.float32),
        pltpu.VMEM((2, length, LANES), jnp.float32),
    ]
    vmem, anywhere = pl.BlockSpec(memory_space=pltpu.VMEM), pl.BlockSpec(memory_space=pl.ANY)
    if exchange:
        run, places, wide = (
            functools.partial(exchange_kernel, length, field_count, gz_count),
            anywhere,
            dict(collective_id=1, has_side_effects=True),
        )
        scratch += [
            pltpu.VMEM(landed, jnp.bfloat16),
            pltpu.VMEM((gz_count, depth_local, LANES), jnp.int32),
            pltpu.SemaphoreType.DMA((2, devices)),
            pltpu.SemaphoreType.DMA((2, devices)),
            pltpu.SemaphoreType.DMA((2,)),
            pltpu.SemaphoreType.DMA((gz_count,)),
            pltpu.SemaphoreType.DMA((gz_count,)),
            pltpu.SemaphoreType.DMA,
        ]
    else:
        run, places, wide = functools.partial(local_kernel, length), vmem, {}
        lines = lax.all_to_all(lines, ("field", "gz"), split_axis=0, concat_axis=0, tiled=True)
        lines = lines.reshape(landed[:-1] + (2 * local_fields, width))
        lines = jnp.pad(lines, ((0, 0),) * 5 + ((0, LANES - width),)).reshape(landed)
        index = lax.all_to_all(index, "gz", split_axis=0, concat_axis=0, tiled=True)
        index = jnp.pad(index, ((0, 0), (0, 0), (0, LANES - width)), constant_values=SHELLS)

    total = pl.pallas_call(
        run,
        out_shape=jax.ShapeDtypeStruct((ROWS * LOW, LANES), jnp.float32),
        in_specs=[vmem, places, places, vmem],
        out_specs=vmem,
        scratch_shapes=scratch,
        compiler_params=pltpu.CompilerParams(vmem_limit_bytes=56 * 1024 * 1024, **wide),
    )(table, lines, index, waves)

    total = total.reshape(ROWS, LOW, LANES)
    total = jnp.concatenate([total[:2], total[2:3] + total[3:4], total[4:]])
    total = all_reduce(total.reshape(-1, LANES), field_count, gz_count)[: 4 * LOW]
    total = total.reshape(4, 2, MUBINS, LANES).transpose(0, 2, 3, 1)
    total = total.reshape(4, MUBINS, SHELLS)
    return total[:3] / jnp.maximum(total[3], 1.0)[None]


def solution(mesh):
    in_specs = (P("gz", None, "field", None, None), P("gz", None, None), P("gz", None, None))
    return jax.shard_map(body, mesh=mesh, in_specs=in_specs, out_specs=P(), check_vma=False)
```

```python
import functools
import math

import jax
import jax.numpy as jnp
import numpy as np
from jax import lax
from jax.experimental import pallas as pl
from jax.experimental.pallas import tpu as pltpu
from jax.sharding import PartitionSpec as P

SHELLS = 256
MUBINS = 8
LANES = 128
LOW = 16
ROWS = 5
PAIRS = 8


def quarter_tables(length, zero):
    quarter, half = length // 4, length // 2
    unit = 2.0 * math.pi / length
    factor = 1.0 / math.sqrt(length)

    def pair(rows, stride):
        shape = (2, rows, half)
        parity = lax.broadcasted_iota(jnp.int32, shape, 0)
        row = lax.broadcasted_iota(jnp.int32, shape, 1) * stride + zero
        depth = 2 * lax.broadcasted_iota(jnp.int32, shape, 2) + parity
        angle = (row * depth % length).astype(jnp.float32) * unit
        return jnp.cos(angle), jnp.sin(angle)

    fine = 16
    ca, sa, cb, sb = lax.optimization_barrier(pair(quarter // fine, fine) + pair(fine, 1))
    ca, sa, cb, sb = ca[:, :, None], sa[:, :, None], cb[:, None], sb[:, None]
    cos_part = ((ca * cb - sa * sb) * factor).reshape(2, quarter, half)
    sin_part = ((sa * cb + ca * sb) * factor).reshape(2, quarter, half)
    row = lax.broadcasted_iota(jnp.int32, sin_part.shape, 1)
    column = lax.broadcasted_iota(jnp.int32, sin_part.shape, 2)
    alternate = (1 - 2 * (column % 2)).astype(jnp.float32) * factor
    sin_part = jnp.where(row == 0, alternate, sin_part)
    return jnp.concatenate(
        [cos_part.astype(jnp.bfloat16), sin_part.astype(jnp.bfloat16)], axis=1
    )


def round16(value):
    return value.astype(jnp.bfloat16).astype(jnp.float32)


def unpack(index_ref, keys):
    depth = index_ref.shape[1]

    def block(g, carry):
        word = index_ref[g]
        mu = word // 65536
        key = (word - mu * 65536) * MUBINS + mu
        upper = key // LOW
        rows = pl.ds(pl.multiple_of(g * depth, depth), depth)
        keys[0, rows, :] = (key - upper * LOW).astype(jnp.float32)
        keys[1, rows, :] = upper.astype(jnp.float32)
        return carry

    lax.fori_loop(0, index_ref.shape[0], block, 0)


def products(table_ref, lines_ref, prod, parity):
    half = table_ref.shape[1]

    def group(f, carry):
        right = lines_ref[f, :, parity].reshape(half, lines_ref.shape[-1])

        def rows_of(i, inner):
            rows = pl.ds(pl.multiple_of(i * 256, 256), 256)
            prod[f, parity, rows, :] = jnp.dot(
                table_ref[parity, rows, :], right, preferred_element_type=jnp.float32
            )
            return inner

        return lax.fori_loop(0, half // 256, rows_of, carry)

    lax.fori_loop(0, prod.shape[0], group, 0)


def local_kernel(length, table_ref, lines_ref, index_ref, wave_ref, out_ref, prod, vals, keys):
    unpack(index_ref, keys)
    products(table_ref, lines_ref, prod, 0)
    products(table_ref, lines_ref, prod, 1)
    bins(length, wave_ref, out_ref, prod, vals, keys)


def exchange_kernel(
    length, field_count, gz_count, table_ref, lines_ref, index_ref, wave_ref, out_ref,
    prod, vals, keys, lines, index, send, recv, own, index_send, index_recv, index_own,
):
    devices = field_count * gz_count
    me_field, me_gz = lax.axis_index("field"), lax.axis_index("gz")
    far = gz_count // 2
    mine = (gz_count - far) * field_count

    def peer(step):
        f = lax.rem(me_field + lax.rem(step, field_count), field_count)
        g = lax.rem(me_gz + step // field_count + far, gz_count)
        return f, g

    def others(run):
        def loop(step, carry):
            run(step)
            return carry

        lax.fori_loop(0, mine, loop, 0)
        lax.fori_loop(mine + 1, devices, loop, 0)

    def along(run):
        def loop(step, carry):
            run(step)
            return carry

        lax.fori_loop(1, gz_count, loop, 0)

    barrier = pltpu.get_barrier_semaphore()
    others(
        lambda step: pl.semaphore_signal(
            barrier, inc=1, device_id=peer(step), device_id_type=pl.DeviceIdType.MESH
        )
    )
    pl.semaphore_wait(barrier, devices - 1)

    def index_copy(step):
        g = lax.rem(me_gz + step, gz_count)
        return pltpu.make_async_remote_copy(
            src_ref=index_ref.at[g],
            dst_ref=index.at[me_gz],
            send_sem=index_send.at[step],
            recv_sem=index_recv.at[step],
            device_id=(me_field, g),
            device_id_type=pl.DeviceIdType.MESH,
        )

    def lines_copy(parity):
        def copy(step):
            f, g = peer(step)
            return pltpu.make_async_remote_copy(
                src_ref=lines_ref.at[f * gz_count + g, parity],
                dst_ref=lines.at[me_field, me_gz, parity],
                send_sem=send.at[parity, step],
                recv_sem=recv.at[parity, step],
                device_id=(f, g),
                device_id_type=pl.DeviceIdType.MESH,
            )

        return copy

    along(lambda step: index_copy(step).start())
    for parity in range(2):
        others(lambda step: lines_copy(parity)(step).start())
    me = me_field * gz_count + me_gz
    kept = [
        pltpu.make_async_copy(
            lines_ref.at[me, parity], lines.at[me_field, me_gz, parity], own.at[parity]
        )
        for parity in range(2)
    ]
    kept_index = pltpu.make_async_copy(index_ref.at[me_gz], index.at[me_gz], index_own)
    for copy in kept + [kept_index]:
        copy.start()

    kept_index.wait()
    along(lambda step: index_copy(step).wait_recv())
    unpack(index, keys)
    for parity in range(2):
        kept[parity].wait()
        others(lambda step: lines_copy(parity)(step).wait_recv())
        products(table_ref, lines, prod, parity)
    bins(length, wave_ref, out_ref, prod, vals, keys)
    along(lambda step: index_copy(step).wait_send())
    for parity in range(2):
        others(lambda step: lines_copy(parity)(step).wait_send())


def bins(length, wave_ref, out_ref, prod, vals, keys):
    quarter, half = length // 4, length // 2
    groups, local = prod.shape[0], prod.shape[3] // (2 * LANES)
    fields = groups * local
    out_ref[...] = jnp.zeros_like(out_ref)
    wave_x = wave_ref[0:1, :]
    wave_y = wave_ref[1:2, :]
    low_iota = lax.broadcasted_iota(jnp.int32, (16, LANES), 0).astype(jnp.float32)
    iotas = [(low_iota + 16.0 * j).astype(jnp.bfloat16) for j in range(LANES // 16)]
    one = jnp.ones((16, LANES), jnp.bfloat16)
    none = jnp.zeros((16, LANES), jnp.bfloat16)

    def cell_row(j, k):
        start = 1 - (k + quarter - 1) // quarter
        return (
            k,
            half - k,
            half + k - quarter * start,
            length - k - quarter * start,
        )[j]

    def tile(t, carry):
        first = pl.multiple_of(t * 8, 8)
        row = lax.broadcasted_iota(jnp.int32, (8, LANES), 0) + first
        special = row == 0

        def load(a, c, parity, sine):
            g, i = a // local, a % local
            at = (c * local + i) * LANES
            return prod[g, parity, pl.ds(sine * quarter + first, 8), at : at + LANES]

        def spectra(a):
            parts = []
            for c in range(2):
                ec, oc = load(a, c, 0, 0), load(a, c, 1, 0)
                es, os = load(a, c, 0, 1), load(a, c, 1, 1)
                p, q, m, n = ec + oc, es + os, ec - oc, os - es
                parts.append(
                    (
                        (p, jnp.where(special, 0.0, q)),
                        (m, jnp.where(special, 0.0, n)),
                        (jnp.where(special, es, m), jnp.where(special, os, -n)),
                        (jnp.where(special, es, p), jnp.where(special, -os, -q)),
                    )
                )
            u, v = parts
            return [(u[j][0] + v[j][1], v[j][0] - u[j][1]) for j in range(4)]

        k = row.astype(jnp.float32)
        zero_wave = (0.0, -half, quarter, -quarter)
        waves = (k, half - k, k - half, -k)
        base = spectra(0)
        second = None
        totals = [None] * 4
        saved = [None] * 4
        pending = [None] * 4
        for a in range(fields):
            spec = base if a == 0 else spectra(a)
            for j in range(4):
                cross = base[j][0] * spec[j][0] + base[j][1] * spec[j][1]
                if a == 0:
                    wz = jnp.where(special, float(zero_wave[j]), waves[j])
                    square = wave_x * wave_x + wave_y * wave_y + wz * wz
                    saved[j] = (wz, 1.0 / square)
                    vals[0, j * 8 : j * 8 + 8] = round16(cross)
                    continue
                wz, inverse = saved[j]
                if a == 1:
                    vals[1, j * 8 : j * 8 + 8] = round16(cross)
                    term = -0.5 * cross
                else:
                    weight = (
                        1.5 * wave_x * wave_x,
                        1.5 * wave_y * wave_y,
                        1.5 * wz * wz,
                        3.0 * wave_x * wave_y,
                        3.0 * wave_x * wz,
                        3.0 * wave_y * wz,
                    )[a - 2]
                    term = weight * inverse * cross
                pending[j] = term if pending[j] is None else pending[j] + term
                if a % local == local - 1:
                    rounded = round16(pending[j])
                    totals[j] = rounded if totals[j] is None else totals[j] + rounded
                    pending[j] = None
        for j in range(4):
            high = round16(totals[j])
            vals[2, j * 8 : j * 8 + 8] = high
            vals[3, j * 8 : j * 8 + 8] = totals[j] - high
        total = out_ref[...]
        for start in range(0, 32, PAIRS):
            left, hot = [], []
            for r in range(start, start + PAIRS):
                cell = cell_row(r // 8, first + r % 8)
                spread = [
                    jnp.broadcast_to(part, (16, LANES)).astype(jnp.bfloat16)
                    for part in [vals[i, r : r + 1] for i in range(4)]
                    + [keys[i, pl.ds(cell, 1), :] for i in range(2)]
                ]
                match = spread[4] == iotas[0]
                left.append(
                    jnp.concatenate(
                        [jnp.where(match, spread[i], none) for i in range(4)]
                        + [jnp.where(match, one, none)],
                        axis=0,
                    )
                )
                hot.append(
                    jnp.concatenate(
                        [jnp.where(spread[5] == it, one, none) for it in iotas], axis=0
                    )
                )
            total = total + lax.dot_general(
                jnp.concatenate(left, axis=1),
                jnp.concatenate(hot, axis=1),
                (((1,), (1,)), ((), ())),
                preferred_element_type=jnp.float32,
            )
        out_ref[...] = total
        return carry

    lax.fori_loop(0, quarter // 8, tile, 0)


def relayout_kernel(fields_ref, out_ref):
    for c in range(2):
        for i in range(fields_ref.shape[2]):
            at = (c * fields_ref.shape[2] + i) * LANES
            for h in range(out_ref.shape[1]):
                block = fields_ref[:, c, i, :, h * LANES : (h + 1) * LANES]
                block = block.reshape(16, 2, block.shape[1], LANES)
                for parity in range(2):
                    out_ref[:, h, parity, :, at : at + LANES] = jnp.swapaxes(
                        block[:, parity], 0, 1
                    )


def relayout(fields):
    depth, _, local, planes, yrows = fields.shape
    parts = yrows // LANES
    out = pl.pallas_call(
        relayout_kernel,
        grid=(depth // 32,),
        out_shape=jax.ShapeDtypeStruct(
            (planes, parts, 2, depth // 2, 2 * local * LANES), fields.dtype
        ),
        in_specs=[pl.BlockSpec((32, 2, local, planes, yrows), lambda i: (i, 0, 0, 0, 0))],
        out_specs=pl.BlockSpec(
            (planes, parts, 2, 16, 2 * local * LANES), lambda i: (0, 0, 0, i, 0)
        ),
    )(fields)
    return out.reshape(planes * parts, 2, depth // 2, 2 * local * LANES)


def reduce_kernel(field_count, gz_count, mine_ref, out_ref, parts, answer, send, recv, send2, recv2):
    devices = field_count * gz_count
    me_field, me_gz = lax.axis_index("field"), lax.axis_index("gz")
    me = me_field * gz_count + me_gz

    def peer(step):
        other = lax.rem(me + step, devices)
        return other, (other // gz_count, lax.rem(other, gz_count))

    barrier = pltpu.get_barrier_semaphore()

    def greet(step, carry):
        _, place = peer(step)
        pl.semaphore_signal(
            barrier, inc=1, device_id=place, device_id_type=pl.DeviceIdType.MESH
        )
        return carry

    lax.fori_loop(1, devices, greet, 0)
    pl.semaphore_wait(barrier, devices - 1)

    def scatter(step):
        other, place = peer(step)
        return pltpu.make_async_remote_copy(
            src_ref=mine_ref.at[other],
            dst_ref=parts.at[step],
            send_sem=send.at[step],
            recv_sem=recv.at[step],
            device_id=place,
            device_id_type=pl.DeviceIdType.MESH,
        )

    def gather(step):
        _, place = peer(step)
        return pltpu.make_async_remote_copy(
            src_ref=answer,
            dst_ref=out_ref.at[me],
            send_sem=send2.at[step],
            recv_sem=recv2.at[step],
            device_id=place,
            device_id_type=pl.DeviceIdType.MESH,
        )

    def start(copy):
        def run(step, carry):
            copy(step).start()
            return carry

        lax.fori_loop(1, devices, run, 0)

    start(scatter)

    def collect(step, total):
        scatter(step).wait_recv()
        return total + parts[step]

    answer[...] = lax.fori_loop(1, devices, collect, mine_ref[me])
    start(gather)
    out_ref[me] = answer[...]

    def finish(step, carry):
        scatter(step).wait_send()
        gather(step).wait()
        return carry

    lax.fori_loop(1, devices, finish, 0)


def all_reduce(total, field_count, gz_count):
    devices = field_count * gz_count
    rows = max(1, total.shape[0] // devices)
    total = jnp.pad(total, ((0, devices * rows - total.shape[0]), (0, 0)))
    total = total.reshape(devices, rows, LANES)
    return pl.pallas_call(
        functools.partial(reduce_kernel, field_count, gz_count),
        out_shape=jax.ShapeDtypeStruct(total.shape, jnp.float32),
        in_specs=[pl.BlockSpec(memory_space=pltpu.VMEM)],
        out_specs=pl.BlockSpec(memory_space=pltpu.VMEM),
        scratch_shapes=[
            pltpu.VMEM(total.shape, jnp.float32),
            pltpu.VMEM(total.shape[1:], jnp.float32),
            pltpu.SemaphoreType.DMA((devices,)),
            pltpu.SemaphoreType.DMA((devices,)),
            pltpu.SemaphoreType.DMA((devices,)),
            pltpu.SemaphoreType.DMA((devices,)),
        ],
        compiler_params=pltpu.CompilerParams(collective_id=0, has_side_effects=True),
    )(total).reshape(devices * rows, LANES)


SLOTS = 6
KEPT = 5


def wave_tables(length):
    quarter, half = length // 4, length // 2
    unit = 2.0 * math.pi / length

    def pair(rows, stride):
        row = np.arange(rows)[None, :, None] * stride
        depth = 2 * np.arange(half)[None, None, :] + np.arange(2)[:, None, None]
        angle = (row * depth % length).astype(np.float32) * np.float32(unit)
        return np.cos(angle), np.sin(angle)

    ca, sa = pair(quarter // 16, 16)
    cb, sb = pair(16, 1)
    return np.stack([ca, sa]), np.stack([cb, sb])


def build_table(length, coarse_ref, fine_ref, table):
    quarter, half = length // 4, length // 2
    factor = 1.0 / math.sqrt(length)
    parts = table.shape[0]
    wide = half // parts

    def rows_of(a, carry):
        rows = pl.ds(pl.multiple_of(a * 16, 16), 16)
        under = pl.ds(pl.multiple_of(quarter + a * 16, 16), 16)
        for parity in range(2):
            for q in range(parts):
                at = slice(q * wide, (q + 1) * wide)
                ca, sa = (coarse_ref[i, parity, pl.ds(a, 1), at] for i in range(2))
                cb, sb = (fine_ref[i, parity, :, at] for i in range(2))
                cos_part = (ca * cb - sa * sb) * factor
                sin_part = (sa * cb + ca * sb) * factor
                row = lax.broadcasted_iota(jnp.int32, sin_part.shape, 0) + a
                column = lax.broadcasted_iota(jnp.int32, sin_part.shape, 1)
                alternate = (1 - 2 * (column % 2)).astype(jnp.float32) * factor
                sin_part = jnp.where(row == 0, alternate, sin_part)
                table[q, parity, rows, :] = cos_part.astype(jnp.bfloat16)
                table[q, parity, under, :] = sin_part.astype(jnp.bfloat16)
        return carry

    lax.fori_loop(0, quarter // 16, rows_of, 0)


def split_keys(index, keys):
    depth = index.shape[1]

    def block(g, carry):
        word = index[g]
        mu = lax.shift_right_logical(word, 16)
        shell = word & 65535
        rows = pl.ds(pl.multiple_of(g * depth, depth), depth)
        keys[0, rows, :] = (mu + MUBINS * lax.shift_right_logical(shell, 7)).astype(jnp.float32)
        keys[1, rows, :] = (shell & (LANES - 1)).astype(jnp.float32)
        return carry

    lax.fori_loop(0, index.shape[0], block, 0)


def arrange(length, me_field, stage, spread, chunk):
    planes = stage.shape[3]
    rows = pl.ds(pl.multiple_of(chunk * 16, 16), 16)

    def put(block, h, i, c):
        block = block.reshape(16, 2, planes, LANES)
        for parity in range(2):
            spread[:, h, i, parity, rows, c * LANES : (c + 1) * LANES] = jnp.swapaxes(
                block[:, parity], 0, 1
            )

    def take(c, i, h):
        return stage[:, c, i, :, h * LANES : (h + 1) * LANES]

    @pl.when(me_field % 2 == 0)
    def _():
        for c in range(2):
            for i in range(2):
                for h in range(2):
                    put(take(c, i, h), h, i, c)

    @pl.when(me_field % 2 == 1)
    def _():
        wave_x = lax.broadcasted_iota(jnp.int32, (planes, LANES), 0).astype(jnp.float32)
        wave_x = wave_x + float(length // 4)
        squared = me_field == 1
        for h in range(2):
            wave_y = lax.broadcasted_iota(jnp.int32, (planes, LANES), 1).astype(jnp.float32)
            wave_y = wave_y + float(length // 8 + h * LANES)
            first = jnp.where(squared, 1.5 * wave_x * wave_x, wave_x)[None]
            other = jnp.where(squared, 1.5 * wave_y * wave_y, wave_y)[None]
            for c in range(2):
                value = first * take(c, 0, h).astype(jnp.float32)
                value = value + other * take(c, 1, h).astype(jnp.float32)
                put(value.astype(jnp.bfloat16), h, 0, c)


def transform(table, land, prod, fields, start, sources, sums):
    wide = prod.shape[3]
    quads = [sums[4 * n : 4 * n + 4] for n in range(4)]

    def group(a, carry):
        for parity in range(2):
            for n, (plane, local) in enumerate(sources):
                right = land[local, a, parity].reshape(-1, wide)
                for mxu in range(2):
                    pltpu.matmul_push_rhs(right, n % 2, mxu)
                    for i in range(4):
                        at = (4 * mxu + i) * LANES
                        pltpu.matmul_acc_lhs(
                            quads[2 * mxu + parity][i],
                            table[plane, parity, at : at + LANES, :],
                            n % 2 if i == 0 else None,
                        )
            for mxu in range(2):
                for i in range(4):
                    at = (4 * mxu + i) * LANES
                    prod[start + a, parity, at : at + LANES, :] = pltpu.matmul_pop(
                        quads[2 * mxu + parity][i]
                    )
        return carry

    lax.fori_loop(0, fields, group, 0)


def histogram(length, plane, prod, vals, keys, acc, low, high, sums):
    quarter, half = length // 4, length // 2
    groups, mxus = 4, 2
    lane = lax.broadcasted_iota(jnp.int32, (8, LANES), 1).astype(jnp.float32)
    wave_x = (length // 4 + plane // 2).astype(jnp.float32)
    wave_y = (length // 8 + (plane % 2) * LANES).astype(jnp.float32) + lane
    flat = wave_x * wave_x + wave_y * wave_y
    low_iota = lax.broadcasted_iota(jnp.int32, (16, LANES), 0).astype(jnp.float32)
    iotas = [(low_iota + 16.0 * j).astype(jnp.bfloat16) for j in range(LANES // 16)]
    one = jnp.ones((16, LANES), jnp.bfloat16)
    none = jnp.zeros((16, LANES), jnp.bfloat16)

    def cell_row(j, k):
        start = 1 - (k + quarter - 1) // quarter
        return (
            k,
            half - k,
            half + k - quarter * start,
            length - k - quarter * start,
        )[j]

    def values(t, edge):
        first = t * 8 if edge else pl.multiple_of(t * 8, 8)
        row = lax.broadcasted_iota(jnp.int32, (8, LANES), 0) + first
        special = row == 0

        def load(a, c, parity, sine):
            at = pl.ds(sine * quarter + first, 8)
            return prod[a, parity, at, c * LANES : (c + 1) * LANES]

        def spectra(a):
            parts = []
            for c in range(2):
                ec, oc = load(a, c, 0, 0), load(a, c, 1, 0)
                es, os = load(a, c, 0, 1), load(a, c, 1, 1)
                p, q, m, n = ec + oc, es + os, ec - oc, os - es
                if edge:
                    parts.append(
                        (
                            (p, jnp.where(special, 0.0, q)),
                            (m, jnp.where(special, 0.0, n)),
                            (jnp.where(special, es, m), jnp.where(special, os, -n)),
                            (jnp.where(special, es, p), jnp.where(special, -os, -q)),
                        )
                    )
                else:
                    parts.append(((p, q), (m, n), (m, n), (p, q)))
            u, v = parts
            result = []
            for j in range(4):
                if edge or j < 2:
                    result.append((u[j][0] + v[j][1], v[j][0] - u[j][1]))
                else:
                    result.append((u[j][0] - v[j][1], v[j][0] + u[j][1]))
            return result

        k = row.astype(jnp.float32)
        zero_wave = (0.0, -half, quarter, -quarter)
        waves = [k, half - k, k - half, -k]
        if edge:
            waves = [jnp.where(special, float(z), w) for z, w in zip(zero_wave, waves)]
            inverse = [1.0 / (flat + w * w) for w in waves]
        else:
            inverse = [1.0 / (flat + w * w) for w in waves[:2]]
            inverse = [inverse[0], inverse[1], inverse[1], inverse[0]]
        base, first_cross, cross_b, cubic, mixed = (spectra(a) for a in range(KEPT))
        for j in range(4):
            re, im = base[j]
            auto = re * re + im * im
            pair = re * first_cross[j][0] + im * first_cross[j][1]
            w = waves[j]
            three, half_more = 3.0 * w, 1.5 * (w * w)
            qre = mixed[j][0] + three * cross_b[j][0] + half_more * cubic[j][0]
            qim = mixed[j][1] + three * cross_b[j][1] + half_more * cubic[j][1]
            quad = inverse[j] * (re * qre + im * qim) - 0.5 * pair
            vals[0, j * 8 : j * 8 + 8] = auto
            vals[1, j * 8 : j * 8 + 8] = pair
            vals[2, j * 8 : j * 8 + 8] = quad

    def one_hots(r, cell):
        spread = [
            jnp.broadcast_to(part, (16, LANES)).astype(jnp.bfloat16)
            for part in [vals[i, r : r + 1] for i in range(3)]
            + [keys[i, pl.ds(cell, 1), :] for i in range(2)]
        ]
        match = spread[3] == iotas[0]
        left = [jnp.where(match, spread[i], none) for i in range(3)]
        left = jnp.concatenate(left + [jnp.where(match, one, none)], axis=0)
        hot = [jnp.where(spread[4] == it, one, none) for it in iotas]
        return left, jnp.concatenate(hot, axis=0)

    def tile(t, edge):
        values(t, edge)
        first = t * 8
        for unit in range(4):
            mxu, stage = unit % mxus, unit // mxus
            lefts, hots = [], []
            for g in range(groups):
                pair = []
                for r in range(unit * 8 + g * 2, unit * 8 + g * 2 + 2):
                    pair.append(one_hots(r, cell_row(r // 8, first + r % 8)))
                lefts.append(jnp.concatenate([x[0] for x in pair], axis=1))
                hots.append(jnp.concatenate([x[1] for x in pair], axis=1))
            pltpu.matmul_push_rhs(jnp.concatenate(lefts, axis=0), stage, mxu, transpose=True)
            for g in range(groups):
                pltpu.matmul_acc_lhs(sums[8 * mxu + g], hots[g], stage if g == 0 else None)

    @pl.when(low == 0)
    def _():
        tile(0, True)

    def step(t, carry):
        tile(t, False)
        return carry

    lax.fori_loop(jnp.maximum(low, 1), high, step, 0)
    total = None
    for g in range(groups):
        block = pltpu.matmul_pop(sums[g]) + pltpu.matmul_pop(sums[8 + g])
        block = block[:, g // 2 * LANES : (g // 2 + 1) * LANES]
        block = jnp.transpose(block)[g % 2 * 64 : g % 2 * 64 + 64]
        total = block if total is None else total + block
    acc[...] += total


def whole_kernel(
    length, coarse_ref, fine_ref, fields_ref, shells_ref, mubins_ref, out_ref,
    stage, spread, mix, joined, first, land, prod, table, raw, index_out, index, keys, vals, acc,
    parts, answer,
    stage_sem, raw_sem, index_sent, index_come, mix_sent, mix_come, land_sent, first_come,
    land_come, part_sent, part_come, answer_sent, answer_come,
):
    fields, cores, chunks = 4, 2, 2
    planes_z = table.shape[0]
    gz_count = planes_z * cores
    owners = gz_count // chunks
    devices = fields * gz_count
    me_field, me_gz = lax.axis_index("field"), lax.axis_index("gz")
    me = me_field * gz_count + me_gz
    me_plane, me_core = me_gz // cores, me_gz % cores
    me_half, me_owner = me_gz // owners, me_gz % owners
    steps = fields_ref.shape[0] // 32
    MESH = pl.DeviceIdType.MESH

    def loop(low, high, run):
        def step(i, carry):
            run(i)
            return carry

        lax.fori_loop(low, high, step, 0)

    def wait(ref, sem):
        pltpu.make_async_copy(ref, ref, sem).wait()

    barrier = pltpu.get_barrier_semaphore()

    def greet(step):
        other = lax.rem(me + step, devices)
        pl.semaphore_signal(
            barrier, inc=1, device_id=(other // gz_count, lax.rem(other, gz_count)),
            device_id_type=MESH,
        )

    loop(1, devices, greet)

    def raw_copy(b):
        lanes = pl.ds(pl.multiple_of((b % 2) * LANES, LANES), LANES)
        at = (slice(None), me_field * (gz_count // 2) + b // 2, lanes)
        return [
            pltpu.make_async_copy(ref.at[at], raw.at[i, b], raw_sem.at[i])
            for i, ref in enumerate((shells_ref, mubins_ref))
        ]

    def fetch(n):
        return pltpu.make_async_copy(
            fields_ref.at[pl.ds(n * 32, 32)], stage.at[n % 2], stage_sem.at[n % 2]
        )

    loop(0, gz_count, lambda b: [copy.start() for copy in raw_copy(b)])
    for n in range(2):
        fetch(n).start()
    for i in range(2):
        wait(raw.at[i], raw_sem.at[i])

    def join(n):
        index_out[n] = raw[0, n] + raw[1, n] * 65536

    loop(0, gz_count, join)
    pl.semaphore_wait(barrier, devices - 1)

    def owner_of(i):
        plane = lax.rem(me_plane + 1 + (i % owners) // 2, 2)
        return plane * cores + lax.rem(me_core + i, cores)

    def forward(source, goal, sent, come, g):
        pltpu.make_async_remote_copy(
            src_ref=source, dst_ref=goal, send_sem=sent, recv_sem=come,
            device_id=(me_field, g), device_id_type=MESH,
        ).start()

    def index_send(i):
        chunk, owner = i // owners, owner_of(i)
        b = chunk * owners + owner
        goal = index.at[chunk, me_gz]
        forward(
            index_out.at[b], goal, index_sent, index_come.at[chunk],
            (1 - me_half) * owners + owner,
        )

        @pl.when(owner != me_owner)
        def _():
            forward(
                index_out.at[b], goal, index_sent, index_come.at[chunk],
                me_half * owners + owner,
            )

        @pl.when(owner == me_owner)
        def _():
            pltpu.make_async_copy(index_out.at[b], goal, index_come.at[chunk]).start()

    loop(0, gz_count, index_send)

    def place(n):
        fetch(n).wait()
        arrange(length, me_field, stage.at[n % 2], spread, n)

        @pl.when(n + 2 < steps)
        def _():
            fetch(n + 2).start()

    loop(0, steps, place)

    even = 1 - me_field % 2
    slot = even * (3 * me_field // 2) + (1 - even) * ((13 - 3 * me_field) // 2)

    def mix_send(i):
        b = (i // owners) * owners + owner_of(i)

        def piece(f, s):
            return spread.at[f * (gz_count // 2) + b // 2, b % 2, s]

        def send(f, s):
            pltpu.make_async_remote_copy(
                src_ref=piece(f, s), dst_ref=mix.at[b, slot + s],
                send_sem=mix_sent, recv_sem=mix_come.at[b],
                device_id=(f, me_gz), device_id_type=MESH,
            ).start()

        def keep(s):
            pltpu.make_async_copy(
                piece(me_field, s), mix.at[b, slot + s], mix_come.at[b]
            ).start()

        others = [lax.rem(me_field + 2, 4), me_field + 1 - 2 * (me_field % 2), 3 - me_field]
        for f in others:
            send(f, 0)
        keep(0)

        @pl.when(even == 1)
        def _():
            for f in others:
                send(f, 1)
            keep(1)

    loop(0, gz_count, mix_send)
    build_table(length, coarse_ref, fine_ref, table)
    acc[...] = jnp.zeros_like(acc)

    def join_send(i):
        chunk, owner = i // owners, owner_of(i)
        b = chunk * owners + owner
        wait(mix.at[b], mix_come.at[b])
        wave_x = (length // 4 + me_field * (gz_count // 2) + b // 2).astype(jnp.float32)
        lane = lax.broadcasted_iota(jnp.int32, (1, 2 * LANES), 1) % LANES
        wave_y = (length // 8 + (b % 2) * LANES + lane).astype(jnp.float32)
        weight = 3.0 * wave_x * wave_y
        for parity in range(2):
            value = mix[b, 5, parity].astype(jnp.float32)
            value = value + weight * mix[b, 4, parity].astype(jnp.float32)
            joined[b, parity] = value.astype(jnp.bfloat16)
        base = (mix.at[b, 0], first.at[chunk, me_plane, 0, :, me_core])
        me_near = me_plane % 2
        pairs = (
            (mix.at[b, pl.ds(1, 3)], land.at[chunk, me_near, pl.ds(0, 3), :, me_core]),
            (joined.at[b], land.at[chunk, me_near, 3, :, me_core]),
        )
        forward(*base, land_sent, first_come.at[chunk, me_gz], (1 - me_half) * owners + owner)

        @pl.when(owner != me_owner)
        def _():
            g = me_half * owners + owner
            forward(*base, land_sent, first_come.at[chunk, me_gz], g)
            for source, goal in pairs:
                forward(source, goal, land_sent, land_come.at[chunk, me_owner], g)

        @pl.when(owner == me_owner)
        def _():
            pltpu.make_async_copy(*base, first_come.at[chunk, me_gz]).start()
            for source, goal in pairs:
                pltpu.make_async_copy(source, goal, land_come.at[chunk, me_owner]).start()

    def transform_lines(chunk, sums):
        near = 1 - 2 * (me_plane % 2)
        sources = [(me_plane + hop, lax.rem(me_plane + hop, 2)) for hop in (0, near)]
        for _, local in sources:
            for core in range(cores):
                wait(land.at[chunk, local, :, :, core], land_come.at[chunk, local * cores + core])
        transform(table, land.at[chunk], prod, KEPT - 1, 1, sources, sums)
        sources = [(n, n) for n in range(planes_z)]
        for plane, _ in sources:
            for core in range(cores):
                block = first.at[chunk, plane, :, :, core]
                wait(block, first_come.at[chunk, plane * cores + core])
        transform(table, first.at[chunk], prod, 1, 0, sources, sums)

    tiles = length // 32
    span = tiles // owners

    def bin_lines(chunk, n, count, sums):
        b = me_field * gz_count + chunk * owners + me_owner
        low, high = n * span, (n + count) * span
        histogram(length, b, prod, vals, keys.at[chunk], acc, low, high, sums)

    loop(0, owners, join_send)
    for chunk in range(chunks):
        wait(index.at[chunk], index_come.at[chunk])
        split_keys(index.at[chunk], keys.at[chunk])
    join_send(owners)

    def crunch(*sums):
        for ref in sums:
            pltpu.matmul_pop(ref)
        transform_lines(0, sums)

        def mixed_step(n):
            bin_lines(0, n, 1, sums)

            @pl.when(n < owners - 1)
            def _():
                join_send(owners + 1 + n)

        loop(0, owners, mixed_step)
        transform_lines(1, sums)
        bin_lines(1, 0, owners, sums)

    pl.run_scoped(
        crunch,
        *(
            pltpu.ACC(mxu)((LANES, 2 * LANES), jnp.float32)
            for mxu in range(2)
            for _ in range(8)
        ),
    )

    ranks = acc.shape[0] // 8
    middle = (planes_z // 2 - 1) * cores
    rank = me_field + fields * lax.div(me_gz - middle, cores)
    root = (me_gz == middle) | (me_gz == middle + cores)

    def part_copy(r):
        return pltpu.make_async_remote_copy(
            src_ref=acc.at[pl.ds(pl.multiple_of(r * 8, 8), 8)], dst_ref=parts.at[me],
            send_sem=part_sent, recv_sem=part_come,
            device_id=(lax.rem(r, fields), middle + cores * (r // fields)),
            device_id_type=MESH,
        )

    def part_send(n):
        r = lax.rem(me_field + n, ranks)

        @pl.when((r != rank) | jnp.logical_not(root))
        def _():
            part_copy(r).start()

    loop(0, ranks, part_send)

    def answer_copy(step):
        other = lax.rem(me + step, devices)
        return pltpu.make_async_remote_copy(
            src_ref=answer.at[rank], dst_ref=answer.at[rank],
            send_sem=answer_sent, recv_sem=answer_come,
            device_id=(other // gz_count, lax.rem(other, gz_count)), device_id_type=MESH,
        )

    @pl.when(root)
    def _():
        parts[me] = acc[pl.ds(pl.multiple_of(rank * 8, 8), 8), :]
        rest = parts.at[pl.ds(0, devices - 1)]
        wait(rest, part_come)
        answer[rank] = lax.fori_loop(
            1, devices, lambda d, total: total + parts[d], parts[0]
        )
        loop(1, devices, lambda step: answer_copy(step).start())
        got = answer.at[pl.ds(0, ranks - 1)]
        wait(got, answer_come)
        wait(rest, answer_sent)
        wait(got, part_sent)

    @pl.when(jnp.logical_not(root))
    def _():
        wait(answer, answer_come)
        wait(answer, part_sent)

    for hi in range(2):
        scale = 1.0 / jnp.maximum(0.5 * answer[6 + hi], 1.0)
        for m in range(3):
            half_scale = 0.5 * scale if m == 0 else scale
            out_ref[m, :, hi * LANES : (hi + 1) * LANES] = answer[2 * m + hi] * half_scale

    for _ in range(2):
        sent = index_out.at[pl.ds(0, gz_count - 1)]
        wait(sent, index_sent)
    wait(mix.at[:, 0], land_sent)
    wait(mix.at[pl.ds(0, 2 * (owners - 1)), pl.ds(0, KEPT)], land_sent)

    @pl.when(even == 1)
    def _():
        wait(spread.at[pl.ds(0, 12)], mix_sent)

    @pl.when(even == 0)
    def _():
        wait(spread.at[pl.ds(0, 12), :, 0], mix_sent)


def whole(fields, shells, mubins, gz_count):
    depth, _, local, planes, yrows = fields.shape
    length = depth * gz_count
    half = length // 2
    coarse, fine = wave_tables(length)
    vmem, anywhere = pl.BlockSpec(memory_space=pltpu.VMEM), pl.BlockSpec(memory_space=pl.ANY)
    wide = 2 * LANES
    dma = pltpu.SemaphoreType.DMA
    low = jnp.bfloat16
    line_block = (2, depth // 2, wide)
    pair_block = (2, 2, depth // 2, wide)
    return pl.pallas_call(
        functools.partial(whole_kernel, length),
        out_shape=jax.ShapeDtypeStruct((3, MUBINS, SHELLS), jnp.float32),
        in_specs=[vmem, vmem, anywhere, anywhere, anywhere],
        out_specs=vmem,
        scratch_shapes=[
            pltpu.VMEM((2, 32) + fields.shape[1:], low),
            pltpu.VMEM((planes, 2, local) + line_block, low),
            pltpu.VMEM((gz_count, SLOTS) + line_block, low),
            pltpu.VMEM((gz_count,) + line_block, low),
            pltpu.VMEM((2, gz_count // 2, 1) + pair_block, low),
            pltpu.VMEM((2, gz_count // 4, KEPT - 1) + pair_block, low),
            pltpu.VMEM((KEPT, 2, half, wide), jnp.float32),
            pltpu.VMEM((gz_count // 2, 2, half, depth), low),
            pltpu.VMEM((2, gz_count, depth, LANES), jnp.int32),
            pltpu.VMEM((gz_count, depth, LANES), jnp.int32),
            pltpu.VMEM((2, gz_count, depth, LANES), jnp.int32),
            pltpu.VMEM((2, 2, length, LANES), jnp.float32),
            pltpu.VMEM((3, 32, LANES), jnp.float32),
            pltpu.VMEM((4 * LOW, LANES), jnp.float32),
            pltpu.VMEM((4 * gz_count, 8, LANES), jnp.float32),
            pltpu.VMEM((8, 8, LANES), jnp.float32),
            dma((2,)), dma((2,)), dma, dma((2,)), dma, dma((gz_count,)), dma,
            dma((2, gz_count)), dma((2, gz_count // 2)), dma, dma, dma, dma,
        ],
        compiler_params=pltpu.CompilerParams(
            vmem_limit_bytes=60 * 1024 * 1024, collective_id=2, has_side_effects=True
        ),
    )(jnp.asarray(coarse), jnp.asarray(fine), fields, shells, mubins)


def body(fields, shells, mubins):
    depth_local, _, local_fields, planes, yrows = fields.shape
    gz_count, field_count = lax.axis_size("gz"), lax.axis_size("field")
    devices = gz_count * field_count
    length = depth_local * gz_count
    half = length // 2
    plane_rows = planes * yrows
    width = plane_rows // devices
    me_gz, me_field = lax.axis_index("gz"), lax.axis_index("field")

    paired = yrows == 2 * LANES and 2 * planes == devices and local_fields == 2
    if paired and depth_local == 2 * LANES and gz_count == 2 * field_count == MUBINS:
        return whole(fields, shells, mubins, gz_count)

    exchange = width == LANES and depth_local % 32 == 0
    if exchange:
        lines = relayout(fields)
    else:
        lines = fields.reshape(depth_local // 2, 2, 2, local_fields, devices, width)
        lines = lines.transpose(4, 1, 0, 2, 3, 5).reshape(
            devices, 2, depth_local // 2, 2 * local_fields * width
        )

    share = planes // field_count
    shells, mubins = (
        lax.dynamic_slice_in_dim(ids, me_field * share, share, 1) for ids in (shells, mubins)
    )
    index = (shells + mubins * 65536).reshape(depth_local, gz_count, width).transpose(1, 0, 2)

    span = 2 * local_fields * LANES
    table = quarter_tables(length, jnp.minimum(me_gz, 0))
    column = (me_field * gz_count + me_gz) * width + jnp.arange(LANES, dtype=jnp.int32)
    waves = jnp.stack([length // 4 + column // yrows, length // 8 + column % yrows])
    waves = jnp.pad(waves.astype(jnp.float32), ((0, 6), (0, 0)))
    landed = (field_count, gz_count, 2, depth_local // 2, span)
    scratch = [
        pltpu.VMEM((field_count, 2, half, span), jnp.float32),
        pltpu.VMEM((4, 32, LANES), jnp.float32),
        pltpu.VMEM((2, length, LANES), jnp.float32),
    ]
    vmem, anywhere = pl.BlockSpec(memory_space=pltpu.VMEM), pl.BlockSpec(memory_space=pl.ANY)
    if exchange:
        run, places, wide = (
            functools.partial(exchange_kernel, length, field_count, gz_count),
            anywhere,
            dict(collective_id=1, has_side_effects=True),
        )
        scratch += [
            pltpu.VMEM(landed, jnp.bfloat16),
            pltpu.VMEM((gz_count, depth_local, LANES), jnp.int32),
            pltpu.SemaphoreType.DMA((2, devices)),
            pltpu.SemaphoreType.DMA((2, devices)),
            pltpu.SemaphoreType.DMA((2,)),
            pltpu.SemaphoreType.DMA((gz_count,)),
            pltpu.SemaphoreType.DMA((gz_count,)),
            pltpu.SemaphoreType.DMA,
        ]
    else:
        run, places, wide = functools.partial(local_kernel, length), vmem, {}
        lines = lax.all_to_all(lines, ("field", "gz"), split_axis=0, concat_axis=0, tiled=True)
        lines = lines.reshape(landed[:-1] + (2 * local_fields, width))
        lines = jnp.pad(lines, ((0, 0),) * 5 + ((0, LANES - width),)).reshape(landed)
        index = lax.all_to_all(index, "gz", split_axis=0, concat_axis=0, tiled=True)
        index = jnp.pad(index, ((0, 0), (0, 0), (0, LANES - width)), constant_values=SHELLS)

    total = pl.pallas_call(
        run,
        out_shape=jax.ShapeDtypeStruct((ROWS * LOW, LANES), jnp.float32),
        in_specs=[vmem, places, places, vmem],
        out_specs=vmem,
        scratch_shapes=scratch,
        compiler_params=pltpu.CompilerParams(vmem_limit_bytes=56 * 1024 * 1024, **wide),
    )(table, lines, index, waves)

    total = total.reshape(ROWS, LOW, LANES)
    total = jnp.concatenate([total[:2], total[2:3] + total[3:4], total[4:]])
    total = all_reduce(total.reshape(-1, LANES), field_count, gz_count)[: 4 * LOW]
    total = total.reshape(4, 2, MUBINS, LANES).transpose(0, 2, 3, 1)
    total = total.reshape(4, MUBINS, SHELLS)
    return total[:3] / jnp.maximum(total[3], 1.0)[None]


def solution(mesh):
    in_specs = (P("gz", None, "field", None, None), P("gz", None, None), P("gz", None, None))
    return jax.shard_map(body, mesh=mesh, in_specs=in_specs, out_specs=P(), check_vma=False)
```

```python
import functools
import math

import jax
import jax.numpy as jnp
import numpy as np
from jax import lax
from jax.experimental import pallas as pl
from jax.experimental.pallas import tpu as pltpu
from jax.sharding import PartitionSpec as P

SHELLS = 256
MUBINS = 8
LANES = 128
LOW = 16
ROWS = 5
PAIRS = 8


def quarter_tables(length, zero):
    quarter, half = length // 4, length // 2
    unit = 2.0 * math.pi / length
    factor = 1.0 / math.sqrt(length)

    def pair(rows, stride):
        shape = (2, rows, half)
        parity = lax.broadcasted_iota(jnp.int32, shape, 0)
        row = lax.broadcasted_iota(jnp.int32, shape, 1) * stride + zero
        depth = 2 * lax.broadcasted_iota(jnp.int32, shape, 2) + parity
        angle = (row * depth % length).astype(jnp.float32) * unit
        return jnp.cos(angle), jnp.sin(angle)

    fine = 16
    ca, sa, cb, sb = lax.optimization_barrier(pair(quarter // fine, fine) + pair(fine, 1))
    ca, sa, cb, sb = ca[:, :, None], sa[:, :, None], cb[:, None], sb[:, None]
    cos_part = ((ca * cb - sa * sb) * factor).reshape(2, quarter, half)
    sin_part = ((sa * cb + ca * sb) * factor).reshape(2, quarter, half)
    row = lax.broadcasted_iota(jnp.int32, sin_part.shape, 1)
    column = lax.broadcasted_iota(jnp.int32, sin_part.shape, 2)
    alternate = (1 - 2 * (column % 2)).astype(jnp.float32) * factor
    sin_part = jnp.where(row == 0, alternate, sin_part)
    return jnp.concatenate(
        [cos_part.astype(jnp.bfloat16), sin_part.astype(jnp.bfloat16)], axis=1
    )


def round16(value):
    return value.astype(jnp.bfloat16).astype(jnp.float32)


def unpack(index_ref, keys):
    depth = index_ref.shape[1]

    def block(g, carry):
        word = index_ref[g]
        mu = word // 65536
        key = (word - mu * 65536) * MUBINS + mu
        upper = key // LOW
        rows = pl.ds(pl.multiple_of(g * depth, depth), depth)
        keys[0, rows, :] = (key - upper * LOW).astype(jnp.float32)
        keys[1, rows, :] = upper.astype(jnp.float32)
        return carry

    lax.fori_loop(0, index_ref.shape[0], block, 0)


def products(table_ref, lines_ref, prod, parity):
    half = table_ref.shape[1]

    def group(f, carry):
        right = lines_ref[f, :, parity].reshape(half, lines_ref.shape[-1])

        def rows_of(i, inner):
            rows = pl.ds(pl.multiple_of(i * 256, 256), 256)
            prod[f, parity, rows, :] = jnp.dot(
                table_ref[parity, rows, :], right, preferred_element_type=jnp.float32
            )
            return inner

        return lax.fori_loop(0, half // 256, rows_of, carry)

    lax.fori_loop(0, prod.shape[0], group, 0)


def local_kernel(length, table_ref, lines_ref, index_ref, wave_ref, out_ref, prod, vals, keys):
    unpack(index_ref, keys)
    products(table_ref, lines_ref, prod, 0)
    products(table_ref, lines_ref, prod, 1)
    bins(length, wave_ref, out_ref, prod, vals, keys)


def exchange_kernel(
    length, field_count, gz_count, table_ref, lines_ref, index_ref, wave_ref, out_ref,
    prod, vals, keys, lines, index, send, recv, own, index_send, index_recv, index_own,
):
    devices = field_count * gz_count
    me_field, me_gz = lax.axis_index("field"), lax.axis_index("gz")
    far = gz_count // 2
    mine = (gz_count - far) * field_count

    def peer(step):
        f = lax.rem(me_field + lax.rem(step, field_count), field_count)
        g = lax.rem(me_gz + step // field_count + far, gz_count)
        return f, g

    def others(run):
        def loop(step, carry):
            run(step)
            return carry

        lax.fori_loop(0, mine, loop, 0)
        lax.fori_loop(mine + 1, devices, loop, 0)

    def along(run):
        def loop(step, carry):
            run(step)
            return carry

        lax.fori_loop(1, gz_count, loop, 0)

    barrier = pltpu.get_barrier_semaphore()
    others(
        lambda step: pl.semaphore_signal(
            barrier, inc=1, device_id=peer(step), device_id_type=pl.DeviceIdType.MESH
        )
    )
    pl.semaphore_wait(barrier, devices - 1)

    def index_copy(step):
        g = lax.rem(me_gz + step, gz_count)
        return pltpu.make_async_remote_copy(
            src_ref=index_ref.at[g],
            dst_ref=index.at[me_gz],
            send_sem=index_send.at[step],
            recv_sem=index_recv.at[step],
            device_id=(me_field, g),
            device_id_type=pl.DeviceIdType.MESH,
        )

    def lines_copy(parity):
        def copy(step):
            f, g = peer(step)
            return pltpu.make_async_remote_copy(
                src_ref=lines_ref.at[f * gz_count + g, parity],
                dst_ref=lines.at[me_field, me_gz, parity],
                send_sem=send.at[parity, step],
                recv_sem=recv.at[parity, step],
                device_id=(f, g),
                device_id_type=pl.DeviceIdType.MESH,
            )

        return copy

    along(lambda step: index_copy(step).start())
    for parity in range(2):
        others(lambda step: lines_copy(parity)(step).start())
    me = me_field * gz_count + me_gz
    kept = [
        pltpu.make_async_copy(
            lines_ref.at[me, parity], lines.at[me_field, me_gz, parity], own.at[parity]
        )
        for parity in range(2)
    ]
    kept_index = pltpu.make_async_copy(index_ref.at[me_gz], index.at[me_gz], index_own)
    for copy in kept + [kept_index]:
        copy.start()

    kept_index.wait()
    along(lambda step: index_copy(step).wait_recv())
    unpack(index, keys)
    for parity in range(2):
        kept[parity].wait()
        others(lambda step: lines_copy(parity)(step).wait_recv())
        products(table_ref, lines, prod, parity)
    bins(length, wave_ref, out_ref, prod, vals, keys)
    along(lambda step: index_copy(step).wait_send())
    for parity in range(2):
        others(lambda step: lines_copy(parity)(step).wait_send())


def bins(length, wave_ref, out_ref, prod, vals, keys):
    quarter, half = length // 4, length // 2
    groups, local = prod.shape[0], prod.shape[3] // (2 * LANES)
    fields = groups * local
    out_ref[...] = jnp.zeros_like(out_ref)
    wave_x = wave_ref[0:1, :]
    wave_y = wave_ref[1:2, :]
    low_iota = lax.broadcasted_iota(jnp.int32, (16, LANES), 0).astype(jnp.float32)
    iotas = [(low_iota + 16.0 * j).astype(jnp.bfloat16) for j in range(LANES // 16)]
    one = jnp.ones((16, LANES), jnp.bfloat16)
    none = jnp.zeros((16, LANES), jnp.bfloat16)

    def cell_row(j, k):
        start = 1 - (k + quarter - 1) // quarter
        return (
            k,
            half - k,
            half + k - quarter * start,
            length - k - quarter * start,
        )[j]

    def tile(t, carry):
        first = pl.multiple_of(t * 8, 8)
        row = lax.broadcasted_iota(jnp.int32, (8, LANES), 0) + first
        special = row == 0

        def load(a, c, parity, sine):
            g, i = a // local, a % local
            at = (c * local + i) * LANES
            return prod[g, parity, pl.ds(sine * quarter + first, 8), at : at + LANES]

        def spectra(a):
            parts = []
            for c in range(2):
                ec, oc = load(a, c, 0, 0), load(a, c, 1, 0)
                es, os = load(a, c, 0, 1), load(a, c, 1, 1)
                p, q, m, n = ec + oc, es + os, ec - oc, os - es
                parts.append(
                    (
                        (p, jnp.where(special, 0.0, q)),
                        (m, jnp.where(special, 0.0, n)),
                        (jnp.where(special, es, m), jnp.where(special, os, -n)),
                        (jnp.where(special, es, p), jnp.where(special, -os, -q)),
                    )
                )
            u, v = parts
            return [(u[j][0] + v[j][1], v[j][0] - u[j][1]) for j in range(4)]

        k = row.astype(jnp.float32)
        zero_wave = (0.0, -half, quarter, -quarter)
        waves = (k, half - k, k - half, -k)
        base = spectra(0)
        second = None
        totals = [None] * 4
        saved = [None] * 4
        pending = [None] * 4
        for a in range(fields):
            spec = base if a == 0 else spectra(a)
            for j in range(4):
                cross = base[j][0] * spec[j][0] + base[j][1] * spec[j][1]
                if a == 0:
                    wz = jnp.where(special, float(zero_wave[j]), waves[j])
                    square = wave_x * wave_x + wave_y * wave_y + wz * wz
                    saved[j] = (wz, 1.0 / square)
                    vals[0, j * 8 : j * 8 + 8] = round16(cross)
                    continue
                wz, inverse = saved[j]
                if a == 1:
                    vals[1, j * 8 : j * 8 + 8] = round16(cross)
                    term = -0.5 * cross
                else:
                    weight = (
                        1.5 * wave_x * wave_x,
                        1.5 * wave_y * wave_y,
                        1.5 * wz * wz,
                        3.0 * wave_x * wave_y,
                        3.0 * wave_x * wz,
                        3.0 * wave_y * wz,
                    )[a - 2]
                    term = weight * inverse * cross
                pending[j] = term if pending[j] is None else pending[j] + term
                if a % local == local - 1:
                    rounded = round16(pending[j])
                    totals[j] = rounded if totals[j] is None else totals[j] + rounded
                    pending[j] = None
        for j in range(4):
            high = round16(totals[j])
            vals[2, j * 8 : j * 8 + 8] = high
            vals[3, j * 8 : j * 8 + 8] = totals[j] - high
        total = out_ref[...]
        for start in range(0, 32, PAIRS):
            left, hot = [], []
            for r in range(start, start + PAIRS):
                cell = cell_row(r // 8, first + r % 8)
                spread = [
                    jnp.broadcast_to(part, (16, LANES)).astype(jnp.bfloat16)
                    for part in [vals[i, r : r + 1] for i in range(4)]
                    + [keys[i, pl.ds(cell, 1), :] for i in range(2)]
                ]
                match = spread[4] == iotas[0]
                left.append(
                    jnp.concatenate(
                        [jnp.where(match, spread[i], none) for i in range(4)]
                        + [jnp.where(match, one, none)],
                        axis=0,
                    )
                )
                hot.append(
                    jnp.concatenate(
                        [jnp.where(spread[5] == it, one, none) for it in iotas], axis=0
                    )
                )
            total = total + lax.dot_general(
                jnp.concatenate(left, axis=1),
                jnp.concatenate(hot, axis=1),
                (((1,), (1,)), ((), ())),
                preferred_element_type=jnp.float32,
            )
        out_ref[...] = total
        return carry

    lax.fori_loop(0, quarter // 8, tile, 0)


def relayout_kernel(fields_ref, out_ref):
    for c in range(2):
        for i in range(fields_ref.shape[2]):
            at = (c * fields_ref.shape[2] + i) * LANES
            for h in range(out_ref.shape[1]):
                block = fields_ref[:, c, i, :, h * LANES : (h + 1) * LANES]
                block = block.reshape(16, 2, block.shape[1], LANES)
                for parity in range(2):
                    out_ref[:, h, parity, :, at : at + LANES] = jnp.swapaxes(
                        block[:, parity], 0, 1
                    )


def relayout(fields):
    depth, _, local, planes, yrows = fields.shape
    parts = yrows // LANES
    out = pl.pallas_call(
        relayout_kernel,
        grid=(depth // 32,),
        out_shape=jax.ShapeDtypeStruct(
            (planes, parts, 2, depth // 2, 2 * local * LANES), fields.dtype
        ),
        in_specs=[pl.BlockSpec((32, 2, local, planes, yrows), lambda i: (i, 0, 0, 0, 0))],
        out_specs=pl.BlockSpec(
            (planes, parts, 2, 16, 2 * local * LANES), lambda i: (0, 0, 0, i, 0)
        ),
    )(fields)
    return out.reshape(planes * parts, 2, depth // 2, 2 * local * LANES)


def reduce_kernel(field_count, gz_count, mine_ref, out_ref, parts, answer, send, recv, send2, recv2):
    devices = field_count * gz_count
    me_field, me_gz = lax.axis_index("field"), lax.axis_index("gz")
    me = me_field * gz_count + me_gz

    def peer(step):
        other = lax.rem(me + step, devices)
        return other, (other // gz_count, lax.rem(other, gz_count))

    barrier = pltpu.get_barrier_semaphore()

    def greet(step, carry):
        _, place = peer(step)
        pl.semaphore_signal(
            barrier, inc=1, device_id=place, device_id_type=pl.DeviceIdType.MESH
        )
        return carry

    lax.fori_loop(1, devices, greet, 0)
    pl.semaphore_wait(barrier, devices - 1)

    def scatter(step):
        other, place = peer(step)
        return pltpu.make_async_remote_copy(
            src_ref=mine_ref.at[other],
            dst_ref=parts.at[step],
            send_sem=send.at[step],
            recv_sem=recv.at[step],
            device_id=place,
            device_id_type=pl.DeviceIdType.MESH,
        )

    def gather(step):
        _, place = peer(step)
        return pltpu.make_async_remote_copy(
            src_ref=answer,
            dst_ref=out_ref.at[me],
            send_sem=send2.at[step],
            recv_sem=recv2.at[step],
            device_id=place,
            device_id_type=pl.DeviceIdType.MESH,
        )

    def start(copy):
        def run(step, carry):
            copy(step).start()
            return carry

        lax.fori_loop(1, devices, run, 0)

    start(scatter)

    def collect(step, total):
        scatter(step).wait_recv()
        return total + parts[step]

    answer[...] = lax.fori_loop(1, devices, collect, mine_ref[me])
    start(gather)
    out_ref[me] = answer[...]

    def finish(step, carry):
        scatter(step).wait_send()
        gather(step).wait()
        return carry

    lax.fori_loop(1, devices, finish, 0)


def all_reduce(total, field_count, gz_count):
    devices = field_count * gz_count
    rows = max(1, total.shape[0] // devices)
    total = jnp.pad(total, ((0, devices * rows - total.shape[0]), (0, 0)))
    total = total.reshape(devices, rows, LANES)
    return pl.pallas_call(
        functools.partial(reduce_kernel, field_count, gz_count),
        out_shape=jax.ShapeDtypeStruct(total.shape, jnp.float32),
        in_specs=[pl.BlockSpec(memory_space=pltpu.VMEM)],
        out_specs=pl.BlockSpec(memory_space=pltpu.VMEM),
        scratch_shapes=[
            pltpu.VMEM(total.shape, jnp.float32),
            pltpu.VMEM(total.shape[1:], jnp.float32),
            pltpu.SemaphoreType.DMA((devices,)),
            pltpu.SemaphoreType.DMA((devices,)),
            pltpu.SemaphoreType.DMA((devices,)),
            pltpu.SemaphoreType.DMA((devices,)),
        ],
        compiler_params=pltpu.CompilerParams(collective_id=0, has_side_effects=True),
    )(total).reshape(devices * rows, LANES)


SLOTS = 6
KEPT = 5


def wave_tables(length):
    quarter, half = length // 4, length // 2
    unit = 2.0 * math.pi / length

    def pair(rows, stride):
        row = np.arange(rows)[None, :, None] * stride
        depth = 2 * np.arange(half)[None, None, :] + np.arange(2)[:, None, None]
        angle = (row * depth % length).astype(np.float32) * np.float32(unit)
        return np.cos(angle), np.sin(angle)

    ca, sa = pair(quarter // 16, 16)
    cb, sb = pair(16, 1)
    return np.stack([ca, sa]), np.stack([cb, sb])


def build_table(length, coarse_ref, fine_ref, table):
    quarter, half = length // 4, length // 2
    factor = 1.0 / math.sqrt(length)
    parts = table.shape[0]
    wide = half // parts

    def rows_of(a, carry):
        rows = pl.ds(pl.multiple_of(a * 16, 16), 16)
        under = pl.ds(pl.multiple_of(quarter + a * 16, 16), 16)
        for parity in range(2):
            for q in range(parts):
                at = slice(q * wide, (q + 1) * wide)
                ca, sa = (coarse_ref[i, parity, pl.ds(a, 1), at] for i in range(2))
                cb, sb = (fine_ref[i, parity, :, at] for i in range(2))
                cos_part = (ca * cb - sa * sb) * factor
                sin_part = (sa * cb + ca * sb) * factor
                row = lax.broadcasted_iota(jnp.int32, sin_part.shape, 0) + a
                column = lax.broadcasted_iota(jnp.int32, sin_part.shape, 1)
                alternate = (1 - 2 * (column % 2)).astype(jnp.float32) * factor
                sin_part = jnp.where(row == 0, alternate, sin_part)
                table[q, parity, rows, :] = cos_part.astype(jnp.bfloat16)
                table[q, parity, under, :] = sin_part.astype(jnp.bfloat16)
        return carry

    lax.fori_loop(0, quarter // 16, rows_of, 0)


def split_keys(index, keys):
    depth = index.shape[1]

    def block(g, carry):
        word = index[g]
        mu = lax.shift_right_logical(word, 16)
        shell = word & 65535
        rows = pl.ds(pl.multiple_of(g * depth, depth), depth)
        keys[0, rows, :] = (mu + MUBINS * lax.shift_right_logical(shell, 7)).astype(jnp.float32)
        keys[1, rows, :] = (shell & (LANES - 1)).astype(jnp.float32)
        return carry

    lax.fori_loop(0, index.shape[0], block, 0)


def arrange(length, me_field, stage, spread, chunk):
    planes = stage.shape[3]
    rows = pl.ds(pl.multiple_of(chunk * 16, 16), 16)

    def put(block, h, i, c):
        block = block.reshape(16, 2, planes, LANES)
        for parity in range(2):
            spread[:, h, i, parity, rows, c * LANES : (c + 1) * LANES] = jnp.swapaxes(
                block[:, parity], 0, 1
            )

    def take(c, i, h):
        return stage[:, c, i, :, h * LANES : (h + 1) * LANES]

    @pl.when(me_field % 2 == 0)
    def _():
        for c in range(2):
            for i in range(2):
                for h in range(2):
                    put(take(c, i, h), h, i, c)

    @pl.when(me_field % 2 == 1)
    def _():
        wave_x = lax.broadcasted_iota(jnp.int32, (planes, LANES), 0).astype(jnp.float32)
        wave_x = wave_x + float(length // 4)
        squared = me_field == 1
        for h in range(2):
            wave_y = lax.broadcasted_iota(jnp.int32, (planes, LANES), 1).astype(jnp.float32)
            wave_y = wave_y + float(length // 8 + h * LANES)
            first = jnp.where(squared, 1.5 * wave_x * wave_x, wave_x)[None]
            other = jnp.where(squared, 1.5 * wave_y * wave_y, wave_y)[None]
            for c in range(2):
                value = first * take(c, 0, h).astype(jnp.float32)
                value = value + other * take(c, 1, h).astype(jnp.float32)
                put(value.astype(jnp.bfloat16), h, 0, c)


def transform(table, land, prod, fields, start, sources, sums):
    wide = prod.shape[3]
    quads = [sums[4 * n : 4 * n + 4] for n in range(4)]

    def group(a, carry):
        for parity in range(2):
            for n, (plane, local) in enumerate(sources):
                right = land[local, a, parity].reshape(-1, wide)
                for mxu in range(2):
                    pltpu.matmul_push_rhs(right, n % 2, mxu)
                    for i in range(4):
                        at = (4 * mxu + i) * LANES
                        pltpu.matmul_acc_lhs(
                            quads[2 * mxu + parity][i],
                            table[plane, parity, at : at + LANES, :],
                            n % 2 if i == 0 else None,
                        )
            for mxu in range(2):
                for i in range(4):
                    at = (4 * mxu + i) * LANES
                    prod[start + a, parity, at : at + LANES, :] = pltpu.matmul_pop(
                        quads[2 * mxu + parity][i]
                    )
        return carry

    lax.fori_loop(0, fields, group, 0)


def histogram(length, plane, prod, vals, keys, acc, low, high, sums, counting):
    quarter, half = length // 4, length // 2
    groups, mxus = 4, 2
    lane = lax.broadcasted_iota(jnp.int32, (8, LANES), 1).astype(jnp.float32)
    wave_x = (length // 4 + plane // 2).astype(jnp.float32)
    wave_y = (length // 8 + (plane % 2) * LANES).astype(jnp.float32) + lane
    flat = wave_x * wave_x + wave_y * wave_y
    low_iota = lax.broadcasted_iota(jnp.int32, (16, LANES), 0).astype(jnp.float32)
    iotas = [(low_iota + 16.0 * j).astype(jnp.bfloat16) for j in range(LANES // 16)]
    one = jnp.ones((16, LANES), jnp.bfloat16)
    none = jnp.zeros((16, LANES), jnp.bfloat16)

    def cell_row(j, k):
        start = 1 - (k + quarter - 1) // quarter
        return (
            k,
            half - k,
            half + k - quarter * start,
            length - k - quarter * start,
        )[j]

    def values(t, edge, slot):
        first = t * 8 if edge else pl.multiple_of(t * 8, 8)
        row = lax.broadcasted_iota(jnp.int32, (8, LANES), 0) + first
        special = row == 0

        def load(a, c, parity, sine):
            at = pl.ds(sine * quarter + first, 8)
            return prod[a, parity, at, c * LANES : (c + 1) * LANES]

        def spectra(a):
            parts = []
            for c in range(2):
                ec, oc = load(a, c, 0, 0), load(a, c, 1, 0)
                es, os = load(a, c, 0, 1), load(a, c, 1, 1)
                p, q, m, n = ec + oc, es + os, ec - oc, os - es
                if edge:
                    parts.append(
                        (
                            (p, jnp.where(special, 0.0, q)),
                            (m, jnp.where(special, 0.0, n)),
                            (jnp.where(special, es, m), jnp.where(special, os, -n)),
                            (jnp.where(special, es, p), jnp.where(special, -os, -q)),
                        )
                    )
                else:
                    parts.append(((p, q), (m, n), (m, n), (p, q)))
            u, v = parts
            result = []
            for j in range(4):
                if edge or j < 2:
                    result.append((u[j][0] + v[j][1], v[j][0] - u[j][1]))
                else:
                    result.append((u[j][0] - v[j][1], v[j][0] + u[j][1]))
            return result

        k = row.astype(jnp.float32)
        zero_wave = (0.0, -half, quarter, -quarter)
        waves = [k, half - k, k - half, -k]
        if edge:
            waves = [jnp.where(special, float(z), w) for z, w in zip(zero_wave, waves)]
            inverse = [1.0 / (flat + w * w) for w in waves]
        else:
            inverse = [1.0 / (flat + w * w) for w in waves[:2]]
            inverse = [inverse[0], inverse[1], inverse[1], inverse[0]]
        base, first_cross, cross_b, cubic, mixed = (spectra(a) for a in range(KEPT))
        for j in range(4):
            re, im = base[j]
            auto = re * re + im * im
            pair = re * first_cross[j][0] + im * first_cross[j][1]
            w = waves[j]
            three, half_more = 3.0 * w, 1.5 * (w * w)
            qre = mixed[j][0] + three * cross_b[j][0] + half_more * cubic[j][0]
            qim = mixed[j][1] + three * cross_b[j][1] + half_more * cubic[j][1]
            quad = inverse[j] * (re * qre + im * qim) - 0.5 * pair
            vals[slot, 0, j * 8 : j * 8 + 8] = jnp.where(counting, 1.0, auto)
            vals[slot, 1, j * 8 : j * 8 + 8] = pair
            vals[slot, 2, j * 8 : j * 8 + 8] = quad

    def one_hots(r, cell, slot):
        spread = [
            jnp.broadcast_to(part, (16, LANES)).astype(jnp.bfloat16)
            for part in [vals[slot, i, r : r + 1] for i in range(3)]
            + [keys[i, pl.ds(cell, 1), :] for i in range(2)]
        ]
        match = spread[3] == iotas[0]
        left = [jnp.where(match, spread[i], none) for i in range(3)]
        left = jnp.concatenate(left + [none], axis=0)
        hot = [jnp.where(spread[4] == it, one, none) for it in iotas]
        return left, jnp.concatenate(hot, axis=0)

    def units(t, slot):
        first = t * 8
        for unit in range(4):
            mxu, stage = unit % mxus, unit // mxus
            lefts, hots = [], []
            for g in range(groups):
                pair = []
                for r in range(unit * 8 + g * 2, unit * 8 + g * 2 + 2):
                    pair.append(one_hots(r, cell_row(r // 8, first + r % 8), slot))
                lefts.append(jnp.concatenate([x[0] for x in pair], axis=1))
                hots.append(jnp.concatenate([x[1] for x in pair], axis=1))
            pltpu.matmul_push_rhs(jnp.concatenate(lefts, axis=0), stage, mxu, transpose=True)
            for g in range(groups):
                pltpu.matmul_acc_lhs(sums[8 * mxu + g], hots[g], stage if g == 0 else None)

    @pl.when(low == 0)
    def _():
        values(0, True, 0)

    @pl.when(low != 0)
    def _():
        values(low, False, 0)

    def step(n, carry):
        for i in range(4):
            t = low + 4 * n + i
            units(t, i % 2)
            values(jnp.minimum(t + 1, quarter // 8 - 1), False, 1 - i % 2)
        return carry

    lax.fori_loop(0, (high - low) // 4, step, 0)
    total = None
    for g in range(groups):
        block = pltpu.matmul_pop(sums[g]) + pltpu.matmul_pop(sums[8 + g])
        block = block[:, g // 2 * LANES : (g // 2 + 1) * LANES]
        block = jnp.transpose(block)[g % 2 * 64 : g % 2 * 64 + 64]
        total = block if total is None else total + block
    acc[...] += total


def whole_kernel(
    length, coarse_ref, fine_ref, fields_ref, shells_ref, mubins_ref, out_ref,
    stage, spread, mix, joined, first, land, prod, table, raw, index_out, index, keys, vals, acc,
    parts, answer,
    stage_sem, raw_sem, index_sent, index_come, mix_sent, mix_come, land_sent, first_come,
    land_come, part_sent, part_come, answer_sent, answer_come,
):
    fields, cores, chunks = 4, 2, 2
    planes_z = table.shape[0]
    gz_count = planes_z * cores
    owners = gz_count // chunks
    devices = fields * gz_count
    me_field, me_gz = lax.axis_index("field"), lax.axis_index("gz")
    me = me_field * gz_count + me_gz
    me_plane, me_core = me_gz // cores, me_gz % cores
    me_half, me_owner = me_gz // owners, me_gz % owners
    steps = fields_ref.shape[0] // 32
    MESH = pl.DeviceIdType.MESH

    def loop(low, high, run):
        def step(i, carry):
            run(i)
            return carry

        lax.fori_loop(low, high, step, 0)

    def wait(ref, sem):
        pltpu.make_async_copy(ref, ref, sem).wait()

    barrier = pltpu.get_barrier_semaphore()

    def greet(step):
        other = lax.rem(me + step, devices)
        pl.semaphore_signal(
            barrier, inc=1, device_id=(other // gz_count, lax.rem(other, gz_count)),
            device_id_type=MESH,
        )

    loop(1, devices, greet)

    def raw_copy(b):
        lanes = pl.ds(pl.multiple_of((b % 2) * LANES, LANES), LANES)
        at = (slice(None), me_field * (gz_count // 2) + b // 2, lanes)
        return [
            pltpu.make_async_copy(ref.at[at], raw.at[i, b], raw_sem.at[i])
            for i, ref in enumerate((shells_ref, mubins_ref))
        ]

    def fetch(n):
        return pltpu.make_async_copy(
            fields_ref.at[pl.ds(n * 32, 32)], stage.at[n % 2], stage_sem.at[n % 2]
        )

    loop(0, gz_count, lambda b: [copy.start() for copy in raw_copy(b)])
    for n in range(2):
        fetch(n).start()
    for i in range(2):
        wait(raw.at[i], raw_sem.at[i])

    def join(n):
        index_out[n] = raw[0, n] + raw[1, n] * 65536

    loop(0, gz_count, join)
    pl.semaphore_wait(barrier, devices - 1)

    def owner_of(i):
        plane = lax.rem(me_plane + 1 + (i % owners) // 2, 2)
        return plane * cores + lax.rem(me_core + i, cores)

    def forward(source, goal, sent, come, g):
        pltpu.make_async_remote_copy(
            src_ref=source, dst_ref=goal, send_sem=sent, recv_sem=come,
            device_id=(me_field, g), device_id_type=MESH,
        ).start()

    def index_send(i):
        chunk, owner = i // owners, owner_of(i)
        b = chunk * owners + owner
        goal = index.at[chunk, me_gz]
        forward(
            index_out.at[b], goal, index_sent, index_come.at[chunk],
            (1 - me_half) * owners + owner,
        )

        @pl.when(owner != me_owner)
        def _():
            forward(
                index_out.at[b], goal, index_sent, index_come.at[chunk],
                me_half * owners + owner,
            )

        @pl.when(owner == me_owner)
        def _():
            pltpu.make_async_copy(index_out.at[b], goal, index_come.at[chunk]).start()

    loop(0, gz_count, index_send)

    def place(n):
        fetch(n).wait()
        arrange(length, me_field, stage.at[n % 2], spread, n)

        @pl.when(n + 2 < steps)
        def _():
            fetch(n + 2).start()

    loop(0, steps, place)

    even = 1 - me_field % 2
    slot = even * (3 * me_field // 2) + (1 - even) * ((13 - 3 * me_field) // 2)

    def mix_send(i):
        b = (i // owners) * owners + owner_of(i)

        def piece(f, s):
            return spread.at[f * (gz_count // 2) + b // 2, b % 2, s]

        def send(f, s):
            pltpu.make_async_remote_copy(
                src_ref=piece(f, s), dst_ref=mix.at[b, slot + s],
                send_sem=mix_sent, recv_sem=mix_come.at[b],
                device_id=(f, me_gz), device_id_type=MESH,
            ).start()

        def keep(s):
            pltpu.make_async_copy(
                piece(me_field, s), mix.at[b, slot + s], mix_come.at[b]
            ).start()

        others = [lax.rem(me_field + 2, 4), me_field + 1 - 2 * (me_field % 2), 3 - me_field]
        for f in others:
            send(f, 0)
        keep(0)

        @pl.when(even == 1)
        def _():
            for f in others:
                send(f, 1)
            keep(1)

    loop(0, gz_count, mix_send)
    build_table(length, coarse_ref, fine_ref, table)
    acc[...] = jnp.zeros_like(acc)

    def join_send(i):
        chunk, owner = i // owners, owner_of(i)
        b = chunk * owners + owner
        wait(mix.at[b], mix_come.at[b])
        wave_x = (length // 4 + me_field * (gz_count // 2) + b // 2).astype(jnp.float32)
        lane = lax.broadcasted_iota(jnp.int32, (1, 2 * LANES), 1) % LANES
        wave_y = (length // 8 + (b % 2) * LANES + lane).astype(jnp.float32)
        weight = 3.0 * wave_x * wave_y
        for parity in range(2):
            value = mix[b, 5, parity].astype(jnp.float32)
            value = value + weight * mix[b, 4, parity].astype(jnp.float32)
            joined[b, parity] = value.astype(jnp.bfloat16)
        base = (mix.at[b, 0], first.at[chunk, me_plane, 0, :, me_core])
        me_near = me_plane % 2
        pairs = (
            (mix.at[b, pl.ds(1, 3)], land.at[chunk, me_near, pl.ds(0, 3), :, me_core]),
            (joined.at[b], land.at[chunk, me_near, 3, :, me_core]),
        )
        forward(*base, land_sent, first_come.at[chunk, me_gz], (1 - me_half) * owners + owner)

        @pl.when(owner != me_owner)
        def _():
            g = me_half * owners + owner
            forward(*base, land_sent, first_come.at[chunk, me_gz], g)
            for source, goal in pairs:
                forward(source, goal, land_sent, land_come.at[chunk, me_owner], g)

        @pl.when(owner == me_owner)
        def _():
            pltpu.make_async_copy(*base, first_come.at[chunk, me_gz]).start()
            for source, goal in pairs:
                pltpu.make_async_copy(source, goal, land_come.at[chunk, me_owner]).start()

    def transform_lines(chunk, sums):
        near = 1 - 2 * (me_plane % 2)
        sources = [(me_plane + hop, lax.rem(me_plane + hop, 2)) for hop in (0, near)]
        for _, local in sources:
            for core in range(cores):
                wait(land.at[chunk, local, :, :, core], land_come.at[chunk, local * cores + core])
        transform(table, land.at[chunk], prod, KEPT - 1, 1, sources, sums)
        sources = [(n, n) for n in range(planes_z)]
        for plane, _ in sources:
            for core in range(cores):
                block = first.at[chunk, plane, :, :, core]
                wait(block, first_come.at[chunk, plane * cores + core])
        transform(table, first.at[chunk], prod, 1, 0, sources, sums)

    tiles = length // 32
    span = tiles // owners

    def bin_lines(chunk, low, high, sums):
        b = me_field * gz_count + chunk * owners + me_owner
        histogram(length, b, prod, vals, keys.at[chunk], acc, low, high, sums, me_half == 1)

    loop(0, owners, join_send)
    for chunk in range(chunks):
        wait(index.at[chunk], index_come.at[chunk])
        split_keys(index.at[chunk], keys.at[chunk])
    join_send(owners)

    def crunch(*sums):
        for ref in sums:
            pltpu.matmul_pop(ref)

        def part(n):
            chunk = n // owners

            @pl.when(n % owners == 0)
            def _():
                transform_lines(chunk, sums)

            low = lax.rem(n, owners) * span
            high = low + span + chunk * (tiles - span)
            bin_lines(chunk, low, high, sums)

            @pl.when(n < owners - 1)
            def _():
                join_send(owners + 1 + n)

        loop(0, owners + 1, part)

    pl.run_scoped(
        crunch,
        *(
            pltpu.ACC(mxu)((LANES, 2 * LANES), jnp.float32)
            for mxu in range(2)
            for _ in range(8)
        ),
    )

    counted = acc[0:LOW, :]
    acc[0:LOW, :] = jnp.where(me_half == 1, 0.0, counted)
    acc[3 * LOW : 4 * LOW, :] = jnp.where(me_half == 1, counted, 0.0)
    ranks = acc.shape[0] // 8
    middle = (planes_z // 2 - 1) * cores
    rank = me_field + fields * lax.div(me_gz - middle, cores)
    root = (me_gz == middle) | (me_gz == middle + cores)

    def part_copy(r):
        return pltpu.make_async_remote_copy(
            src_ref=acc.at[pl.ds(pl.multiple_of(r * 8, 8), 8)], dst_ref=parts.at[me],
            send_sem=part_sent, recv_sem=part_come,
            device_id=(lax.rem(r, fields), middle + cores * (r // fields)),
            device_id_type=MESH,
        )

    def part_send(n):
        r = lax.rem(me_field + n, ranks)

        @pl.when((r != rank) | jnp.logical_not(root))
        def _():
            part_copy(r).start()

    loop(0, ranks, part_send)

    def answer_copy(step):
        other = lax.rem(me + step, devices)
        return pltpu.make_async_remote_copy(
            src_ref=answer.at[rank], dst_ref=answer.at[rank],
            send_sem=answer_sent, recv_sem=answer_come,
            device_id=(other // gz_count, lax.rem(other, gz_count)), device_id_type=MESH,
        )

    @pl.when(root)
    def _():
        parts[me] = acc[pl.ds(pl.multiple_of(rank * 8, 8), 8), :]
        rest = parts.at[pl.ds(0, devices - 1)]
        wait(rest, part_come)
        answer[rank] = lax.fori_loop(
            1, devices, lambda d, total: total + parts[d], parts[0]
        )
        loop(1, devices, lambda step: answer_copy(step).start())
        got = answer.at[pl.ds(0, ranks - 1)]
        wait(got, answer_come)
        wait(rest, answer_sent)
        wait(got, part_sent)

    @pl.when(jnp.logical_not(root))
    def _():
        wait(answer, answer_come)
        wait(answer, part_sent)

    for hi in range(2):
        scale = 1.0 / jnp.maximum(answer[6 + hi], 1.0)
        for m in range(3):
            out_ref[m, :, hi * LANES : (hi + 1) * LANES] = answer[2 * m + hi] * scale

    for _ in range(2):
        sent = index_out.at[pl.ds(0, gz_count - 1)]
        wait(sent, index_sent)
    wait(mix.at[:, 0], land_sent)
    wait(mix.at[pl.ds(0, 2 * (owners - 1)), pl.ds(0, KEPT)], land_sent)

    @pl.when(even == 1)
    def _():
        wait(spread.at[pl.ds(0, 12)], mix_sent)

    @pl.when(even == 0)
    def _():
        wait(spread.at[pl.ds(0, 12), :, 0], mix_sent)


def whole(fields, shells, mubins, gz_count):
    depth, _, local, planes, yrows = fields.shape
    length = depth * gz_count
    half = length // 2
    coarse, fine = wave_tables(length)
    vmem, anywhere = pl.BlockSpec(memory_space=pltpu.VMEM), pl.BlockSpec(memory_space=pl.ANY)
    wide = 2 * LANES
    dma = pltpu.SemaphoreType.DMA
    low = jnp.bfloat16
    line_block = (2, depth // 2, wide)
    pair_block = (2, 2, depth // 2, wide)
    return pl.pallas_call(
        functools.partial(whole_kernel, length),
        out_shape=jax.ShapeDtypeStruct((3, MUBINS, SHELLS), jnp.float32),
        in_specs=[vmem, vmem, anywhere, anywhere, anywhere],
        out_specs=vmem,
        scratch_shapes=[
            pltpu.VMEM((2, 32) + fields.shape[1:], low),
            pltpu.VMEM((planes, 2, local) + line_block, low),
            pltpu.VMEM((gz_count, SLOTS) + line_block, low),
            pltpu.VMEM((gz_count,) + line_block, low),
            pltpu.VMEM((2, gz_count // 2, 1) + pair_block, low),
            pltpu.VMEM((2, gz_count // 4, KEPT - 1) + pair_block, low),
            pltpu.VMEM((KEPT, 2, half, wide), jnp.float32),
            pltpu.VMEM((gz_count // 2, 2, half, depth), low),
            pltpu.VMEM((2, gz_count, depth, LANES), jnp.int32),
            pltpu.VMEM((gz_count, depth, LANES), jnp.int32),
            pltpu.VMEM((2, gz_count, depth, LANES), jnp.int32),
            pltpu.VMEM((2, 2, length, LANES), jnp.float32),
            pltpu.VMEM((2, 3, 32, LANES), jnp.float32),
            pltpu.VMEM((4 * LOW, LANES), jnp.float32),
            pltpu.VMEM((4 * gz_count, 8, LANES), jnp.float32),
            pltpu.VMEM((8, 8, LANES), jnp.float32),
            dma((2,)), dma((2,)), dma, dma((2,)), dma, dma((gz_count,)), dma,
            dma((2, gz_count)), dma((2, gz_count // 2)), dma, dma, dma, dma,
        ],
        compiler_params=pltpu.CompilerParams(
            vmem_limit_bytes=60 * 1024 * 1024, collective_id=2, has_side_effects=True
        ),
    )(jnp.asarray(coarse), jnp.asarray(fine), fields, shells, mubins)


def body(fields, shells, mubins):
    depth_local, _, local_fields, planes, yrows = fields.shape
    gz_count, field_count = lax.axis_size("gz"), lax.axis_size("field")
    devices = gz_count * field_count
    length = depth_local * gz_count
    half = length // 2
    plane_rows = planes * yrows
    width = plane_rows // devices
    me_gz, me_field = lax.axis_index("gz"), lax.axis_index("field")

    paired = yrows == 2 * LANES and 2 * planes == devices and local_fields == 2
    if paired and depth_local == 2 * LANES and gz_count == 2 * field_count == MUBINS:
        return whole(fields, shells, mubins, gz_count)

    exchange = width == LANES and depth_local % 32 == 0
    if exchange:
        lines = relayout(fields)
    else:
        lines = fields.reshape(depth_local // 2, 2, 2, local_fields, devices, width)
        lines = lines.transpose(4, 1, 0, 2, 3, 5).reshape(
            devices, 2, depth_local // 2, 2 * local_fields * width
        )

    share = planes // field_count
    shells, mubins = (
        lax.dynamic_slice_in_dim(ids, me_field * share, share, 1) for ids in (shells, mubins)
    )
    index = (shells + mubins * 65536).reshape(depth_local, gz_count, width).transpose(1, 0, 2)

    span = 2 * local_fields * LANES
    table = quarter_tables(length, jnp.minimum(me_gz, 0))
    column = (me_field * gz_count + me_gz) * width + jnp.arange(LANES, dtype=jnp.int32)
    waves = jnp.stack([length // 4 + column // yrows, length // 8 + column % yrows])
    waves = jnp.pad(waves.astype(jnp.float32), ((0, 6), (0, 0)))
    landed = (field_count, gz_count, 2, depth_local // 2, span)
    scratch = [
        pltpu.VMEM((field_count, 2, half, span), jnp.float32),
        pltpu.VMEM((4, 32, LANES), jnp.float32),
        pltpu.VMEM((2, length, LANES), jnp.float32),
    ]
    vmem, anywhere = pl.BlockSpec(memory_space=pltpu.VMEM), pl.BlockSpec(memory_space=pl.ANY)
    if exchange:
        run, places, wide = (
            functools.partial(exchange_kernel, length, field_count, gz_count),
            anywhere,
            dict(collective_id=1, has_side_effects=True),
        )
        scratch += [
            pltpu.VMEM(landed, jnp.bfloat16),
            pltpu.VMEM((gz_count, depth_local, LANES), jnp.int32),
            pltpu.SemaphoreType.DMA((2, devices)),
            pltpu.SemaphoreType.DMA((2, devices)),
            pltpu.SemaphoreType.DMA((2,)),
            pltpu.SemaphoreType.DMA((gz_count,)),
            pltpu.SemaphoreType.DMA((gz_count,)),
            pltpu.SemaphoreType.DMA,
        ]
    else:
        run, places, wide = functools.partial(local_kernel, length), vmem, {}
        lines = lax.all_to_all(lines, ("field", "gz"), split_axis=0, concat_axis=0, tiled=True)
        lines = lines.reshape(landed[:-1] + (2 * local_fields, width))
        lines = jnp.pad(lines, ((0, 0),) * 5 + ((0, LANES - width),)).reshape(landed)
        index = lax.all_to_all(index, "gz", split_axis=0, concat_axis=0, tiled=True)
        index = jnp.pad(index, ((0, 0), (0, 0), (0, LANES - width)), constant_values=SHELLS)

    total = pl.pallas_call(
        run,
        out_shape=jax.ShapeDtypeStruct((ROWS * LOW, LANES), jnp.float32),
        in_specs=[vmem, places, places, vmem],
        out_specs=vmem,
        scratch_shapes=scratch,
        compiler_params=pltpu.CompilerParams(vmem_limit_bytes=56 * 1024 * 1024, **wide),
    )(table, lines, index, waves)

    total = total.reshape(ROWS, LOW, LANES)
    total = jnp.concatenate([total[:2], total[2:3] + total[3:4], total[4:]])
    total = all_reduce(total.reshape(-1, LANES), field_count, gz_count)[: 4 * LOW]
    total = total.reshape(4, 2, MUBINS, LANES).transpose(0, 2, 3, 1)
    total = total.reshape(4, MUBINS, SHELLS)
    return total[:3] / jnp.maximum(total[3], 1.0)[None]


def solution(mesh):
    in_specs = (P("gz", None, "field", None, None), P("gz", None, None), P("gz", None, None))
    return jax.shard_map(body, mesh=mesh, in_specs=in_specs, out_specs=P(), check_vma=False)
```

```python
import functools
import math

import jax
import jax.numpy as jnp
import numpy as np
from jax import lax
from jax.experimental import pallas as pl
from jax.experimental.pallas import tpu as pltpu
from jax.sharding import PartitionSpec as P

SHELLS = 256
MUBINS = 8
LANES = 128
LOW = 16
ROWS = 5
PAIRS = 8


def quarter_tables(length, zero):
    quarter, half = length // 4, length // 2
    unit = 2.0 * math.pi / length
    factor = 1.0 / math.sqrt(length)

    def pair(rows, stride):
        shape = (2, rows, half)
        parity = lax.broadcasted_iota(jnp.int32, shape, 0)
        row = lax.broadcasted_iota(jnp.int32, shape, 1) * stride + zero
        depth = 2 * lax.broadcasted_iota(jnp.int32, shape, 2) + parity
        angle = (row * depth % length).astype(jnp.float32) * unit
        return jnp.cos(angle), jnp.sin(angle)

    fine = 16
    ca, sa, cb, sb = lax.optimization_barrier(pair(quarter // fine, fine) + pair(fine, 1))
    ca, sa, cb, sb = ca[:, :, None], sa[:, :, None], cb[:, None], sb[:, None]
    cos_part = ((ca * cb - sa * sb) * factor).reshape(2, quarter, half)
    sin_part = ((sa * cb + ca * sb) * factor).reshape(2, quarter, half)
    row = lax.broadcasted_iota(jnp.int32, sin_part.shape, 1)
    column = lax.broadcasted_iota(jnp.int32, sin_part.shape, 2)
    alternate = (1 - 2 * (column % 2)).astype(jnp.float32) * factor
    sin_part = jnp.where(row == 0, alternate, sin_part)
    return jnp.concatenate(
        [cos_part.astype(jnp.bfloat16), sin_part.astype(jnp.bfloat16)], axis=1
    )


def round16(value):
    return value.astype(jnp.bfloat16).astype(jnp.float32)


def unpack(index_ref, keys):
    depth = index_ref.shape[1]

    def block(g, carry):
        word = index_ref[g]
        mu = word // 65536
        key = (word - mu * 65536) * MUBINS + mu
        upper = key // LOW
        rows = pl.ds(pl.multiple_of(g * depth, depth), depth)
        keys[0, rows, :] = (key - upper * LOW).astype(jnp.float32)
        keys[1, rows, :] = upper.astype(jnp.float32)
        return carry

    lax.fori_loop(0, index_ref.shape[0], block, 0)


def products(table_ref, lines_ref, prod, parity):
    half = table_ref.shape[1]

    def group(f, carry):
        right = lines_ref[f, :, parity].reshape(half, lines_ref.shape[-1])

        def rows_of(i, inner):
            rows = pl.ds(pl.multiple_of(i * 256, 256), 256)
            prod[f, parity, rows, :] = jnp.dot(
                table_ref[parity, rows, :], right, preferred_element_type=jnp.float32
            )
            return inner

        return lax.fori_loop(0, half // 256, rows_of, carry)

    lax.fori_loop(0, prod.shape[0], group, 0)


def local_kernel(length, table_ref, lines_ref, index_ref, wave_ref, out_ref, prod, vals, keys):
    unpack(index_ref, keys)
    products(table_ref, lines_ref, prod, 0)
    products(table_ref, lines_ref, prod, 1)
    bins(length, wave_ref, out_ref, prod, vals, keys)


def exchange_kernel(
    length, field_count, gz_count, table_ref, lines_ref, index_ref, wave_ref, out_ref,
    prod, vals, keys, lines, index, send, recv, own, index_send, index_recv, index_own,
):
    devices = field_count * gz_count
    me_field, me_gz = lax.axis_index("field"), lax.axis_index("gz")
    far = gz_count // 2
    mine = (gz_count - far) * field_count

    def peer(step):
        f = lax.rem(me_field + lax.rem(step, field_count), field_count)
        g = lax.rem(me_gz + step // field_count + far, gz_count)
        return f, g

    def others(run):
        def loop(step, carry):
            run(step)
            return carry

        lax.fori_loop(0, mine, loop, 0)
        lax.fori_loop(mine + 1, devices, loop, 0)

    def along(run):
        def loop(step, carry):
            run(step)
            return carry

        lax.fori_loop(1, gz_count, loop, 0)

    barrier = pltpu.get_barrier_semaphore()
    others(
        lambda step: pl.semaphore_signal(
            barrier, inc=1, device_id=peer(step), device_id_type=pl.DeviceIdType.MESH
        )
    )
    pl.semaphore_wait(barrier, devices - 1)

    def index_copy(step):
        g = lax.rem(me_gz + step, gz_count)
        return pltpu.make_async_remote_copy(
            src_ref=index_ref.at[g],
            dst_ref=index.at[me_gz],
            send_sem=index_send.at[step],
            recv_sem=index_recv.at[step],
            device_id=(me_field, g),
            device_id_type=pl.DeviceIdType.MESH,
        )

    def lines_copy(parity):
        def copy(step):
            f, g = peer(step)
            return pltpu.make_async_remote_copy(
                src_ref=lines_ref.at[f * gz_count + g, parity],
                dst_ref=lines.at[me_field, me_gz, parity],
                send_sem=send.at[parity, step],
                recv_sem=recv.at[parity, step],
                device_id=(f, g),
                device_id_type=pl.DeviceIdType.MESH,
            )

        return copy

    along(lambda step: index_copy(step).start())
    for parity in range(2):
        others(lambda step: lines_copy(parity)(step).start())
    me = me_field * gz_count + me_gz
    kept = [
        pltpu.make_async_copy(
            lines_ref.at[me, parity], lines.at[me_field, me_gz, parity], own.at[parity]
        )
        for parity in range(2)
    ]
    kept_index = pltpu.make_async_copy(index_ref.at[me_gz], index.at[me_gz], index_own)
    for copy in kept + [kept_index]:
        copy.start()

    kept_index.wait()
    along(lambda step: index_copy(step).wait_recv())
    unpack(index, keys)
    for parity in range(2):
        kept[parity].wait()
        others(lambda step: lines_copy(parity)(step).wait_recv())
        products(table_ref, lines, prod, parity)
    bins(length, wave_ref, out_ref, prod, vals, keys)
    along(lambda step: index_copy(step).wait_send())
    for parity in range(2):
        others(lambda step: lines_copy(parity)(step).wait_send())


def bins(length, wave_ref, out_ref, prod, vals, keys):
    quarter, half = length // 4, length // 2
    groups, local = prod.shape[0], prod.shape[3] // (2 * LANES)
    fields = groups * local
    out_ref[...] = jnp.zeros_like(out_ref)
    wave_x = wave_ref[0:1, :]
    wave_y = wave_ref[1:2, :]
    low_iota = lax.broadcasted_iota(jnp.int32, (16, LANES), 0).astype(jnp.float32)
    iotas = [(low_iota + 16.0 * j).astype(jnp.bfloat16) for j in range(LANES // 16)]
    one = jnp.ones((16, LANES), jnp.bfloat16)
    none = jnp.zeros((16, LANES), jnp.bfloat16)

    def cell_row(j, k):
        start = 1 - (k + quarter - 1) // quarter
        return (
            k,
            half - k,
            half + k - quarter * start,
            length - k - quarter * start,
        )[j]

    def tile(t, carry):
        first = pl.multiple_of(t * 8, 8)
        row = lax.broadcasted_iota(jnp.int32, (8, LANES), 0) + first
        special = row == 0

        def load(a, c, parity, sine):
            g, i = a // local, a % local
            at = (c * local + i) * LANES
            return prod[g, parity, pl.ds(sine * quarter + first, 8), at : at + LANES]

        def spectra(a):
            parts = []
            for c in range(2):
                ec, oc = load(a, c, 0, 0), load(a, c, 1, 0)
                es, os = load(a, c, 0, 1), load(a, c, 1, 1)
                p, q, m, n = ec + oc, es + os, ec - oc, os - es
                parts.append(
                    (
                        (p, jnp.where(special, 0.0, q)),
                        (m, jnp.where(special, 0.0, n)),
                        (jnp.where(special, es, m), jnp.where(special, os, -n)),
                        (jnp.where(special, es, p), jnp.where(special, -os, -q)),
                    )
                )
            u, v = parts
            return [(u[j][0] + v[j][1], v[j][0] - u[j][1]) for j in range(4)]

        k = row.astype(jnp.float32)
        zero_wave = (0.0, -half, quarter, -quarter)
        waves = (k, half - k, k - half, -k)
        base = spectra(0)
        second = None
        totals = [None] * 4
        saved = [None] * 4
        pending = [None] * 4
        for a in range(fields):
            spec = base if a == 0 else spectra(a)
            for j in range(4):
                cross = base[j][0] * spec[j][0] + base[j][1] * spec[j][1]
                if a == 0:
                    wz = jnp.where(special, float(zero_wave[j]), waves[j])
                    square = wave_x * wave_x + wave_y * wave_y + wz * wz
                    saved[j] = (wz, 1.0 / square)
                    vals[0, j * 8 : j * 8 + 8] = round16(cross)
                    continue
                wz, inverse = saved[j]
                if a == 1:
                    vals[1, j * 8 : j * 8 + 8] = round16(cross)
                    term = -0.5 * cross
                else:
                    weight = (
                        1.5 * wave_x * wave_x,
                        1.5 * wave_y * wave_y,
                        1.5 * wz * wz,
                        3.0 * wave_x * wave_y,
                        3.0 * wave_x * wz,
                        3.0 * wave_y * wz,
                    )[a - 2]
                    term = weight * inverse * cross
                pending[j] = term if pending[j] is None else pending[j] + term
                if a % local == local - 1:
                    rounded = round16(pending[j])
                    totals[j] = rounded if totals[j] is None else totals[j] + rounded
                    pending[j] = None
        for j in range(4):
            high = round16(totals[j])
            vals[2, j * 8 : j * 8 + 8] = high
            vals[3, j * 8 : j * 8 + 8] = totals[j] - high
        total = out_ref[...]
        for start in range(0, 32, PAIRS):
            left, hot = [], []
            for r in range(start, start + PAIRS):
                cell = cell_row(r // 8, first + r % 8)
                spread = [
                    jnp.broadcast_to(part, (16, LANES)).astype(jnp.bfloat16)
                    for part in [vals[i, r : r + 1] for i in range(4)]
                    + [keys[i, pl.ds(cell, 1), :] for i in range(2)]
                ]
                match = spread[4] == iotas[0]
                left.append(
                    jnp.concatenate(
                        [jnp.where(match, spread[i], none) for i in range(4)]
                        + [jnp.where(match, one, none)],
                        axis=0,
                    )
                )
                hot.append(
                    jnp.concatenate(
                        [jnp.where(spread[5] == it, one, none) for it in iotas], axis=0
                    )
                )
            total = total + lax.dot_general(
                jnp.concatenate(left, axis=1),
                jnp.concatenate(hot, axis=1),
                (((1,), (1,)), ((), ())),
                preferred_element_type=jnp.float32,
            )
        out_ref[...] = total
        return carry

    lax.fori_loop(0, quarter // 8, tile, 0)


def relayout_kernel(fields_ref, out_ref):
    for c in range(2):
        for i in range(fields_ref.shape[2]):
            at = (c * fields_ref.shape[2] + i) * LANES
            for h in range(out_ref.shape[1]):
                block = fields_ref[:, c, i, :, h * LANES : (h + 1) * LANES]
                block = block.reshape(16, 2, block.shape[1], LANES)
                for parity in range(2):
                    out_ref[:, h, parity, :, at : at + LANES] = jnp.swapaxes(
                        block[:, parity], 0, 1
                    )


def relayout(fields):
    depth, _, local, planes, yrows = fields.shape
    parts = yrows // LANES
    out = pl.pallas_call(
        relayout_kernel,
        grid=(depth // 32,),
        out_shape=jax.ShapeDtypeStruct(
            (planes, parts, 2, depth // 2, 2 * local * LANES), fields.dtype
        ),
        in_specs=[pl.BlockSpec((32, 2, local, planes, yrows), lambda i: (i, 0, 0, 0, 0))],
        out_specs=pl.BlockSpec(
            (planes, parts, 2, 16, 2 * local * LANES), lambda i: (0, 0, 0, i, 0)
        ),
    )(fields)
    return out.reshape(planes * parts, 2, depth // 2, 2 * local * LANES)


def reduce_kernel(field_count, gz_count, mine_ref, out_ref, parts, answer, send, recv, send2, recv2):
    devices = field_count * gz_count
    me_field, me_gz = lax.axis_index("field"), lax.axis_index("gz")
    me = me_field * gz_count + me_gz

    def peer(step):
        other = lax.rem(me + step, devices)
        return other, (other // gz_count, lax.rem(other, gz_count))

    barrier = pltpu.get_barrier_semaphore()

    def greet(step, carry):
        _, place = peer(step)
        pl.semaphore_signal(
            barrier, inc=1, device_id=place, device_id_type=pl.DeviceIdType.MESH
        )
        return carry

    lax.fori_loop(1, devices, greet, 0)
    pl.semaphore_wait(barrier, devices - 1)

    def scatter(step):
        other, place = peer(step)
        return pltpu.make_async_remote_copy(
            src_ref=mine_ref.at[other],
            dst_ref=parts.at[step],
            send_sem=send.at[step],
            recv_sem=recv.at[step],
            device_id=place,
            device_id_type=pl.DeviceIdType.MESH,
        )

    def gather(step):
        _, place = peer(step)
        return pltpu.make_async_remote_copy(
            src_ref=answer,
            dst_ref=out_ref.at[me],
            send_sem=send2.at[step],
            recv_sem=recv2.at[step],
            device_id=place,
            device_id_type=pl.DeviceIdType.MESH,
        )

    def start(copy):
        def run(step, carry):
            copy(step).start()
            return carry

        lax.fori_loop(1, devices, run, 0)

    start(scatter)

    def collect(step, total):
        scatter(step).wait_recv()
        return total + parts[step]

    answer[...] = lax.fori_loop(1, devices, collect, mine_ref[me])
    start(gather)
    out_ref[me] = answer[...]

    def finish(step, carry):
        scatter(step).wait_send()
        gather(step).wait()
        return carry

    lax.fori_loop(1, devices, finish, 0)


def all_reduce(total, field_count, gz_count):
    devices = field_count * gz_count
    rows = max(1, total.shape[0] // devices)
    total = jnp.pad(total, ((0, devices * rows - total.shape[0]), (0, 0)))
    total = total.reshape(devices, rows, LANES)
    return pl.pallas_call(
        functools.partial(reduce_kernel, field_count, gz_count),
        out_shape=jax.ShapeDtypeStruct(total.shape, jnp.float32),
        in_specs=[pl.BlockSpec(memory_space=pltpu.VMEM)],
        out_specs=pl.BlockSpec(memory_space=pltpu.VMEM),
        scratch_shapes=[
            pltpu.VMEM(total.shape, jnp.float32),
            pltpu.VMEM(total.shape[1:], jnp.float32),
            pltpu.SemaphoreType.DMA((devices,)),
            pltpu.SemaphoreType.DMA((devices,)),
            pltpu.SemaphoreType.DMA((devices,)),
            pltpu.SemaphoreType.DMA((devices,)),
        ],
        compiler_params=pltpu.CompilerParams(collective_id=0, has_side_effects=True),
    )(total).reshape(devices * rows, LANES)


SLOTS = 6
KEPT = 5


def wave_tables(length):
    quarter, half = length // 4, length // 2
    unit = 2.0 * math.pi / length

    def pair(rows, stride):
        row = np.arange(rows)[None, :, None] * stride
        depth = 2 * np.arange(half)[None, None, :] + np.arange(2)[:, None, None]
        angle = (row * depth % length).astype(np.float32) * np.float32(unit)
        return np.cos(angle), np.sin(angle)

    ca, sa = pair(quarter // 16, 16)
    cb, sb = pair(16, 1)
    return np.stack([ca, sa]), np.stack([cb, sb])


def build_table(length, coarse_ref, fine_ref, table):
    quarter, half = length // 4, length // 2
    factor = 1.0 / math.sqrt(length)
    parts = table.shape[0]
    wide = half // parts

    def rows_of(a, carry):
        rows = pl.ds(pl.multiple_of(a * 16, 16), 16)
        under = pl.ds(pl.multiple_of(quarter + a * 16, 16), 16)
        for parity in range(2):
            for q in range(parts):
                at = slice(q * wide, (q + 1) * wide)
                ca, sa = (coarse_ref[i, parity, pl.ds(a, 1), at] for i in range(2))
                cb, sb = (fine_ref[i, parity, :, at] for i in range(2))
                cos_part = (ca * cb - sa * sb) * factor
                sin_part = (sa * cb + ca * sb) * factor
                row = lax.broadcasted_iota(jnp.int32, sin_part.shape, 0) + a
                column = lax.broadcasted_iota(jnp.int32, sin_part.shape, 1)
                alternate = (1 - 2 * (column % 2)).astype(jnp.float32) * factor
                sin_part = jnp.where(row == 0, alternate, sin_part)
                table[q, parity, rows, :] = cos_part.astype(jnp.bfloat16)
                table[q, parity, under, :] = sin_part.astype(jnp.bfloat16)
        return carry

    lax.fori_loop(0, quarter // 16, rows_of, 0)


def split_keys(index, keys):
    depth = index.shape[1]

    def block(g, carry):
        word = index[g]
        mu = lax.shift_right_logical(word, 16)
        shell = word & 65535
        rows = pl.ds(pl.multiple_of(g * depth, depth), depth)
        keys[0, rows, :] = (mu + MUBINS * lax.shift_right_logical(shell, 7)).astype(jnp.float32)
        keys[1, rows, :] = (shell & (LANES - 1)).astype(jnp.float32)
        return carry

    lax.fori_loop(0, index.shape[0], block, 0)


def arrange(length, me_field, stage, spread, chunk):
    planes = stage.shape[3]
    rows = pl.ds(pl.multiple_of(chunk * 16, 16), 16)

    def put(block, h, i, c):
        block = block.reshape(16, 2, planes, LANES)
        for parity in range(2):
            spread[:, h, i, parity, rows, c * LANES : (c + 1) * LANES] = jnp.swapaxes(
                block[:, parity], 0, 1
            )

    def take(c, i, h):
        return stage[:, c, i, :, h * LANES : (h + 1) * LANES]

    @pl.when(me_field % 2 == 0)
    def _():
        for c in range(2):
            for i in range(2):
                for h in range(2):
                    put(take(c, i, h), h, i, c)

    @pl.when(me_field % 2 == 1)
    def _():
        wave_x = lax.broadcasted_iota(jnp.int32, (planes, LANES), 0).astype(jnp.float32)
        wave_x = wave_x + float(length // 4)
        squared = me_field == 1
        for h in range(2):
            wave_y = lax.broadcasted_iota(jnp.int32, (planes, LANES), 1).astype(jnp.float32)
            wave_y = wave_y + float(length // 8 + h * LANES)
            first = jnp.where(squared, 1.5 * wave_x * wave_x, wave_x)[None]
            other = jnp.where(squared, 1.5 * wave_y * wave_y, wave_y)[None]
            for c in range(2):
                value = first * take(c, 0, h).astype(jnp.float32)
                value = value + other * take(c, 1, h).astype(jnp.float32)
                put(value.astype(jnp.bfloat16), h, 0, c)


def transform(table, land, prod, fields, start, sources, sums):
    wide = prod.shape[3]
    quads = [sums[4 * n : 4 * n + 4] for n in range(4)]

    def group(a, carry):
        for parity in range(2):
            for n, (plane, local) in enumerate(sources):
                right = land[local, a, parity].reshape(-1, wide)
                for mxu in range(2):
                    pltpu.matmul_push_rhs(right, n % 2, mxu)
                    for i in range(4):
                        at = (4 * mxu + i) * LANES
                        pltpu.matmul_acc_lhs(
                            quads[2 * mxu + parity][i],
                            table[plane, parity, at : at + LANES, :],
                            n % 2 if i == 0 else None,
                        )
            for mxu in range(2):
                for i in range(4):
                    at = (4 * mxu + i) * LANES
                    prod[start + a, parity, at : at + LANES, :] = pltpu.matmul_pop(
                        quads[2 * mxu + parity][i]
                    )
        return carry

    lax.fori_loop(0, fields, group, 0)


def histogram(length, plane, prod, vals, keys, acc, low, high, sums, counting):
    quarter, half = length // 4, length // 2
    groups, mxus = 4, 2
    lane = lax.broadcasted_iota(jnp.int32, (8, LANES), 1).astype(jnp.float32)
    wave_x = (length // 4 + plane // 2).astype(jnp.float32)
    wave_y = (length // 8 + (plane % 2) * LANES).astype(jnp.float32) + lane
    flat = wave_x * wave_x + wave_y * wave_y
    low_iota = lax.broadcasted_iota(jnp.int32, (16, LANES), 0).astype(jnp.float32)
    iotas = [(low_iota + 16.0 * j).astype(jnp.bfloat16) for j in range(LANES // 16)]
    one = jnp.ones((16, LANES), jnp.bfloat16)
    none = jnp.zeros((16, LANES), jnp.bfloat16)

    def cell_row(j, k):
        start = 1 - (k + quarter - 1) // quarter
        return (
            k,
            half - k,
            half + k - quarter * start,
            length - k - quarter * start,
        )[j]

    def values(t, edge, slot):
        first = t * 8 if edge else pl.multiple_of(t * 8, 8)
        row = lax.broadcasted_iota(jnp.int32, (8, LANES), 0) + first
        special = row == 0

        def load(a, c, parity, sine):
            at = pl.ds(sine * quarter + first, 8)
            return prod[a, parity, at, c * LANES : (c + 1) * LANES]

        def spectra(a):
            parts = []
            for c in range(2):
                ec, oc = load(a, c, 0, 0), load(a, c, 1, 0)
                es, os = load(a, c, 0, 1), load(a, c, 1, 1)
                p, q, m, n = ec + oc, es + os, ec - oc, os - es
                if edge:
                    parts.append(
                        (
                            (p, jnp.where(special, 0.0, q)),
                            (m, jnp.where(special, 0.0, n)),
                            (jnp.where(special, es, m), jnp.where(special, os, -n)),
                            (jnp.where(special, es, p), jnp.where(special, -os, -q)),
                        )
                    )
                else:
                    parts.append(((p, q), (m, n), (m, n), (p, q)))
            u, v = parts
            result = []
            for j in range(4):
                if edge or j < 2:
                    result.append((u[j][0] + v[j][1], v[j][0] - u[j][1]))
                else:
                    result.append((u[j][0] - v[j][1], v[j][0] + u[j][1]))
            return result

        k = row.astype(jnp.float32)
        zero_wave = (0.0, -half, quarter, -quarter)
        waves = [k, half - k, k - half, -k]
        if edge:
            waves = [jnp.where(special, float(z), w) for z, w in zip(zero_wave, waves)]
            inverse = [1.0 / (flat + w * w) for w in waves]
        else:
            inverse = [1.0 / (flat + w * w) for w in waves[:2]]
            inverse = [inverse[0], inverse[1], inverse[1], inverse[0]]
        base, first_cross, cross_b, cubic, mixed = (spectra(a) for a in range(KEPT))
        for j in range(4):
            re, im = base[j]
            auto = re * re + im * im
            pair = re * first_cross[j][0] + im * first_cross[j][1]
            w = waves[j]
            three, half_more = 3.0 * w, 1.5 * (w * w)
            qre = mixed[j][0] + three * cross_b[j][0] + half_more * cubic[j][0]
            qim = mixed[j][1] + three * cross_b[j][1] + half_more * cubic[j][1]
            quad = inverse[j] * (re * qre + im * qim) - 0.5 * pair
            vals[slot, 0, j * 8 : j * 8 + 8] = jnp.where(counting, 1.0, auto)
            vals[slot, 1, j * 8 : j * 8 + 8] = pair
            vals[slot, 2, j * 8 : j * 8 + 8] = quad

    def one_hots(r, cell, slot):
        spread = [
            jnp.broadcast_to(part, (16, LANES)).astype(jnp.bfloat16)
            for part in [vals[slot, i, r : r + 1] for i in range(3)]
            + [keys[i, pl.ds(cell, 1), :] for i in range(2)]
        ]
        match = spread[3] == iotas[0]
        left = [jnp.where(match, spread[i], none) for i in range(3)]
        left = jnp.concatenate(left + [none], axis=0)
        hot = [jnp.where(spread[4] == it, one, none) for it in iotas]
        return left, jnp.concatenate(hot, axis=0)

    def units(t, slot):
        first = t * 8
        for unit in range(4):
            mxu, stage = unit % mxus, unit // mxus
            lefts, hots = [], []
            for g in range(groups):
                pair = []
                for r in range(unit * 8 + g * 2, unit * 8 + g * 2 + 2):
                    pair.append(one_hots(r, cell_row(r // 8, first + r % 8), slot))
                lefts.append(jnp.concatenate([x[0] for x in pair], axis=1))
                hots.append(jnp.concatenate([x[1] for x in pair], axis=1))
            pltpu.matmul_push_rhs(jnp.concatenate(lefts, axis=0), stage, mxu, transpose=True)
            for g in range(groups):
                pltpu.matmul_acc_lhs(sums[8 * mxu + g], hots[g], stage if g == 0 else None)

    @pl.when(low == 0)
    def _():
        values(0, True, 0)

    @pl.when(low != 0)
    def _():
        values(low, False, 0)

    def step(n, carry):
        for i in range(8):
            t = low + 8 * n + i
            units(t, i % 2)
            values(jnp.minimum(t + 1, quarter // 8 - 1), False, 1 - i % 2)
        return carry

    lax.fori_loop(0, (high - low) // 8, step, 0)
    total = None
    for g in range(groups):
        block = pltpu.matmul_pop(sums[g]) + pltpu.matmul_pop(sums[8 + g])
        block = block[:, g // 2 * LANES : (g // 2 + 1) * LANES]
        block = jnp.transpose(block)[g % 2 * 64 : g % 2 * 64 + 64]
        total = block if total is None else total + block
    acc[...] += total


def whole_kernel(
    length, coarse_ref, fine_ref, fields_ref, shells_ref, mubins_ref, out_ref,
    stage, spread, mix, joined, first, land, prod, table, raw, index_out, index, keys, vals, acc,
    parts, answer,
    stage_sem, raw_sem, index_sent, index_come, mix_sent, mix_come, land_sent, first_come,
    land_come, part_sent, part_come, answer_sent, answer_come,
):
    fields, cores, chunks = 4, 2, 2
    planes_z = table.shape[0]
    gz_count = planes_z * cores
    owners = gz_count // chunks
    devices = fields * gz_count
    me_field, me_gz = lax.axis_index("field"), lax.axis_index("gz")
    me = me_field * gz_count + me_gz
    me_plane, me_core = me_gz // cores, me_gz % cores
    me_half, me_owner = me_gz // owners, me_gz % owners
    steps = fields_ref.shape[0] // 32
    MESH = pl.DeviceIdType.MESH

    def loop(low, high, run):
        def step(i, carry):
            run(i)
            return carry

        lax.fori_loop(low, high, step, 0)

    def wait(ref, sem):
        pltpu.make_async_copy(ref, ref, sem).wait()

    barrier = pltpu.get_barrier_semaphore()

    def greet(step):
        other = lax.rem(me + step, devices)
        pl.semaphore_signal(
            barrier, inc=1, device_id=(other // gz_count, lax.rem(other, gz_count)),
            device_id_type=MESH,
        )

    loop(1, devices, greet)

    def raw_copy(b):
        lanes = pl.ds(pl.multiple_of((b % 2) * LANES, LANES), LANES)
        at = (slice(None), me_field * (gz_count // 2) + b // 2, lanes)
        return [
            pltpu.make_async_copy(ref.at[at], raw.at[i, b], raw_sem.at[i])
            for i, ref in enumerate((shells_ref, mubins_ref))
        ]

    def fetch(n):
        return pltpu.make_async_copy(
            fields_ref.at[pl.ds(n * 32, 32)], stage.at[n % 2], stage_sem.at[n % 2]
        )

    loop(0, gz_count, lambda b: [copy.start() for copy in raw_copy(b)])
    for n in range(2):
        fetch(n).start()
    for i in range(2):
        wait(raw.at[i], raw_sem.at[i])

    def join(n):
        index_out[n] = raw[0, n] + raw[1, n] * 65536

    loop(0, gz_count, join)
    pl.semaphore_wait(barrier, devices - 1)

    def owner_of(i):
        plane = lax.rem(me_plane + 1 + (i % owners) // 2, 2)
        return plane * cores + lax.rem(me_core + i, cores)

    def forward(source, goal, sent, come, g):
        pltpu.make_async_remote_copy(
            src_ref=source, dst_ref=goal, send_sem=sent, recv_sem=come,
            device_id=(me_field, g), device_id_type=MESH,
        ).start()

    def index_send(i):
        chunk, owner = i // owners, owner_of(i)
        b = chunk * owners + owner
        goal = index.at[chunk, me_gz]
        forward(
            index_out.at[b], goal, index_sent, index_come.at[chunk],
            (1 - me_half) * owners + owner,
        )

        @pl.when(owner != me_owner)
        def _():
            forward(
                index_out.at[b], goal, index_sent, index_come.at[chunk],
                me_half * owners + owner,
            )

        @pl.when(owner == me_owner)
        def _():
            pltpu.make_async_copy(index_out.at[b], goal, index_come.at[chunk]).start()

    loop(0, gz_count, index_send)

    def place(n):
        fetch(n).wait()
        arrange(length, me_field, stage.at[n % 2], spread, n)

        @pl.when(n + 2 < steps)
        def _():
            fetch(n + 2).start()

    loop(0, steps, place)

    even = 1 - me_field % 2
    slot = even * (3 * me_field // 2) + (1 - even) * ((13 - 3 * me_field) // 2)

    def mix_send(i):
        b = (i // owners) * owners + owner_of(i)

        def piece(f, s):
            return spread.at[f * (gz_count // 2) + b // 2, b % 2, s]

        def send(f, s):
            pltpu.make_async_remote_copy(
                src_ref=piece(f, s), dst_ref=mix.at[b, slot + s],
                send_sem=mix_sent, recv_sem=mix_come.at[b],
                device_id=(f, me_gz), device_id_type=MESH,
            ).start()

        def keep(s):
            pltpu.make_async_copy(
                piece(me_field, s), mix.at[b, slot + s], mix_come.at[b]
            ).start()

        others = [lax.rem(me_field + 2, 4), me_field + 1 - 2 * (me_field % 2), 3 - me_field]
        for f in others:
            send(f, 0)
        keep(0)

        @pl.when(even == 1)
        def _():
            for f in others:
                send(f, 1)
            keep(1)

    loop(0, gz_count, mix_send)
    build_table(length, coarse_ref, fine_ref, table)
    acc[...] = jnp.zeros_like(acc)

    def join_send(i):
        chunk, owner = i // owners, owner_of(i)
        b = chunk * owners + owner
        wait(mix.at[b], mix_come.at[b])
        wave_x = (length // 4 + me_field * (gz_count // 2) + b // 2).astype(jnp.float32)
        lane = lax.broadcasted_iota(jnp.int32, (1, 2 * LANES), 1) % LANES
        wave_y = (length // 8 + (b % 2) * LANES + lane).astype(jnp.float32)
        weight = 3.0 * wave_x * wave_y
        for parity in range(2):
            value = mix[b, 5, parity].astype(jnp.float32)
            value = value + weight * mix[b, 4, parity].astype(jnp.float32)
            joined[b, parity] = value.astype(jnp.bfloat16)
        base = (mix.at[b, 0], first.at[chunk, me_plane, 0, :, me_core])
        me_near = me_plane % 2
        pairs = (
            (mix.at[b, pl.ds(1, 3)], land.at[chunk, me_near, pl.ds(0, 3), :, me_core]),
            (joined.at[b], land.at[chunk, me_near, 3, :, me_core]),
        )
        forward(*base, land_sent, first_come.at[chunk, me_gz], (1 - me_half) * owners + owner)

        @pl.when(owner != me_owner)
        def _():
            g = me_half * owners + owner
            forward(*base, land_sent, first_come.at[chunk, me_gz], g)
            for source, goal in pairs:
                forward(source, goal, land_sent, land_come.at[chunk, me_owner], g)

        @pl.when(owner == me_owner)
        def _():
            pltpu.make_async_copy(*base, first_come.at[chunk, me_gz]).start()
            for source, goal in pairs:
                pltpu.make_async_copy(source, goal, land_come.at[chunk, me_owner]).start()

    def transform_lines(chunk, sums):
        near = 1 - 2 * (me_plane % 2)
        sources = [(me_plane + hop, lax.rem(me_plane + hop, 2)) for hop in (0, near)]
        for _, local in sources:
            for core in range(cores):
                wait(land.at[chunk, local, :, :, core], land_come.at[chunk, local * cores + core])
        transform(table, land.at[chunk], prod, KEPT - 1, 1, sources, sums)
        sources = [(n, n) for n in range(planes_z)]
        for plane, _ in sources:
            for core in range(cores):
                block = first.at[chunk, plane, :, :, core]
                wait(block, first_come.at[chunk, plane * cores + core])
        transform(table, first.at[chunk], prod, 1, 0, sources, sums)

    tiles = length // 32
    span = tiles // owners

    def bin_lines(chunk, low, high, sums):
        b = me_field * gz_count + chunk * owners + me_owner
        histogram(length, b, prod, vals, keys.at[chunk], acc, low, high, sums, me_half == 1)

    loop(0, owners, join_send)
    for chunk in range(chunks):
        wait(index.at[chunk], index_come.at[chunk])
        split_keys(index.at[chunk], keys.at[chunk])
    join_send(owners)

    def crunch(*sums):
        for ref in sums:
            pltpu.matmul_pop(ref)

        def part(n):
            chunk = n // owners

            @pl.when(n % owners == 0)
            def _():
                transform_lines(chunk, sums)

            low = lax.rem(n, owners) * span
            high = low + span + chunk * (tiles - span)
            bin_lines(chunk, low, high, sums)

            @pl.when(n < owners - 1)
            def _():
                join_send(owners + 1 + n)

        loop(0, owners + 1, part)

    pl.run_scoped(
        crunch,
        *(
            pltpu.ACC(mxu)((LANES, 2 * LANES), jnp.float32)
            for mxu in range(2)
            for _ in range(8)
        ),
    )

    counted = acc[0:LOW, :]
    acc[0:LOW, :] = jnp.where(me_half == 1, 0.0, counted)
    acc[3 * LOW : 4 * LOW, :] = jnp.where(me_half == 1, counted, 0.0)
    ranks = acc.shape[0] // 8
    middle = (planes_z // 2 - 1) * cores
    rank = me_field + fields * lax.div(me_gz - middle, cores)
    root = (me_gz == middle) | (me_gz == middle + cores)

    def part_copy(r):
        return pltpu.make_async_remote_copy(
            src_ref=acc.at[pl.ds(pl.multiple_of(r * 8, 8), 8)], dst_ref=parts.at[me],
            send_sem=part_sent, recv_sem=part_come,
            device_id=(lax.rem(r, fields), middle + cores * (r // fields)),
            device_id_type=MESH,
        )

    def part_send(n):
        r = lax.rem(me_field + n, ranks)

        @pl.when((r != rank) | jnp.logical_not(root))
        def _():
            part_copy(r).start()

    loop(0, ranks, part_send)

    def answer_copy(step):
        other = lax.rem(me + step, devices)
        return pltpu.make_async_remote_copy(
            src_ref=answer.at[rank], dst_ref=answer.at[rank],
            send_sem=answer_sent, recv_sem=answer_come,
            device_id=(other // gz_count, lax.rem(other, gz_count)), device_id_type=MESH,
        )

    @pl.when(root)
    def _():
        parts[me] = acc[pl.ds(pl.multiple_of(rank * 8, 8), 8), :]
        rest = parts.at[pl.ds(0, devices - 1)]
        wait(rest, part_come)
        answer[rank] = lax.fori_loop(
            1, devices, lambda d, total: total + parts[d], parts[0]
        )
        loop(1, devices, lambda step: answer_copy(step).start())
        got = answer.at[pl.ds(0, ranks - 1)]
        wait(got, answer_come)
        wait(rest, answer_sent)
        wait(got, part_sent)

    @pl.when(jnp.logical_not(root))
    def _():
        wait(answer, answer_come)
        wait(answer, part_sent)

    for hi in range(2):
        scale = 1.0 / jnp.maximum(answer[6 + hi], 1.0)
        for m in range(3):
            out_ref[m, :, hi * LANES : (hi + 1) * LANES] = answer[2 * m + hi] * scale

    for _ in range(2):
        sent = index_out.at[pl.ds(0, gz_count - 1)]
        wait(sent, index_sent)
    wait(mix.at[:, 0], land_sent)
    wait(mix.at[pl.ds(0, 2 * (owners - 1)), pl.ds(0, KEPT)], land_sent)

    @pl.when(even == 1)
    def _():
        wait(spread.at[pl.ds(0, 12)], mix_sent)

    @pl.when(even == 0)
    def _():
        wait(spread.at[pl.ds(0, 12), :, 0], mix_sent)


def whole(fields, shells, mubins, gz_count):
    depth, _, local, planes, yrows = fields.shape
    length = depth * gz_count
    half = length // 2
    coarse, fine = wave_tables(length)
    vmem, anywhere = pl.BlockSpec(memory_space=pltpu.VMEM), pl.BlockSpec(memory_space=pl.ANY)
    wide = 2 * LANES
    dma = pltpu.SemaphoreType.DMA
    low = jnp.bfloat16
    line_block = (2, depth // 2, wide)
    pair_block = (2, 2, depth // 2, wide)
    return pl.pallas_call(
        functools.partial(whole_kernel, length),
        out_shape=jax.ShapeDtypeStruct((3, MUBINS, SHELLS), jnp.float32),
        in_specs=[vmem, vmem, anywhere, anywhere, anywhere],
        out_specs=vmem,
        scratch_shapes=[
            pltpu.VMEM((2, 32) + fields.shape[1:], low),
            pltpu.VMEM((planes, 2, local) + line_block, low),
            pltpu.VMEM((gz_count, SLOTS) + line_block, low),
            pltpu.VMEM((gz_count,) + line_block, low),
            pltpu.VMEM((2, gz_count // 2, 1) + pair_block, low),
            pltpu.VMEM((2, gz_count // 4, KEPT - 1) + pair_block, low),
            pltpu.VMEM((KEPT, 2, half, wide), jnp.float32),
            pltpu.VMEM((gz_count // 2, 2, half, depth), low),
            pltpu.VMEM((2, gz_count, depth, LANES), jnp.int32),
            pltpu.VMEM((gz_count, depth, LANES), jnp.int32),
            pltpu.VMEM((2, gz_count, depth, LANES), jnp.int32),
            pltpu.VMEM((2, 2, length, LANES), jnp.float32),
            pltpu.VMEM((2, 3, 32, LANES), jnp.float32),
            pltpu.VMEM((4 * LOW, LANES), jnp.float32),
            pltpu.VMEM((4 * gz_count, 8, LANES), jnp.float32),
            pltpu.VMEM((8, 8, LANES), jnp.float32),
            dma((2,)), dma((2,)), dma, dma((2,)), dma, dma((gz_count,)), dma,
            dma((2, gz_count)), dma((2, gz_count // 2)), dma, dma, dma, dma,
        ],
        compiler_params=pltpu.CompilerParams(
            vmem_limit_bytes=60 * 1024 * 1024, collective_id=2, has_side_effects=True
        ),
    )(jnp.asarray(coarse), jnp.asarray(fine), fields, shells, mubins)


def body(fields, shells, mubins):
    depth_local, _, local_fields, planes, yrows = fields.shape
    gz_count, field_count = lax.axis_size("gz"), lax.axis_size("field")
    devices = gz_count * field_count
    length = depth_local * gz_count
    half = length // 2
    plane_rows = planes * yrows
    width = plane_rows // devices
    me_gz, me_field = lax.axis_index("gz"), lax.axis_index("field")

    paired = yrows == 2 * LANES and 2 * planes == devices and local_fields == 2
    if paired and depth_local == 2 * LANES and gz_count == 2 * field_count == MUBINS:
        return whole(fields, shells, mubins, gz_count)

    exchange = width == LANES and depth_local % 32 == 0
    if exchange:
        lines = relayout(fields)
    else:
        lines = fields.reshape(depth_local // 2, 2, 2, local_fields, devices, width)
        lines = lines.transpose(4, 1, 0, 2, 3, 5).reshape(
            devices, 2, depth_local // 2, 2 * local_fields * width
        )

    share = planes // field_count
    shells, mubins = (
        lax.dynamic_slice_in_dim(ids, me_field * share, share, 1) for ids in (shells, mubins)
    )
    index = (shells + mubins * 65536).reshape(depth_local, gz_count, width).transpose(1, 0, 2)

    span = 2 * local_fields * LANES
    table = quarter_tables(length, jnp.minimum(me_gz, 0))
    column = (me_field * gz_count + me_gz) * width + jnp.arange(LANES, dtype=jnp.int32)
    waves = jnp.stack([length // 4 + column // yrows, length // 8 + column % yrows])
    waves = jnp.pad(waves.astype(jnp.float32), ((0, 6), (0, 0)))
    landed = (field_count, gz_count, 2, depth_local // 2, span)
    scratch = [
        pltpu.VMEM((field_count, 2, half, span), jnp.float32),
        pltpu.VMEM((4, 32, LANES), jnp.float32),
        pltpu.VMEM((2, length, LANES), jnp.float32),
    ]
    vmem, anywhere = pl.BlockSpec(memory_space=pltpu.VMEM), pl.BlockSpec(memory_space=pl.ANY)
    if exchange:
        run, places, wide = (
            functools.partial(exchange_kernel, length, field_count, gz_count),
            anywhere,
            dict(collective_id=1, has_side_effects=True),
        )
        scratch += [
            pltpu.VMEM(landed, jnp.bfloat16),
            pltpu.VMEM((gz_count, depth_local, LANES), jnp.int32),
            pltpu.SemaphoreType.DMA((2, devices)),
            pltpu.SemaphoreType.DMA((2, devices)),
            pltpu.SemaphoreType.DMA((2,)),
            pltpu.SemaphoreType.DMA((gz_count,)),
            pltpu.SemaphoreType.DMA((gz_count,)),
            pltpu.SemaphoreType.DMA,
        ]
    else:
        run, places, wide = functools.partial(local_kernel, length), vmem, {}
        lines = lax.all_to_all(lines, ("field", "gz"), split_axis=0, concat_axis=0, tiled=True)
        lines = lines.reshape(landed[:-1] + (2 * local_fields, width))
        lines = jnp.pad(lines, ((0, 0),) * 5 + ((0, LANES - width),)).reshape(landed)
        index = lax.all_to_all(index, "gz", split_axis=0, concat_axis=0, tiled=True)
        index = jnp.pad(index, ((0, 0), (0, 0), (0, LANES - width)), constant_values=SHELLS)

    total = pl.pallas_call(
        run,
        out_shape=jax.ShapeDtypeStruct((ROWS * LOW, LANES), jnp.float32),
        in_specs=[vmem, places, places, vmem],
        out_specs=vmem,
        scratch_shapes=scratch,
        compiler_params=pltpu.CompilerParams(vmem_limit_bytes=56 * 1024 * 1024, **wide),
    )(table, lines, index, waves)

    total = total.reshape(ROWS, LOW, LANES)
    total = jnp.concatenate([total[:2], total[2:3] + total[3:4], total[4:]])
    total = all_reduce(total.reshape(-1, LANES), field_count, gz_count)[: 4 * LOW]
    total = total.reshape(4, 2, MUBINS, LANES).transpose(0, 2, 3, 1)
    total = total.reshape(4, MUBINS, SHELLS)
    return total[:3] / jnp.maximum(total[3], 1.0)[None]


def solution(mesh):
    in_specs = (P("gz", None, "field", None, None), P("gz", None, None), P("gz", None, None))
    return jax.shard_map(body, mesh=mesh, in_specs=in_specs, out_specs=P(), check_vma=False)
```
